128 devices in a mesh: blk: 8 (over y, core), grp: 16 (over x, z).
Axes of the slice: x: 4, y: 4, z: 4, core: 2. Of those that a mesh axis runs over, the one named last changes fastest.
Arguments:
- gas_state: bfloat16 [16, 32, 131072], P(None, None, ('grp', 'blk')), may hold values from -6 to 6
- cos_zenith: bfloat16 [131072], P(('grp', 'blk')), may hold values from 0.049804688 to 1
- daylit: int32 [131072], P(('grp', 'blk')), may hold values from 0 to 1
- fine_area: float32 [524288], P(('grp', 'blk')), may hold values from 0.25 to 4
- fine_albedo: float32 [2, 524288], P(None, ('grp', 'blk')), may hold values from 0.05 to 0.85
- parent_of: int32 [524288], P(('grp', 'blk')), may hold values from 0 to 8191, as said below
- optics_weight: bfloat16 [64, 16], replicated, may hold values from -1.5 to 1.5
- solar_weight: float32 [32], replicated, may hold values from 0.01 to 0.1
- neighbours: int32 [3, 131072], P(None, ('grp', 'blk')), may hold values from 0 to 131071, as said below
- side_weight: float32 [3, 131072], P(None, ('grp', 'blk')), may hold values from 0.05 to 0.3
Outputs:
- fluxes: float32 [2, 33, 131072], P(None, None, ('grp', 'blk'))
The draws below stay inside these ranges and needn't reach their ends.
Inputs may be any that keep to these rules, and one draw needn't show every extreme that they name: `parent_of`: the fine cells of one index of grp have their parents among that index's columns, numbered from 0 within it; each column has exactly 4 fine cells, and the 128 fine cells of an aligned block share 128 // 4 consecutive columns. `neighbours`: every neighbour lies within 128 columns of its column and among the columns of the same index of grp; a neighbour may be the column itself.
All inputs are finite; a program needn't handle non-finite values.
Results may differ from the reference program's by a relative error of at most 0.0003.
Values may be sent and summed in bfloat16 or wider, within the bound.
No kernel may reach another device: no remote copies, remote signals or barrier semaphores. Data moves between devices by JAX's collectives and lax.ppermute only.
A program may use at most 64 MiB of HBM per device.

```python
import math
import jax
import jax.numpy as jnp
from jax import lax

G = 32
F = 16
LEV = 32
COLS_DEV = 1024
CB = 128
KIDS = 4
FB = 128
REACH = 128
GROUP_COLS = 8192
COLUMNS = 131072
FINE = 524288
N_BLK = 8
N_GRP = 16


def draw_daylit(key, part):
    devices = N_GRP * N_BLK
    nblocks = COLS_DEV // CB
    key_one, key_two, key_three = jax.random.split(jax.random.fold_in(key, 11), 3)
    blk_place = jnp.arange(devices, dtype=jnp.int32) % N_BLK
    trend = blk_place * nblocks // max(N_BLK - 1, 1)
    jitter = jax.random.randint(key_one, (devices,), -(nblocks // 2), nblocks // 2 + 1)
    lit_blocks = jnp.clip(trend + jitter, 0, nblocks)
    scores = jax.random.randint(key_two, (devices, nblocks), 0, 1 << 16) * nblocks + jnp.arange(nblocks, dtype=jnp.int32)[None, :]
    ordering = jnp.argsort(scores, axis=1)
    ranking = jnp.argsort(ordering, axis=1)
    partial_len = jax.random.randint(key_three, (devices, 1, 1), 1, CB)
    inside = jnp.arange(CB, dtype=jnp.int32)[None, None, :]
    fully = ranking[:, :, None] < lit_blocks[:, None, None]
    border = (ranking[:, :, None] == lit_blocks[:, None, None]) & (inside < partial_len)
    return (fully | border).astype(jnp.int32).reshape(COLUMNS)


def draw_parent_of(key, part):
    per_span = FB // KIDS
    spans = GROUP_COLS // per_span
    key_one, key_two = jax.random.split(jax.random.fold_in(key, 23))
    scores = jax.random.randint(key_one, (N_GRP, spans), 0, 1 << 12) * spans + jnp.arange(spans, dtype=jnp.int32)[None, :]
    span_order = jnp.argsort(scores, axis=1).astype(jnp.int32)
    inner_scores = jax.random.randint(key_two, (N_GRP, spans, FB), 0, 1 << 16) * FB + jnp.arange(FB, dtype=jnp.int32)[None, None, :]
    inner = jnp.argsort(inner_scores, axis=2).astype(jnp.int32) % per_span
    parent = span_order[:, :, None] * per_span + inner
    return parent.reshape(FINE).astype(jnp.int32)


def draw_neighbours(key, part):
    column = jnp.arange(COLUMNS, dtype=jnp.int32)
    lower = column // GROUP_COLS * GROUP_COLS
    offsets = jax.random.randint(jax.random.fold_in(key, 37), (3, COLUMNS), -REACH, REACH + 1)
    return jnp.clip(column[None, :] + offsets, lower[None, :], lower[None, :] + GROUP_COLS - 1).astype(jnp.int32)


def block_scale(key, dims, shards, low, top_value):
    def one(axis_at, blocks):
        draws = jax.random.uniform(jax.random.fold_in(jax.random.fold_in(key, 6), axis_at), (blocks,), jnp.float32, low / len(shards), top_value / len(shards))
        return jnp.repeat(jnp.exp(draws), dims[axis_at] // blocks).reshape((-1,) + (1,) * (len(dims) - axis_at - 1))

    gain = one(*shards[0])
    for cut in shards[1:]:
        gain = gain * one(*cut)
    return gain


def bell_draw(own_key, extent, scale, bound, shards=(), kind=jnp.bfloat16):
    values = scale * jax.random.normal(own_key, extent, jnp.float32)
    if shards:
        values = values * block_scale(own_key, extent, shards, -0.22, 0.18)
    return jnp.clip(values, -bound, bound).astype(kind)


def setup_inputs(seed: int = 0) -> dict:
    seeds = jax.random.split(jax.random.key(seed), 11)
    gas_state = bell_draw(seeds[0], (F, LEV, COLUMNS), 1.0, 6.0, ((2, 128),))
    cos_zenith = jnp.clip(0.049804688 + 0.9501953 * jax.random.uniform(seeds[1], (COLUMNS,), jnp.float32) ** block_scale(seeds[1], (COLUMNS,), ((0, 128),), -0.2, 0.2), 0.049804688, 1.0).astype(jnp.bfloat16)
    daylit = draw_daylit(jax.random.fold_in(seeds[10], 71), 0)
    fine_area = jnp.clip(jnp.exp(math.log(4.0) - 2.7725887 * jax.random.uniform(seeds[3], (FINE,), jnp.float32) ** block_scale(seeds[3], (FINE,), ((0, 128),), -0.2, 0.2)), 0.25, 4.0)
    fine_albedo = jnp.clip(0.05 + 0.8 * jax.random.uniform(seeds[4], (2, FINE), jnp.float32) ** block_scale(seeds[4], (2, FINE), ((1, 128),), -0.2, 0.2), 0.05, 0.85)
    parent_of = draw_parent_of(jax.random.fold_in(seeds[10], 71), 0)
    optics_weight = bell_draw(seeds[6], (2 * G, F), F ** -0.5, 1.5)
    solar_weight = jnp.clip(jnp.exp(jax.random.uniform(seeds[7], (G,), jnp.float32, math.log(0.01), math.log(0.1))), 0.01, 0.1)
    neighbours = draw_neighbours(jax.random.fold_in(seeds[10], 71), 0)
    side_weight = jnp.clip(0.05 + 0.25 * jax.random.uniform(seeds[9], (3, COLUMNS), jnp.float32) ** block_scale(seeds[9], (3, COLUMNS), ((1, 128),), -0.2, 0.2), 0.05, 0.3)
    return dict(gas_state=gas_state, cos_zenith=cos_zenith, daylit=daylit, fine_area=fine_area, fine_albedo=fine_albedo, parent_of=parent_of, optics_weight=optics_weight, solar_weight=solar_weight, neighbours=neighbours, side_weight=side_weight)


ASYM = 0.8
TAU_SCALE = 0.08
SSA_MAX = 0.98

def column_fluxes(optics_mix, cosine_col, albedo_direct, albedo_diffuse, lit_flag, solar_weight):
    gpoints = solar_weight.shape[0]
    width = cosine_col.shape[0]
    optical_depth = TAU_SCALE * jax.nn.softplus(optics_mix[:, :gpoints])
    single_albedo = SSA_MAX * jax.nn.sigmoid(optics_mix[:, gpoints:])
    slant = cosine_col[None, None, :]
    direct_share = jnp.exp(-optical_depth / slant)
    gamma_one = 2.0 - single_albedo * (1.25 + 0.75 * ASYM)
    gamma_two = 0.75 * single_albedo * (1.0 - ASYM)
    eigen_rate = jnp.sqrt((gamma_one - gamma_two) * (gamma_one + gamma_two))
    damping = jnp.exp(-eigen_rate * optical_depth)
    damped_sq = damping * damping
    divisor = eigen_rate + gamma_one + (eigen_rate - gamma_one) * damped_sq
    reflect = gamma_two * (1.0 - damped_sq) / divisor
    transmit = 2.0 * eigen_rate * damping / divisor
    back_share = 0.5 * (1.0 - ASYM * slant)
    scattered = single_albedo * (1.0 - direct_share)
    rising = scattered * back_share
    falling = scattered - rising
    top_flux = solar_weight[:, None] * cosine_col[None, :]
    direct = top_flux[None] * jnp.concatenate([jnp.ones_like(top_flux)[None], jnp.cumprod(direct_share, axis=0)], axis=0)

    def ascend(carry, layer):
        albedo, source = carry
        inverse = 1.0 / (1.0 - albedo * layer[0])
        new_albedo = layer[0] + layer[1] * layer[1] * albedo * inverse
        new_source = layer[2] * layer[4] + layer[1] * (source + albedo * layer[3] * layer[4]) * inverse
        return ((new_albedo, new_source), (albedo, source, inverse))
    ground = (jnp.broadcast_to(albedo_diffuse[None, :], top_flux.shape), albedo_direct[None, :] * direct[-1])
    (top_albedo, source_top), below = lax.scan(ascend, ground, (reflect, transmit, rising, falling, direct[:-1]), reverse=True)

    def descend(diffuse, layer):
        updated = (layer[1] * diffuse + layer[0] * layer[6] + layer[3] * layer[4]) * layer[7]
        return (updated, (updated, layer[5] * updated + layer[6]))
    last_diffuse, (diffuse_down, diffuse_up) = lax.scan(descend, jnp.zeros_like(top_flux), (reflect, transmit, rising, falling, direct[:-1], below[0], below[1], below[2]))
    first_row = jnp.zeros((1, width), jnp.float32)
    downward = lax.optimization_barrier(jnp.sum(direct, axis=1)) + jnp.concatenate([first_row, lax.optimization_barrier(jnp.sum(diffuse_down, axis=1))], axis=0)
    upward = jnp.concatenate([lax.optimization_barrier(jnp.sum(source_top, axis=0))[None], lax.optimization_barrier(jnp.sum(diffuse_up, axis=1))], axis=0)
    return jnp.stack([downward, upward]) * lit_flag[None, None, :]

def reference(gas_state, cos_zenith, daylit, fine_area, fine_albedo, parent_of, optics_weight, solar_weight, neighbours, side_weight):
    weights = jnp.stack([fine_area, fine_area * fine_albedo[0], fine_area * fine_albedo[1]])
    fine_group = (jnp.arange(FINE, dtype=jnp.int32) // (KIDS * GROUP_COLS)).astype(jnp.int32)
    parent_global = (parent_of + fine_group * GROUP_COLS).astype(jnp.int32)
    totals = jax.vmap(lambda values: jax.ops.segment_sum(values, parent_global, num_segments=COLUMNS))(weights)
    albedo = (totals[1:] / totals[0]).astype(jnp.bfloat16).astype(jnp.float32)
    cosine_all = cos_zenith.astype(jnp.float32)
    lit_all = daylit.astype(jnp.float32)
    matrix = optics_weight.astype(jnp.float32)
    nblocks = COLUMNS // COLS_DEV

    def one_block(number):
        begin_at = (number * COLS_DEV).astype(jnp.int32)
        inputs = lax.dynamic_slice_in_dim(gas_state, begin_at, COLS_DEV, 2).astype(jnp.float32)
        optics_mix = jnp.einsum('gf,fln->lgn', matrix, inputs, precision=lax.Precision.HIGHEST)
        cosine_col = lax.dynamic_slice_in_dim(cosine_all, begin_at, COLS_DEV, 0)
        albedo_cols = lax.dynamic_slice_in_dim(albedo, begin_at, COLS_DEV, 1)
        lit_cols = lax.dynamic_slice_in_dim(lit_all, begin_at, COLS_DEV, 0)
        return column_fluxes(optics_mix, cosine_col, albedo_cols[0], albedo_cols[1], lit_cols, solar_weight)
    stacked = lax.map(one_block, jnp.arange(nblocks, dtype=jnp.int32))
    column_flux = jnp.moveaxis(stacked, 0, 2).reshape(2, LEV + 1, COLUMNS)
    result = column_flux
    for index_k in range(3):
        beside = jnp.take(column_flux, neighbours[index_k], axis=2)
        result = result + side_weight[index_k][None, None, :] * (beside - column_flux)
    return result
```

```python
import jax
import jax.numpy as jnp
from jax import lax
from jax.experimental import pallas as pl
from jax.experimental.pallas import tpu as pltpu
from jax.sharding import PartitionSpec as P

F = 16
LEV = 32
CB = 128
G = 32
KIDS = 4
NB = 8
NBLK = 8
ROWS = 72
HALF = 16
FINE_BLOCKS = NB * KIDS

ASYM = 0.8
TAU_SCALE = 0.08
SSA_MAX = 0.98
LOG2E = 1.4426950408889634

F32 = jnp.float32
BF16 = jnp.bfloat16


def recip(x):
    return pl.reciprocal(x, approx=False)


def sum_tiles(x):
    return (x[0:8] + x[8:16]) + (x[16:24] + x[24:32])


def surface_kernel(parent_ref, area_ref, albedo_ref, placed_ref, part_ref):
    sub = lax.broadcasted_iota(jnp.int32, (CB, CB), 0)
    for j in range(FINE_BLOCKS):
        parent = parent_ref[j : j + 1, :]
        hot = jnp.where((parent & (CB - 1)) == sub, 1.0, 0.0).astype(BF16)
        area = area_ref[j : j + 1, :]
        terms = jnp.concatenate(
            [area, area * albedo_ref[j, 0:1, :], area * albedo_ref[j, 1:2, :]], axis=0
        )
        first = terms.astype(BF16)
        rest = terms - first.astype(F32)
        second = rest.astype(BF16)
        third = (rest - second.astype(F32)).astype(BF16)
        dims = (((1,), (1,)), ((), ()))
        total = lax.dot_general(first, hot, dims, preferred_element_type=F32)
        total = total + (
            lax.dot_general(second, hot, dims, preferred_element_type=F32)
            + lax.dot_general(third, hot, dims, preferred_element_type=F32)
        )
        for row in range(3):
            part_ref[row, j : j + 1, :] = total[row : row + 1, :]
    area = part_ref[0]
    here = area > 0.0
    safe = jnp.where(here, area, 1.0)
    owner = parent_ref[:, 0:1] >> 7
    slot = lax.broadcasted_iota(jnp.int32, (FINE_BLOCKS, NBLK * NB), 1)
    where_to = jnp.where(owner == slot, 1.0, 0.0).astype(BF16)
    for s in range(2):
        albedo = jnp.where(here, part_ref[1 + s] / safe, 0.0).astype(BF16)
        dense = lax.dot_general(
            where_to, albedo, (((0,), (0,)), ((), ())), preferred_element_type=F32
        ).astype(BF16)
        for d in range(NBLK):
            placed_ref[d, s] = dense[d * NB : (d + 1) * NB]


def surface(parent_of, fine_area, fine_albedo):
    return pl.pallas_call(
        surface_kernel,
        out_shape=jax.ShapeDtypeStruct((NBLK, 2, NB, CB), BF16),
        scratch_shapes=[pltpu.VMEM((3, FINE_BLOCKS, CB), F32)],
        name="surface",
    )(
        parent_of.reshape(FINE_BLOCKS, CB),
        fine_area.reshape(FINE_BLOCKS, CB),
        fine_albedo.reshape(2, FINE_BLOCKS, CB).transpose(1, 0, 2),
    )


def expand_weight(w_ref, wide_ref):
    row = lax.broadcasted_iota(jnp.int32, (F, F * HALF), 0)
    col = lax.broadcasted_iota(jnp.int32, (F, F * HALF), 1)
    spread = jnp.where(col // HALF == row, 1.0, 0.0).astype(BF16)
    wide = lax.dot_general(
        w_ref[...], spread, (((0,), (0,)), ((), ())), preferred_element_type=F32
    )
    level = lax.broadcasted_iota(jnp.int32, (2 * G, F * HALF), 1) % HALF
    for l in range(HALF):
        wide_ref[l * 2 * G : (l + 1) * 2 * G, :] = jnp.where(level == l, wide, 0.0).astype(BF16)


def solar_column(solar_ref):
    row = lax.broadcasted_iota(jnp.int32, (G, G), 0)
    col = lax.broadcasted_iota(jnp.int32, (G, G), 1)
    return jnp.sum(jnp.where(row == col, solar_ref[...], 0.0), axis=1, keepdims=True)


def layer_terms(mix_depth, mix_albedo, slant_rate):
    scaled = mix_depth * LOG2E
    soft = jnp.maximum(scaled, jnp.log2(1.0 + jnp.exp2(jnp.minimum(scaled, 60.0))))
    e_dir = jnp.exp2(soft * slant_rate)
    c = 2.0 * TAU_SCALE
    bend = jnp.tanh(0.5 * mix_albedo)
    half = 0.5 * SSA_MAX
    share = 1.25 + 0.75 * ASYM - 1.0
    lower = c * (1.0 - half) - (c * half) * bend
    upper = c * (1.0 - half * share) - (c * half * share) * bend
    product = lower * upper
    root = product * lax.rsqrt(product)
    damping = jnp.exp2(-(root * soft))
    gamma_one = lower + upper
    gamma_two = upper - lower
    rate = root + root
    plus = gamma_one + rate
    minus = gamma_one - rate
    damped_sq = damping * damping
    divisor = plus - minus * damped_sq
    mirrored = plus * damped_sq - minus
    reflect = gamma_two - gamma_two * damped_sq
    transmit = (rate + rate) * damping
    return e_dir, gamma_two, divisor, mirrored, reflect, transmit


def eliminate(mixes, cosine, solar, store, esum):
    slant_rate = -TAU_SCALE / cosine
    back_share = 0.5 * (1.0 - ASYM * cosine)
    scale = 1.0 / (2.0 * TAU_SCALE * (1.0 - (1.25 + 0.75 * ASYM - 1.0)))
    rising = back_share * scale
    falling = (1.0 - back_share) * scale
    direct = solar * cosine
    above = jnp.zeros((G, CB), F32)
    source = jnp.zeros((G, CB), F32)
    for l in range(LEV):
        mix_depth, mix_albedo = mixes(l)
        e_dir, gamma_two, divisor, mirrored, reflect, transmit = layer_terms(
            mix_depth, mix_albedo, slant_rate
        )
        esum[l] = sum_tiles(direct + source)
        below = direct * e_dir
        scattered = gamma_two * (direct - below)
        up_source = scattered * rising
        inverse = recip(divisor - above * reflect)
        through = transmit * inverse
        offset = (reflect * source + divisor * up_source) * inverse
        store(l, above, through, offset)
        source = scattered * falling + through * (source + above * up_source)
        above = (reflect + above * mirrored) * inverse
        direct = below
    esum[LEV] = sum_tiles(direct + source)
    return above, source, direct


def substitute(load, esum, above, source, direct, albedo_direct, albedo_diffuse, lit, put):
    upward = (albedo_diffuse * source + albedo_direct * direct) * recip(
        1.0 - albedo_diffuse * above
    )
    for l in range(LEV, -1, -1):
        if l < LEV:
            above, through, offset = load(l)
            upward = through * upward + offset
        down = jnp.sum(esum[l] + sum_tiles(above * upward), axis=0, keepdims=True)
        up = jnp.sum(sum_tiles(upward), axis=0, keepdims=True)
        put(l, down * lit, up * lit)


def mix_all(gas_ref, wide_ref, mix_ref):
    for half in range(LEV // HALF):
        gas = gas_ref[:, half * HALF : (half + 1) * HALF, :].reshape(F * HALF, CB)
        mix_ref[half] = jnp.dot(wide_ref[...], gas, preferred_element_type=F32)

    def mixes(l):
        at = (l % HALF) * 2 * G
        return (
            mix_ref[l // HALF, at : at + G, :],
            mix_ref[l // HALF, at + G : at + 2 * G, :],
        )

    return mixes


def edge_down_kernel(
    gas_ref, weight_ref, cosine_ref, solar_ref, coef_ref, esum_ref, last_ref, wide_ref, mix_ref
):
    expand_weight(weight_ref, wide_ref)
    cosine_all = cosine_ref[...].astype(F32)
    solar = solar_column(solar_ref)

    def one(e, carry):
        lanes = pl.ds(pl.multiple_of(e * (NB - 1) * CB, CB), CB)
        mixes = mix_all(gas_ref.at[:, :, lanes], wide_ref, mix_ref)
        cosine = jnp.where(e == 0, cosine_all[0:1], cosine_all[NB - 1 : NB])

        def store(l, above, through, offset):
            coef_ref[e, l, 0] = above
            coef_ref[e, l, 1] = through
            coef_ref[e, l, 2] = offset

        above, source, direct = eliminate(mixes, cosine, solar, store, esum_ref.at[e])
        last_ref[e, 0] = above
        last_ref[e, 1] = source
        last_ref[e, 2] = direct
        return carry

    lax.fori_loop(0, 2, one, 0)


IN_VMEM = pl.BlockSpec(memory_space=pltpu.VMEM)


def edge_down(gas_state, weight, cosine, solar):
    return pl.pallas_call(
        edge_down_kernel,
        in_specs=[IN_VMEM] * 4,
        out_specs=[IN_VMEM] * 3,
        out_shape=[
            jax.ShapeDtypeStruct((2, LEV, 3, G, CB), F32),
            jax.ShapeDtypeStruct((2, LEV + 1, 8, CB), F32),
            jax.ShapeDtypeStruct((2, 3, G, CB), F32),
        ],
        scratch_shapes=[
            pltpu.VMEM((2 * G * HALF, F * HALF), BF16),
            pltpu.VMEM((LEV // HALF, 2 * G * HALF, CB), F32),
        ],
        compiler_params=pltpu.CompilerParams(vmem_limit_bytes=16 << 20),
        cost_estimate=pl.CostEstimate(
            flops=60000000, transcendentals=0, bytes_accessed=4000000
        ),
        name="edge_down",
    )(gas_state, weight, cosine, solar)


def gather_albedo(routed_ref, s):
    total = routed_ref[0, s].astype(F32)
    for d in range(1, NBLK):
        total = total + routed_ref[d, s].astype(F32)
    return total


def edge_up_kernel(
    coef_ref, esum_ref, last_ref, routed_ref, daylit_ref, first_ref, final_ref
):
    albedo_direct = gather_albedo(routed_ref, 0)
    albedo_diffuse = gather_albedo(routed_ref, 1)
    lit = daylit_ref[...].astype(F32)
    for e, edge_ref in enumerate((first_ref, final_ref)):
        at = slice(e * (NB - 1), e * (NB - 1) + 1)

        def load(l):
            return coef_ref[e, l, 0], coef_ref[e, l, 1], coef_ref[e, l, 2]

        def put(l, down, up):
            edge_ref[2 * l : 2 * l + 1, :] = down
            edge_ref[2 * l + 1 : 2 * l + 2, :] = up

        edge_ref[ROWS - 8 : ROWS, :] = jnp.zeros((8, CB), F32)
        substitute(
            load,
            esum_ref.at[e],
            last_ref[e, 0],
            last_ref[e, 1],
            last_ref[e, 2],
            albedo_direct[at],
            albedo_diffuse[at],
            lit[at],
            put,
        )


def edge_up(coef, esum, last, routed, daylit):
    return pl.pallas_call(
        edge_up_kernel,
        in_specs=[IN_VMEM] * 5,
        out_specs=[IN_VMEM] * 2,
        out_shape=[jax.ShapeDtypeStruct((ROWS, CB), F32)] * 2,
        compiler_params=pltpu.CompilerParams(vmem_limit_bytes=16 << 20),
        cost_estimate=pl.CostEstimate(flops=4000000, transcendentals=0, bytes_accessed=4000000),
        name="edge_up",
    )(coef, esum, last, routed, daylit)


def correct(block, before, own, after, neighbour_ref, side_ref, put):
    lanes, firsts, lasts, weights = [], [], [], []
    for k in range(3):
        at = neighbour_ref[k : k + 1, :]
        place = ((at >> 7) - block + 1) & (NB - 1)
        lanes.append(jnp.broadcast_to(at & (CB - 1), (8, CB)))
        firsts.append(jnp.broadcast_to(place, (8, CB)) == 0)
        lasts.append(jnp.broadcast_to(place, (8, CB)) == 2)
        weights.append(jnp.broadcast_to(side_ref[k : k + 1, :], (8, CB)))
    for row in range(0, ROWS, 8):
        rows = [part(row) for part in (before, own, after)]
        total = rows[1]
        for k in range(3):
            low, mid, high = [
                jnp.take_along_axis(x, lanes[k], axis=1, mode="promise_in_bounds") for x in rows
            ]
            beside = jnp.where(firsts[k], low, jnp.where(lasts[k], high, mid))
            total = total + weights[k] * (beside - rows[1])
        put(row, total)


def put_rows(out_ref, lanes):
    def put(row, total):
        for l in range(row // 2, min(row // 2 + 4, LEV + 1)):
            at = 2 * l - row
            out_ref[l, :, lanes] = total[at : at + 2]

    return put


def inner_kernel(
    gas_ref,
    weight_ref,
    cosine_ref,
    solar_ref,
    routed_ref,
    daylit_ref,
    first_ref,
    final_ref,
    neighbour_ref,
    side_ref,
    out_ref,
    near_ref,
    wide_ref,
    mix_ref,
    coef_ref,
    esum_ref,
    flux_ref,
    column_ref,
):
    i = pl.program_id(0)

    @pl.when(i == 0)
    def _():
        expand_weight(weight_ref, wide_ref)
        column_ref[0] = cosine_ref[...].astype(F32)
        column_ref[1] = daylit_ref[...].astype(F32)
        column_ref[2] = gather_albedo(routed_ref, 0)
        column_ref[3] = gather_albedo(routed_ref, 1)
        flux_ref[...] = jnp.zeros_like(flux_ref)
        flux_ref[0] = first_ref[...]
        flux_ref[NB - 1] = final_ref[...]

    b = i + 1
    mixes = mix_all(gas_ref, wide_ref, mix_ref)

    def store(l, above, through, offset):
        coef_ref[l, 0] = above
        coef_ref[l, 1] = through
        coef_ref[l, 2] = offset

    def load(l):
        return coef_ref[l, 0], coef_ref[l, 1], coef_ref[l, 2]

    def put(l, down, up):
        flux_ref[b, 2 * l : 2 * l + 1, :] = down
        flux_ref[b, 2 * l + 1 : 2 * l + 2, :] = up

    above, source, direct = eliminate(
        mixes, column_ref[0, pl.ds(b, 1), :], solar_column(solar_ref), store, esum_ref
    )
    substitute(
        load,
        esum_ref,
        above,
        source,
        direct,
        column_ref[2, pl.ds(b, 1), :],
        column_ref[3, pl.ds(b, 1), :],
        column_ref[1, pl.ds(b, 1), :],
        put,
    )

    def finish(block):
        lanes = pl.ds(pl.multiple_of(block * CB, CB), CB)
        correct(
            block,
            lambda row: flux_ref[block - 1, row : row + 8, :],
            lambda row: flux_ref[block, row : row + 8, :],
            lambda row: flux_ref[block + 1, row : row + 8, :],
            neighbour_ref.at[:, lanes],
            side_ref.at[:, lanes],
            put_rows(out_ref, lanes),
        )

    @pl.when(i > 0)
    def _():
        finish(i)

    @pl.when(i == NB - 3)
    def _():
        finish(NB - 2)
        near_ref[0] = flux_ref[1]
        near_ref[1] = flux_ref[NB - 2]


def inner(gas_state, weight, cosine, solar, routed, daylit, first, final, neighbours, side_weight):
    cols = NB * CB
    return pl.pallas_call(
        inner_kernel,
        grid=(NB - 2,),
        in_specs=[
            pl.BlockSpec((F, LEV, CB), lambda i: (0, 0, i + 1)),
            pl.BlockSpec((F, 2 * G), lambda i: (0, 0)),
            pl.BlockSpec((NB, CB), lambda i: (0, 0)),
            pl.BlockSpec((1, G), lambda i: (0, 0)),
            pl.BlockSpec((NBLK, 2, NB, CB), lambda i: (0, 0, 0, 0)),
            pl.BlockSpec((NB, CB), lambda i: (0, 0)),
            pl.BlockSpec((ROWS, CB), lambda i: (0, 0)),
            pl.BlockSpec((ROWS, CB), lambda i: (0, 0)),
            pl.BlockSpec((3, cols), lambda i: (0, 0)),
            pl.BlockSpec((3, cols), lambda i: (0, 0)),
        ],
        out_specs=[
            pl.BlockSpec((LEV + 1, 2, cols), lambda i: (0, 0, 0)),
            pl.BlockSpec((2, ROWS, CB), lambda i: (0, 0, 0)),
        ],
        out_shape=[
            jax.ShapeDtypeStruct((LEV + 1, 2, cols), F32),
            jax.ShapeDtypeStruct((2, ROWS, CB), F32),
        ],
        scratch_shapes=[
            pltpu.VMEM((2 * G * HALF, F * HALF), BF16),
            pltpu.VMEM((LEV // HALF, 2 * G * HALF, CB), F32),
            pltpu.VMEM((LEV, 3, G, CB), F32),
            pltpu.VMEM((LEV + 1, 8, CB), F32),
            pltpu.VMEM((NB, ROWS, CB), F32),
            pltpu.VMEM((4, NB, CB), F32),
        ],
        compiler_params=pltpu.CompilerParams(vmem_limit_bytes=16 << 20),
        cost_estimate=pl.CostEstimate(
            flops=200000000, transcendentals=0, bytes_accessed=4000000
        ),
        name="inner",
    )(gas_state, weight, cosine, solar, routed, daylit, first, final, neighbours, side_weight)


def edge_side_kernel(
    low_ref, high_ref, first_ref, final_ref, near_ref, neighbour_ref, side_ref, full_ref, out_ref
):
    del full_ref
    e = pl.program_id(0)
    start = e == 0

    def pick(one, other):
        return lambda row: jnp.where(start, one[row : row + 8, :], other[row : row + 8, :])

    correct(
        e * (NB - 1),
        pick(low_ref, near_ref.at[1]),
        pick(first_ref, final_ref),
        pick(near_ref.at[0], high_ref),
        neighbour_ref,
        side_ref,
        put_rows(out_ref, slice(0, CB)),
    )


def edge_side(low, high, first, final, near, neighbours, side_weight, full):
    return pl.pallas_call(
        edge_side_kernel,
        grid=(2,),
        in_specs=[pl.BlockSpec((ROWS, CB), lambda e: (0, 0))] * 4
        + [
            pl.BlockSpec((2, ROWS, CB), lambda e: (0, 0, 0)),
            pl.BlockSpec((3, CB), lambda e: (0, (NB - 1) * e)),
            pl.BlockSpec((3, CB), lambda e: (0, (NB - 1) * e)),
            pl.BlockSpec(memory_space=pl.ANY),
        ],
        out_specs=pl.BlockSpec((LEV + 1, 2, CB), lambda e: (0, 0, (NB - 1) * e)),
        out_shape=jax.ShapeDtypeStruct(full.shape, F32),
        input_output_aliases={7: 0},
        compiler_params=pltpu.CompilerParams(vmem_limit_bytes=16 << 20),
        name="edge_side",
    )(low, high, first, final, near, neighbours, side_weight, full)


def local(
    gas_state,
    cos_zenith,
    daylit,
    fine_area,
    fine_albedo,
    parent_of,
    optics_weight,
    solar_weight,
    neighbours,
    side_weight,
):
    cosine = cos_zenith.reshape(NB, CB)
    lit = daylit.reshape(NB, CB)
    solar = solar_weight.reshape(1, G)
    placed = surface(parent_of, fine_area, fine_albedo)
    routed = lax.all_to_all(placed, "blk", 0, 0, tiled=True)
    weight = optics_weight.T
    coef, esum, last = edge_down(gas_state, weight, cosine, solar)
    first, final = edge_up(coef, esum, last, routed, lit)
    count = lax.axis_size("blk")
    forward = [(i, i + 1) for i in range(count - 1)]
    backward = [(i + 1, i) for i in range(count - 1)]
    low = lax.ppermute(final, "blk", forward)
    high = lax.ppermute(first, "blk", backward)
    full, near = inner(
        gas_state, weight, cosine, solar, routed, lit, first, final, neighbours, side_weight
    )
    done = edge_side(low, high, first, final, near, neighbours, side_weight, full)
    return done.transpose(1, 0, 2)


def solution(mesh):
    both = ("grp", "blk")
    in_specs = (
        P(None, None, both),
        P(both),
        P(both),
        P(both),
        P(None, both),
        P(both),
        P(),
        P(),
        P(None, both),
        P(None, both),
    )
    return jax.shard_map(
        local, mesh=mesh, in_specs=in_specs, out_specs=P(None, None, both), check_vma=False
    )
```

```python
import jax
import jax.numpy as jnp
from jax import lax
from jax.experimental import pallas as pl
from jax.experimental.pallas import tpu as pltpu
from jax.sharding import PartitionSpec as P

F = 16
LEV = 32
CB = 128
G = 32
KIDS = 4
NB = 8
NBLK = 8
ROWS = 72
STEP = 8
FINE_BLOCKS = NB * KIDS
COLS = NB * CB

ASYM = 0.8
TAU_SCALE = 0.08
SSA_MAX = 0.98
LOG2E = 1.4426950408889634

SLOPE = 0.5 * (1.25 + 0.75 * ASYM)
UNIT = 0.5 * SLOPE * SSA_MAX
SHIFT = 1.0 / UNIT - 1.0
BETA = 0.375 * (1.0 - ASYM) / SLOPE
RATE = -2.0 * TAU_SCALE * UNIT
SCATTER = UNIT / (0.375 * (1.0 - ASYM))

F32 = jnp.float32
BF16 = jnp.bfloat16
IN_VMEM = pl.BlockSpec(memory_space=pltpu.VMEM)
IN_HBM = pl.BlockSpec(memory_space=pltpu.HBM)
UNREAD = pl.BlockSpec(memory_space=pl.ANY)


def params(mebibytes):
    return pltpu.CompilerParams(vmem_limit_bytes=mebibytes << 20)


def shape(dims, kind=F32):
    return jax.ShapeDtypeStruct(dims, kind)


def sum_tiles(x):
    return (x[0:8] + x[8:16]) + (x[16:24] + x[24:32])


def block_lanes(block):
    return pl.ds(pl.multiple_of(block * CB, CB), CB)


def place_albedo(parent_ref, area_ref, albedo_ref, part_ref, mine):
    sub = lax.broadcasted_iota(jnp.int32, (CB, CB), 0)
    for j in range(FINE_BLOCKS):
        parent = parent_ref[j : j + 1, :]
        hot = jnp.where((parent & (CB - 1)) == sub, 1.0, 0.0).astype(BF16)
        area = area_ref[j : j + 1, :]
        terms = jnp.concatenate(
            [area, area * albedo_ref[j, 0:1, :], area * albedo_ref[j, 1:2, :]], axis=0
        )
        first = terms.astype(BF16)
        rest = terms - first.astype(F32)
        second = rest.astype(BF16)
        third = (rest - second.astype(F32)).astype(BF16)
        dims = (((1,), (1,)), ((), ()))
        total = lax.dot_general(first, hot, dims, preferred_element_type=F32)
        total = total + (
            lax.dot_general(second, hot, dims, preferred_element_type=F32)
            + lax.dot_general(third, hot, dims, preferred_element_type=F32)
        )
        for row in range(3):
            part_ref[row, j : j + 1, :] = total[row : row + 1, :]
    area = part_ref[0]
    here = area > 0.0
    safe = jnp.where(here, area, 1.0)
    owner = (parent_ref[:, 0:1] >> 7) ^ (mine * NB)
    slot = lax.broadcasted_iota(jnp.int32, (FINE_BLOCKS, NBLK * NB), 1)
    where_to = jnp.where(owner == slot, 1.0, 0.0).astype(BF16)
    placed = []
    for s in range(2):
        albedo = jnp.where(here, part_ref[1 + s] / safe, 0.0).astype(BF16)
        placed.append(
            lax.dot_general(
                where_to, albedo, (((0,), (0,)), ((), ())), preferred_element_type=F32
            ).astype(BF16)
        )
    return placed


def spread_weights(weight_ref, wide_ref):
    row = lax.broadcasted_iota(jnp.int32, (F, F * STEP), 0)
    col = lax.broadcasted_iota(jnp.int32, (F, F * STEP), 1)
    spread = jnp.where(col // STEP == row, 1.0, 0.0).astype(BF16)
    depth = lax.broadcasted_iota(jnp.int32, (F, 2 * G), 1) < G
    scaled = weight_ref[...].astype(F32) * jnp.where(depth, LOG2E, 0.5)
    high = scaled.astype(BF16)
    low = (scaled - high.astype(F32)).astype(BF16)
    wide = jnp.concatenate(
        [
            lax.dot_general(x, spread, (((0,), (0,)), ((), ())), preferred_element_type=F32)
            for x in (high, low)
        ],
        axis=1,
    )
    level = lax.broadcasted_iota(jnp.int32, (2 * G, 2 * F * STEP), 1) % STEP
    for l in range(STEP):
        wide_ref[l * 2 * G : (l + 1) * 2 * G, :] = jnp.where(level == l, wide, 0.0).astype(BF16)


def column_constants(cosine, lit, column_ref):
    back = 0.5 * (1.0 - ASYM * cosine)
    column_ref[0] = -TAU_SCALE / cosine
    column_ref[1] = back * SCATTER
    column_ref[2] = (1.0 - back) * SCATTER
    column_ref[3] = cosine
    column_ref[4] = lit


def surface_kernel(
    parent_hbm,
    area_hbm,
    albedo_hbm,
    weight_hbm,
    cosine_hbm,
    lit_hbm,
    solar_hbm,
    neighbour_hbm,
    side_hbm,
    gas_hbm,
    send_ref,
    keep_ref,
    gas_ref,
    wide_ref,
    column_ref,
    solar_ref,
    neighbour_ref,
    side_ref,
    parent_ref,
    area_ref,
    albedo_ref,
    weight_ref,
    cosine_ref,
    lit_ref,
    sun_ref,
    part_ref,
    sems,
):
    pairs = (
        (parent_hbm, parent_ref),
        (area_hbm, area_ref),
        (albedo_hbm, albedo_ref),
        (weight_hbm, weight_ref),
        (cosine_hbm, cosine_ref),
        (lit_hbm, lit_ref),
        (solar_hbm, sun_ref),
        (neighbour_hbm, neighbour_ref),
        (side_hbm, side_ref),
        (gas_hbm, gas_ref),
    )
    copies = [
        pltpu.make_async_copy(source, target, sems.at[i])
        for i, (source, target) in enumerate(pairs)
    ]
    for copy in copies:
        copy.start()
    for copy in copies[:7]:
        copy.wait()
    mine = lax.axis_index("blk")
    placed = place_albedo(parent_ref, area_ref, albedo_ref, part_ref, mine)
    for s in range(2):
        for i in range(NBLK // 2):
            keep_ref[i, s] = placed[s][2 * i * NB : (2 * i + 1) * NB]
            send_ref[i, s] = placed[s][(2 * i + 1) * NB : (2 * i + 2) * NB]
    spread_weights(weight_ref, wide_ref)
    column_constants(cosine_ref[...].astype(F32), lit_ref[...].astype(F32), column_ref)
    row = lax.broadcasted_iota(jnp.int32, (G, G), 0)
    col = lax.broadcasted_iota(jnp.int32, (G, G), 1)
    sun = jnp.sum(jnp.where(row == col, sun_ref[...], 0.0), axis=1, keepdims=True)
    solar_ref[...] = jnp.broadcast_to(sun, (G, CB))
    for copy in copies[7:]:
        copy.wait()


def surface(
    parent_of,
    fine_area,
    fine_albedo,
    optics_weight,
    cos_zenith,
    daylit,
    solar_weight,
    neighbours,
    side_weight,
    gas_state,
):
    return pl.pallas_call(
        surface_kernel,
        in_specs=[IN_HBM] * 10,
        out_specs=[IN_VMEM] * 8,
        out_shape=[
            shape((NBLK // 2, 2, NB, CB), BF16),
            shape((NBLK // 2, 2, NB, CB), BF16),
            shape((F, LEV, COLS), BF16),
            shape((2 * G * STEP, 2 * F * STEP), BF16),
            shape((5, NB, CB)),
            shape((G, CB)),
            shape((3, COLS), jnp.int32),
            shape((3, COLS)),
        ],
        scratch_shapes=[
            pltpu.VMEM((FINE_BLOCKS, CB), jnp.int32),
            pltpu.VMEM((FINE_BLOCKS, CB), F32),
            pltpu.VMEM((FINE_BLOCKS, 2, CB), F32),
            pltpu.VMEM((F, 2 * G), BF16),
            pltpu.VMEM((NB, CB), BF16),
            pltpu.VMEM((NB, CB), jnp.int32),
            pltpu.VMEM((1, G), F32),
            pltpu.VMEM((3, FINE_BLOCKS, CB), F32),
            pltpu.SemaphoreType.DMA((10,)),
        ],
        compiler_params=params(4),
        name="surface",
    )(
        *[
            pltpu.with_memory_space_constraint(x, pltpu.HBM)
            for x in (
                parent_of.reshape(FINE_BLOCKS, CB),
                fine_area.reshape(FINE_BLOCKS, CB),
                fine_albedo.reshape(2, FINE_BLOCKS, CB).transpose(1, 0, 2),
                optics_weight.T,
                cos_zenith.reshape(NB, CB),
                daylit.reshape(NB, CB),
                solar_weight.reshape(1, G),
                neighbours,
                side_weight,
                gas_state,
            )
        ]
    )


def merge_kernel(keep_ref, got_ref, after_ref, send_ref, next_ref):
    del after_ref
    for i in range(keep_ref.shape[0]):
        total = (keep_ref[i].astype(F32) + got_ref[i].astype(F32)).astype(BF16)
        target = send_ref if i % 2 else next_ref
        target[i // 2] = total


def merge(keep, got, after):
    half = shape((keep.shape[0] // 2,) + keep.shape[1:], BF16)
    return pl.pallas_call(
        merge_kernel,
        in_specs=[IN_VMEM, IN_VMEM, UNREAD],
        out_specs=[IN_VMEM] * 2,
        out_shape=[half, half],
        compiler_params=params(2),
        name="merge",
    )(keep, got, after)


def layer_terms(depth_mix, albedo_mix, slant_rate):
    soft = jnp.maximum(depth_mix, jnp.log2(1.0 + jnp.exp2(jnp.minimum(depth_mix, 60.0))))
    e_dir = jnp.exp2(soft * slant_rate)
    bend = jnp.tanh(albedo_mix)
    gamma_one = SHIFT - bend
    gamma_two = BETA * bend + BETA
    product = (gamma_one - gamma_two) * (gamma_one + gamma_two)
    root = product * lax.rsqrt(product)
    damping = jnp.exp2(RATE * (root * soft))
    plus = gamma_one + root
    minus = gamma_one - root
    damped_sq = damping * damping
    divisor = plus - minus * damped_sq
    mirrored = plus * damped_sq - minus
    reflect = gamma_two - gamma_two * damped_sq
    transmit = (root + root) * damping
    return e_dir, gamma_two, divisor, mirrored, reflect, transmit


def mix_all(gas_ref, lanes, wide_ref):
    products = []
    for step in range(LEV // STEP):
        gas = gas_ref[:, step * STEP : (step + 1) * STEP, lanes].reshape(F * STEP, CB)
        products.append(
            jnp.dot(
                wide_ref[...],
                jnp.concatenate([gas, gas], axis=0),
                preferred_element_type=F32,
            )
        )
    return products


def eliminate(block, gas_ref, wide_ref, column_ref, solar_ref, coef_ref, esum_ref, state_ref):
    products = mix_all(gas_ref, block_lanes(block), wide_ref)
    slant_rate, rising, falling, cosine = [
        column_ref[i, pl.ds(block, 1), :] for i in range(4)
    ]
    direct = solar_ref[...] * cosine
    above = jnp.zeros((G, CB), F32)
    source = jnp.zeros((G, CB), F32)
    for l in range(LEV):
        at = (l % STEP) * 2 * G
        mix = products[l // STEP]
        e_dir, gamma_two, divisor, mirrored, reflect, transmit = layer_terms(
            mix[at : at + G], mix[at + G : at + 2 * G], slant_rate
        )
        esum_ref[l] = sum_tiles(direct + source)
        below = direct * e_dir
        scattered = gamma_two * (direct - below)
        up_source = scattered * rising
        inverse = pl.reciprocal(divisor - above * reflect, approx=False)
        incident = (source + above * up_source) * inverse
        coef_ref[l, 0] = above
        coef_ref[l, 1] = transmit * inverse
        coef_ref[l, 2] = up_source + reflect * incident
        source = scattered * falling + transmit * incident
        above = (reflect + above * mirrored) * inverse
        direct = below
    esum_ref[LEV] = sum_tiles(direct + source)
    state_ref[0] = above
    state_ref[1] = source
    state_ref[2] = direct


def add_sublanes(rows):
    sub = lax.broadcasted_iota(jnp.int32, (8, CB), 0)
    four, two, one = sub < 4, (sub & 2) == 0, (sub & 1) == 0
    rows = [
        jnp.where(four, rows[r], rows[r + 4])
        + pltpu.roll(jnp.where(four, rows[r + 4], rows[r]), 4, 0)
        for r in range(4)
    ]
    rows = [
        jnp.where(
            two,
            rows[r] + pltpu.roll(rows[r], 6, 0),
            rows[r + 2] + pltpu.roll(rows[r + 2], 2, 0),
        )
        for r in range(2)
    ]
    return jnp.where(
        one, rows[0] + pltpu.roll(rows[0], 7, 0), rows[1] + pltpu.roll(rows[1], 1, 0)
    )


def substitute(coef_ref, esum_ref, state_ref, albedo_direct, albedo_diffuse, lit, flux_ref):
    above, source, direct = state_ref[0], state_ref[1], state_ref[2]
    upward = (albedo_diffuse * source + albedo_direct * direct) * pl.reciprocal(
        1.0 - albedo_diffuse * above, approx=False
    )
    none = jnp.zeros((8, CB), F32)
    pending = [esum_ref[LEV] + sum_tiles(above * upward), sum_tiles(upward)] + [none] * 6
    flux_ref[2 * LEV : 2 * LEV + 8, :] = add_sublanes(pending) * lit
    pending = []
    for l in range(LEV - 1, -1, -1):
        upward = coef_ref[l, 1] * upward + coef_ref[l, 2]
        pending = [
            esum_ref[l] + sum_tiles(coef_ref[l, 0] * upward),
            sum_tiles(upward),
        ] + pending
        if l % 4 == 0:
            flux_ref[2 * l : 2 * l + 8, :] = add_sublanes(pending) * lit
            pending = []


COEF = (LEV, 3, G, CB)
ESUM = (LEV + 1, 8, CB)
STATE = (3, G, CB)


def down_kernel(block):
    def kernel(gas_ref, wide_ref, column_ref, solar_ref, after_ref, coef_ref, esum_ref, state_ref):
        del after_ref
        eliminate(block, gas_ref, wide_ref, column_ref, solar_ref, coef_ref, esum_ref, state_ref)

    return kernel


def down(block, gas, wide, column, solar, after):
    return pl.pallas_call(
        down_kernel(block),
        in_specs=[IN_VMEM] * 4 + [UNREAD],
        out_specs=[IN_VMEM] * 3,
        out_shape=[shape(COEF), shape(ESUM), shape(STATE)],
        compiler_params=params(6),
        cost_estimate=pl.CostEstimate(
            flops=200000000, transcendentals=0, bytes_accessed=4000000
        ),
        name="down",
    )(gas, wide, column, solar, after)


EARLY = (0, NB - 1, 1)


def up_kernel(*refs):
    parts, (keep_ref, got_ref, column_ref), flux_refs, (albedo_ref,) = (
        [refs[3 * i : 3 * i + 3] for i in range(3)],
        refs[9:12],
        refs[12:15],
        refs[15:16],
    )
    for s in range(2):
        albedo_ref[s] = keep_ref[0, s].astype(F32) + got_ref[0, s].astype(F32)
    for block, part, flux_ref in zip(EARLY, parts, flux_refs):
        at = slice(block, block + 1)
        substitute(
            *part, albedo_ref[0, at, :], albedo_ref[1, at, :], column_ref[4, at, :], flux_ref
        )


def up(parts, keep, got, column):
    return pl.pallas_call(
        up_kernel,
        in_specs=[IN_VMEM] * 12,
        out_specs=[IN_VMEM] * 4,
        out_shape=[shape((ROWS, CB))] * 3 + [shape((2, NB, CB))],
        compiler_params=params(2),
        cost_estimate=pl.CostEstimate(flops=4000000, transcendentals=0, bytes_accessed=4000000),
        name="up",
    )(*[x for part in parts for x in part], keep, got, column)


def correct(block, before, own, after, neighbour_ref, side_ref, out_ref):
    lanes = block_lanes(block)
    at_lane, firsts, lasts, weights = [], [], [], []
    for k in range(3):
        at = jnp.broadcast_to(neighbour_ref[k : k + 1, lanes], (8, CB))
        place = ((at >> 7) - block + 1) & (NB - 1)
        at_lane.append(at & (CB - 1))
        firsts.append(place == 0)
        lasts.append(place == 2)
        weights.append(jnp.broadcast_to(side_ref[k : k + 1, lanes], (8, CB)))
    for row in range(0, ROWS, 8):
        rows = [part[row : row + 8, :] for part in (before, own, after)]
        total = rows[1]
        for k in range(3):
            low, mid, high = [
                jnp.take_along_axis(x, at_lane[k], axis=1, mode="promise_in_bounds")
                for x in rows
            ]
            beside = jnp.where(firsts[k], low, jnp.where(lasts[k], high, mid))
            total = total + weights[k] * (beside - rows[1])
        for l in range(row // 2, min(row // 2 + 4, LEV + 1)):
            out_ref[l, :, lanes] = total[2 * l - row : 2 * l - row + 2]


def inner_kernel(
    gas_ref,
    wide_ref,
    column_ref,
    solar_ref,
    albedo_ref,
    first_ref,
    final_ref,
    second_ref,
    neighbour_ref,
    side_ref,
    out_ref,
    near_ref,
    coef_ref,
    esum_ref,
    state_ref,
    flux_ref,
):
    flux_ref[0] = first_ref[...]
    flux_ref[1] = second_ref[...]
    flux_ref[NB - 1] = final_ref[...]

    def start(n):
        at = n % 2
        eliminate(
            n,
            gas_ref,
            wide_ref,
            column_ref,
            solar_ref,
            coef_ref.at[at],
            esum_ref.at[at],
            state_ref.at[at],
        )

    def finish(n):
        at = n % 2
        row = pl.ds(n, 1)
        substitute(
            coef_ref.at[at],
            esum_ref.at[at],
            state_ref.at[at],
            albedo_ref[0, row, :],
            albedo_ref[1, row, :],
            column_ref[4, row, :],
            flux_ref.at[n],
        )

    def side(n):
        correct(
            n,
            flux_ref.at[(n + NB - 1) % NB],
            flux_ref.at[n],
            flux_ref.at[n + 1],
            neighbour_ref,
            side_ref,
            out_ref,
        )

    start(2)

    def turn(n, carry):
        start(n)
        finish(n - 1)
        side(n - 3)
        return carry

    lax.fori_loop(3, NB - 1, turn, 0)
    finish(NB - 2)
    for n in range(NB - 4, NB - 1):
        side(n)
    near_ref[0] = flux_ref[1]
    near_ref[1] = flux_ref[NB - 2]


def inner(gas, wide, column, solar, albedo, first, final, second, neighbours, side_weight):
    return pl.pallas_call(
        inner_kernel,
        in_specs=[IN_VMEM] * 10,
        out_specs=[IN_VMEM] * 2,
        out_shape=[shape((LEV + 1, 2, COLS)), shape((2, ROWS, CB))],
        scratch_shapes=[
            pltpu.VMEM((2,) + COEF, F32),
            pltpu.VMEM((2,) + ESUM, F32),
            pltpu.VMEM((2,) + STATE, F32),
            pltpu.VMEM((NB, ROWS, CB), F32),
        ],
        compiler_params=params(10),
        cost_estimate=pl.CostEstimate(
            flops=2000000000, transcendentals=0, bytes_accessed=4000000
        ),
        name="inner",
    )(gas, wide, column, solar, albedo, first, final, second, neighbours, side_weight)


def edge_side_kernel(
    low_ref,
    high_ref,
    first_ref,
    final_ref,
    near_ref,
    neighbour_ref,
    side_ref,
    full_ref,
    out_hbm,
    edge_ref,
    sems,
):
    middle = pl.ds(CB, COLS - 2 * CB)
    copies = [
        pltpu.make_async_copy(full_ref.at[:, :, middle], out_hbm.at[:, :, middle], sems.at[0])
    ]
    copies[0].start()
    edges = (
        (0, low_ref, first_ref, near_ref.at[0]),
        (NB - 1, near_ref.at[1], final_ref, high_ref),
    )
    for i, (block, before, own, after) in enumerate(edges):
        correct(block, before, own, after, neighbour_ref, side_ref, edge_ref)
        lanes = pl.ds(block * CB, CB)
        copies.append(
            pltpu.make_async_copy(
                edge_ref.at[:, :, lanes], out_hbm.at[:, :, lanes], sems.at[1 + i]
            )
        )
        copies[-1].start()
    for copy in copies:
        copy.wait()


def edge_side(low, high, first, final, near, neighbours, side_weight, full):
    return pl.pallas_call(
        edge_side_kernel,
        in_specs=[IN_VMEM] * 8,
        out_specs=IN_HBM,
        out_shape=shape((LEV + 1, 2, COLS)),
        scratch_shapes=[
            pltpu.VMEM((LEV + 1, 2, COLS), F32),
            pltpu.SemaphoreType.DMA((3,)),
        ],
        compiler_params=params(4),
        name="edge_side",
    )(low, high, first, final, near, neighbours, side_weight, full)


def exchange(x, bit):
    count = lax.axis_size("blk")
    return lax.ppermute(x, "blk", [(i, i ^ bit) for i in range(count)])


def local(
    gas_state,
    cos_zenith,
    daylit,
    fine_area,
    fine_albedo,
    parent_of,
    optics_weight,
    solar_weight,
    neighbours,
    side_weight,
):
    send, keep, gas, wide, column, solar, beside, weights = surface(
        parent_of,
        fine_area,
        fine_albedo,
        optics_weight,
        cos_zenith,
        daylit,
        solar_weight,
        neighbours,
        side_weight,
        gas_state,
    )
    parts = []
    for i, block in enumerate(EARLY):
        got = exchange(send, 1 << i)
        parts.append(down(block, gas, wide, column, solar, keep))
        if i < 2:
            send, keep = merge(keep, got, parts[-1][2])
    first, final, second, albedo = up(parts, keep, got, column)
    count = lax.axis_size("blk")
    low = lax.ppermute(final, "blk", [(i, (i + 1) % count) for i in range(count)])
    high = lax.ppermute(first, "blk", [((i + 1) % count, i) for i in range(count)])
    full, near = inner(
        gas, wide, column, solar, albedo, first, final, second, beside, weights
    )
    done = edge_side(low, high, first, final, near, beside, weights, full)
    return done.transpose(1, 0, 2)


def solution(mesh):
    both = ("grp", "blk")
    in_specs = (
        P(None, None, both),
        P(both),
        P(both),
        P(both),
        P(None, both),
        P(both),
        P(),
        P(),
        P(None, both),
        P(None, both),
    )
    return jax.shard_map(
        local, mesh=mesh, in_specs=in_specs, out_specs=P(None, None, both), check_vma=False
    )
```

```python
import jax
import jax.numpy as jnp
from jax import lax
from jax.experimental import pallas as pl
from jax.experimental.pallas import tpu as pltpu
from jax.sharding import PartitionSpec as P

F = 16
LEV = 32
CB = 128
G = 32
KIDS = 4
NB = 8
NBLK = 8
ROWS = 72
STEP = 8
FINE_BLOCKS = NB * KIDS
COLS = NB * CB

ASYM = 0.8
TAU_SCALE = 0.08
SSA_MAX = 0.98
LOG2E = 1.4426950408889634

SLOPE = 0.5 * (1.25 + 0.75 * ASYM)
UNIT = 0.5 * SLOPE * SSA_MAX
SHIFT = 1.0 / UNIT - 1.0
BETA = 0.375 * (1.0 - ASYM) / SLOPE
RATE = -2.0 * TAU_SCALE * UNIT
SCATTER = UNIT / (0.375 * (1.0 - ASYM))

F32 = jnp.float32
BF16 = jnp.bfloat16
IN_VMEM = pl.BlockSpec(memory_space=pltpu.VMEM)
IN_HBM = pl.BlockSpec(memory_space=pltpu.HBM)
UNREAD = pl.BlockSpec(memory_space=pl.ANY)


def params(mebibytes):
    return pltpu.CompilerParams(vmem_limit_bytes=mebibytes << 20)


def shape(dims, kind=F32):
    return jax.ShapeDtypeStruct(dims, kind)


def sum_tiles(x):
    return (x[0:8] + x[8:16]) + (x[16:24] + x[24:32])


def block_lanes(block):
    return pl.ds(pl.multiple_of(block * CB, CB), CB)


def place_albedo(parent_ref, area_ref, albedo_ref, mine):
    sub = lax.broadcasted_iota(jnp.int32, (CB, CB), 0).astype(F32).astype(BF16)
    line = lax.broadcasted_iota(jnp.int32, (8, CB), 0)
    one, zero = jnp.ones((), BF16), jnp.zeros((), BF16)
    totals = [[], [], []]
    for group in range(0, FINE_BLOCKS, 8):
        rows = slice(group, group + 8)
        area = area_ref[rows, :]
        terms = [area, area * albedo_ref[0, rows, :], area * albedo_ref[1, rows, :]]
        pieces = []
        for term in terms:
            for _ in range(3):
                piece = term.astype(BF16).astype(F32)
                pieces.append(piece)
                term = term - piece
        column = (parent_ref[rows, :] & (CB - 1)).astype(F32).astype(BF16)
        hots, values = [], []
        for j in range(8):
            hots.append(
                jnp.where(jnp.broadcast_to(column[j : j + 1, :], (CB, CB)) == sub, one, zero)
            )
            values.append(
                jnp.concatenate([jnp.where(line == j, x, 0.0) for x in pieces], axis=0).astype(
                    BF16
                )
            )
        total = lax.dot_general(
            jnp.concatenate(values, axis=1),
            jnp.concatenate(hots, axis=1),
            (((1,), (1,)), ((), ())),
            preferred_element_type=F32,
        )
        for i in range(3):
            at = 24 * i
            totals[i].append(
                total[at : at + 8] + (total[at + 8 : at + 16] + total[at + 16 : at + 24])
            )
    area = jnp.concatenate(totals[0], axis=0)
    here = area > 0.0
    safe = jnp.where(here, area, 1.0)
    owner = (parent_ref[:, 0:1] >> 7) ^ (mine * NB)
    slot = lax.broadcasted_iota(jnp.int32, (FINE_BLOCKS, NBLK * NB), 1)
    where_to = jnp.where(owner == slot, 1.0, 0.0).astype(BF16)
    placed = []
    for s in range(2):
        total = jnp.concatenate(totals[1 + s], axis=0)
        albedo = jnp.where(here, total / safe, 0.0).astype(BF16)
        placed.append(
            lax.dot_general(
                where_to, albedo, (((0,), (0,)), ((), ())), preferred_element_type=F32
            ).astype(BF16)
        )
    return placed


def spread_weights(weight_ref, wide_ref):
    row = lax.broadcasted_iota(jnp.int32, (F, F * STEP), 0)
    col = lax.broadcasted_iota(jnp.int32, (F, F * STEP), 1)
    spread = jnp.where(col // STEP == row, 1.0, 0.0).astype(BF16)
    depth = lax.broadcasted_iota(jnp.int32, (F, 2 * G), 1) < G
    scaled = weight_ref[...].astype(F32) * jnp.where(depth, LOG2E, 0.5)
    high = scaled.astype(BF16)
    low = (scaled - high.astype(F32)).astype(BF16)
    wide = jnp.concatenate(
        [
            lax.dot_general(x, spread, (((0,), (0,)), ((), ())), preferred_element_type=F32)
            for x in (high, low)
        ],
        axis=1,
    )
    level = lax.broadcasted_iota(jnp.int32, (2 * G, 2 * F * STEP), 1) % STEP
    for l in range(STEP):
        wide_ref[l * 2 * G : (l + 1) * 2 * G, :] = jnp.where(level == l, wide, 0.0).astype(BF16)


def column_constants(cosine, lit, column_ref):
    back = 0.5 * (1.0 - ASYM * cosine)
    column_ref[0] = -TAU_SCALE / cosine
    column_ref[1] = back * SCATTER
    column_ref[2] = (1.0 - back) * SCATTER
    column_ref[3] = cosine
    column_ref[4] = lit


def surface_kernel(
    parent_hbm,
    area_hbm,
    albedo_hbm,
    weight_hbm,
    cosine_hbm,
    lit_hbm,
    solar_hbm,
    neighbour_hbm,
    side_hbm,
    gas_hbm,
    send_ref,
    keep_ref,
    gas_ref,
    wide_ref,
    column_ref,
    solar_ref,
    neighbour_ref,
    side_ref,
    parent_ref,
    area_ref,
    albedo_ref,
    weight_ref,
    cosine_ref,
    lit_ref,
    sun_ref,
    sems,
):
    pairs = (
        (parent_hbm, parent_ref),
        (area_hbm, area_ref),
        (albedo_hbm.at[:, 0, :], albedo_ref.at[0]),
        (albedo_hbm.at[:, 1, :], albedo_ref.at[1]),
        (weight_hbm, weight_ref),
        (cosine_hbm, cosine_ref),
        (lit_hbm, lit_ref),
        (solar_hbm, sun_ref),
        (neighbour_hbm, neighbour_ref),
        (side_hbm, side_ref),
        (gas_hbm, gas_ref),
    )
    copies = [
        pltpu.make_async_copy(source, target, sems.at[i])
        for i, (source, target) in enumerate(pairs)
    ]
    for copy in copies:
        copy.start()
    for copy in copies[:8]:
        copy.wait()
    mine = lax.axis_index("blk")
    placed = place_albedo(parent_ref, area_ref, albedo_ref, mine)
    for s in range(2):
        for i in range(NBLK // 2):
            keep_ref[i, s] = placed[s][2 * i * NB : (2 * i + 1) * NB]
            send_ref[i, s] = placed[s][(2 * i + 1) * NB : (2 * i + 2) * NB]
    spread_weights(weight_ref, wide_ref)
    column_constants(cosine_ref[...].astype(F32), lit_ref[...].astype(F32), column_ref)
    row = lax.broadcasted_iota(jnp.int32, (G, G), 0)
    col = lax.broadcasted_iota(jnp.int32, (G, G), 1)
    sun = jnp.sum(jnp.where(row == col, sun_ref[...], 0.0), axis=1, keepdims=True)
    solar_ref[...] = jnp.broadcast_to(sun, (G, CB))
    for copy in copies[8:]:
        copy.wait()


def surface(
    parent_of,
    fine_area,
    fine_albedo,
    optics_weight,
    cos_zenith,
    daylit,
    solar_weight,
    neighbours,
    side_weight,
    gas_state,
):
    return pl.pallas_call(
        surface_kernel,
        in_specs=[IN_HBM] * 10,
        out_specs=[IN_VMEM] * 8,
        out_shape=[
            shape((NBLK // 2, 2, NB, CB), BF16),
            shape((NBLK // 2, 2, NB, CB), BF16),
            shape((F, LEV, COLS), BF16),
            shape((2 * G * STEP, 2 * F * STEP), BF16),
            shape((5, NB, CB)),
            shape((G, CB)),
            shape((3, COLS), jnp.int32),
            shape((3, COLS)),
        ],
        scratch_shapes=[
            pltpu.VMEM((FINE_BLOCKS, CB), jnp.int32),
            pltpu.VMEM((FINE_BLOCKS, CB), F32),
            pltpu.VMEM((2, FINE_BLOCKS, CB), F32),
            pltpu.VMEM((F, 2 * G), BF16),
            pltpu.VMEM((NB, CB), BF16),
            pltpu.VMEM((NB, CB), jnp.int32),
            pltpu.VMEM((1, G), F32),
            pltpu.SemaphoreType.DMA((11,)),
        ],
        compiler_params=params(4),
        name="surface",
    )(
        *[
            pltpu.with_memory_space_constraint(x, pltpu.HBM)
            for x in (
                parent_of.reshape(FINE_BLOCKS, CB),
                fine_area.reshape(FINE_BLOCKS, CB),
                fine_albedo.reshape(2, FINE_BLOCKS, CB).transpose(1, 0, 2),
                optics_weight.T,
                cos_zenith.reshape(NB, CB),
                daylit.reshape(NB, CB),
                solar_weight.reshape(1, G),
                neighbours,
                side_weight,
                gas_state,
            )
        ]
    )


def merge_kernel(keep_ref, got_ref, after_ref, send_ref, next_ref):
    del after_ref
    for i in range(keep_ref.shape[0]):
        total = (keep_ref[i].astype(F32) + got_ref[i].astype(F32)).astype(BF16)
        target = send_ref if i % 2 else next_ref
        target[i // 2] = total


def merge(keep, got, after):
    half = shape((keep.shape[0] // 2,) + keep.shape[1:], BF16)
    return pl.pallas_call(
        merge_kernel,
        in_specs=[IN_VMEM, IN_VMEM, UNREAD],
        out_specs=[IN_VMEM] * 2,
        out_shape=[half, half],
        compiler_params=params(2),
        name="merge",
    )(keep, got, after)


def layer_terms(depth_mix, albedo_mix, slant_rate):
    soft = jnp.maximum(depth_mix, jnp.log2(1.0 + jnp.exp2(jnp.minimum(depth_mix, 60.0))))
    e_dir = jnp.exp2(soft * slant_rate)
    bend = jnp.tanh(albedo_mix)
    gamma_one = SHIFT - bend
    gamma_two = BETA * bend + BETA
    product = (gamma_one - gamma_two) * (gamma_one + gamma_two)
    root = product * lax.rsqrt(product)
    damping = jnp.exp2(RATE * (root * soft))
    damped_sq = damping * damping
    lost = 1.0 - damped_sq
    even = root + root * damped_sq
    odd = gamma_one * lost
    transmit = (root + root) * damping
    return e_dir, gamma_two, even + odd, even - odd, gamma_two * lost, transmit


def mix_all(gas_ref, lanes, wide_ref):
    products = []
    for step in range(LEV // STEP):
        gas = gas_ref[:, step * STEP : (step + 1) * STEP, lanes].reshape(F * STEP, CB)
        products.append(
            jnp.dot(
                wide_ref[...],
                jnp.concatenate([gas, gas], axis=0),
                preferred_element_type=F32,
            )
        )
    return products


def eliminate(block, gas_ref, wide_ref, column_ref, solar_ref, coef_ref, esum_ref, state_ref):
    products = mix_all(gas_ref, block_lanes(block), wide_ref)
    slant_rate, rising, falling, cosine = [
        column_ref[i, pl.ds(block, 1), :] for i in range(4)
    ]
    direct = solar_ref[...] * cosine
    above = jnp.zeros((G, CB), F32)
    source = jnp.zeros((G, CB), F32)
    for l in range(LEV):
        at = (l % STEP) * 2 * G
        mix = products[l // STEP]
        e_dir, gamma_two, divisor, mirrored, reflect, transmit = layer_terms(
            mix[at : at + G], mix[at + G : at + 2 * G], slant_rate
        )
        esum_ref[l] = sum_tiles(direct + source)
        below = direct * e_dir
        scattered = gamma_two * (direct - below)
        up_source = scattered * rising
        inverse = pl.reciprocal(divisor - above * reflect, approx=False)
        incident = (source + above * up_source) * inverse
        coef_ref[l, 0] = above
        coef_ref[l, 1] = transmit * inverse
        coef_ref[l, 2] = up_source + reflect * incident
        source = scattered * falling + transmit * incident
        above = (reflect + above * mirrored) * inverse
        direct = below
    esum_ref[LEV] = sum_tiles(direct + source)
    state_ref[0] = above
    state_ref[1] = source
    state_ref[2] = direct


def add_sublanes(rows):
    sub = lax.broadcasted_iota(jnp.int32, (8, CB), 0)
    four, two, one = sub < 4, (sub & 2) == 0, (sub & 1) == 0
    rows = [
        jnp.where(four, rows[r], rows[r + 4])
        + pltpu.roll(jnp.where(four, rows[r + 4], rows[r]), 4, 0)
        for r in range(4)
    ]
    rows = [
        jnp.where(
            two,
            rows[r] + pltpu.roll(rows[r], 6, 0),
            rows[r + 2] + pltpu.roll(rows[r + 2], 2, 0),
        )
        for r in range(2)
    ]
    return jnp.where(
        one, rows[0] + pltpu.roll(rows[0], 7, 0), rows[1] + pltpu.roll(rows[1], 1, 0)
    )


def substitute(coef_ref, esum_ref, state_ref, albedo_direct, albedo_diffuse, lit, flux_ref):
    above, source, direct = state_ref[0], state_ref[1], state_ref[2]
    upward = (albedo_diffuse * source + albedo_direct * direct) * pl.reciprocal(
        1.0 - albedo_diffuse * above, approx=False
    )
    none = jnp.zeros((8, CB), F32)
    pending = [esum_ref[LEV] + sum_tiles(above * upward), sum_tiles(upward)] + [none] * 6
    flux_ref[2 * LEV : 2 * LEV + 8, :] = add_sublanes(pending) * lit
    pending = []
    for l in range(LEV - 1, -1, -1):
        upward = coef_ref[l, 1] * upward + coef_ref[l, 2]
        pending = [
            esum_ref[l] + sum_tiles(coef_ref[l, 0] * upward),
            sum_tiles(upward),
        ] + pending
        if l % 4 == 0:
            flux_ref[2 * l : 2 * l + 8, :] = add_sublanes(pending) * lit
            pending = []


COEF = (LEV, 3, G, CB)
ESUM = (LEV + 1, 8, CB)
STATE = (3, G, CB)


def down_kernel(blocks):
    def kernel(gas_ref, wide_ref, column_ref, solar_ref, after_ref, coef_ref, esum_ref, state_ref):
        del after_ref
        for i, block in enumerate(blocks):
            eliminate(
                block,
                gas_ref,
                wide_ref,
                column_ref,
                solar_ref,
                coef_ref.at[i],
                esum_ref.at[i],
                state_ref.at[i],
            )

    return kernel


def down(blocks, gas, wide, column, solar, after):
    count = len(blocks)
    return pl.pallas_call(
        down_kernel(blocks),
        in_specs=[IN_VMEM] * 4 + [UNREAD],
        out_specs=[IN_VMEM] * 3,
        out_shape=[shape((count,) + x) for x in (COEF, ESUM, STATE)],
        compiler_params=params(24),
        cost_estimate=pl.CostEstimate(
            flops=200000000 * count, transcendentals=0, bytes_accessed=4000000
        ),
        name="down",
    )(gas, wide, column, solar, after)


WINDOWS = ((0,), (NB - 1, 1), (2, 3, 4))
LATE = (5, 6)


def ground(albedo_ref, column_ref, block):
    row = slice(block, block + 1)
    return albedo_ref[0, row, :], albedo_ref[1, row, :], column_ref[4, row, :]


def up_kernel(
    coef_a,
    esum_a,
    state_a,
    coef_b,
    esum_b,
    state_b,
    keep_ref,
    got_ref,
    column_ref,
    first_ref,
    final_ref,
    near_ref,
    far_ref,
    albedo_ref,
):
    for s in range(2):
        albedo_ref[s] = keep_ref[0, s].astype(F32) + got_ref[0, s].astype(F32)
    substitute(
        coef_a.at[0], esum_a.at[0], state_a.at[0], *ground(albedo_ref, column_ref, 0), first_ref
    )
    substitute(
        coef_b.at[0],
        esum_b.at[0],
        state_b.at[0],
        *ground(albedo_ref, column_ref, NB - 1),
        final_ref,
    )
    even = lax.axis_index("blk") % 2 == 0
    near_ref[...] = jnp.where(even, final_ref[...], first_ref[...])
    far_ref[...] = jnp.where(even, first_ref[...], final_ref[...])


def up(parts, keep, got, column):
    return pl.pallas_call(
        up_kernel,
        in_specs=[IN_VMEM] * 9,
        out_specs=[IN_VMEM] * 5,
        out_shape=[shape((ROWS, CB))] * 4 + [shape((2, NB, CB))],
        compiler_params=params(2),
        cost_estimate=pl.CostEstimate(flops=4000000, transcendentals=0, bytes_accessed=4000000),
        name="up",
    )(*parts[0], *parts[1], keep, got, column)


def correct(block, before, own, after, neighbour_ref, side_ref, out_ref):
    lanes = slice(block * CB, (block + 1) * CB)
    at_lane, firsts, lasts, weights = [], [], [], []
    for k in range(3):
        at = jnp.broadcast_to(neighbour_ref[k : k + 1, lanes], (8, CB))
        place = ((at >> 7) - block + 1) & (NB - 1)
        at_lane.append(at & (CB - 1))
        firsts.append(place == 0)
        lasts.append(place == 2)
        weights.append(jnp.broadcast_to(side_ref[k : k + 1, lanes], (8, CB)))
    for row in range(0, ROWS, 8):
        rows = [part(row) for part in (before, own, after)]
        total = rows[1]
        for k in range(3):
            low, mid, high = [
                jnp.take_along_axis(x, at_lane[k], axis=1, mode="promise_in_bounds")
                for x in rows
            ]
            beside = jnp.where(firsts[k], low, jnp.where(lasts[k], high, mid))
            total = total + weights[k] * (beside - rows[1])
        for l in range(row // 2, min(row // 2 + 4, LEV + 1)):
            out_ref[l, :, lanes] = total[2 * l - row : 2 * l - row + 2]


def rows_of(ref):
    return lambda row: ref[row : row + 8, :]


def inner_kernel(
    gas_ref,
    wide_ref,
    column_ref,
    solar_ref,
    albedo_ref,
    first_ref,
    final_ref,
    coef_b,
    esum_b,
    state_b,
    coef_c,
    esum_c,
    state_c,
    neighbour_ref,
    side_ref,
    out_ref,
    near_ref,
    coef_ref,
    esum_ref,
    state_ref,
    flux_ref,
):
    kept = {1: (coef_b.at[1], esum_b.at[1], state_b.at[1])}
    for i, n in enumerate(WINDOWS[2]):
        kept[n] = coef_c.at[i], esum_c.at[i], state_c.at[i]
    for i, n in enumerate(LATE):
        kept[n] = coef_ref.at[i], esum_ref.at[i], state_ref.at[i]
    flux = {0: first_ref, 1: near_ref.at[0], NB - 2: near_ref.at[1], NB - 1: final_ref}
    for n in range(2, NB - 2):
        flux[n] = flux_ref.at[n - 2]

    def start(n):
        eliminate(n, gas_ref, wide_ref, column_ref, solar_ref, *kept[n])

    def finish(n):
        substitute(*kept[n], *ground(albedo_ref, column_ref, n), flux[n])

    def side(n):
        before, own, after = [rows_of(flux[n + i]) for i in (-1, 0, 1)]
        correct(n, before, own, after, neighbour_ref, side_ref, out_ref)

    start(5)
    finish(1)
    finish(2)
    side(1)
    start(6)
    finish(3)
    finish(4)
    side(2)
    side(3)
    finish(5)
    finish(6)
    side(4)
    side(5)
    side(6)


def inner(gas, wide, column, solar, albedo, first, final, parts, neighbours, side_weight):
    count = len(LATE)
    return pl.pallas_call(
        inner_kernel,
        in_specs=[IN_VMEM] * 15,
        out_specs=[IN_VMEM] * 2,
        out_shape=[shape((LEV + 1, 2, COLS)), shape((2, ROWS, CB))],
        scratch_shapes=[
            pltpu.VMEM((count,) + COEF, F32),
            pltpu.VMEM((count,) + ESUM, F32),
            pltpu.VMEM((count,) + STATE, F32),
            pltpu.VMEM((NB - 4, ROWS, CB), F32),
        ],
        compiler_params=params(24),
        cost_estimate=pl.CostEstimate(
            flops=2000000000, transcendentals=0, bytes_accessed=4000000
        ),
        name="inner",
    )(
        gas,
        wide,
        column,
        solar,
        albedo,
        first,
        final,
        *parts[1],
        *parts[2],
        neighbours,
        side_weight,
    )


def edge_side_kernel(
    near_got,
    far_got,
    first_ref,
    final_ref,
    inside_ref,
    neighbour_ref,
    side_ref,
    full_ref,
    out_hbm,
    edge_ref,
    sems,
):
    def copy(source, lanes, i):
        return pltpu.make_async_copy(
            source.at[:, :, lanes], out_hbm.at[:, :, lanes], sems.at[i]
        )

    copies = [copy(full_ref, pl.ds(CB, COLS - 2 * CB), 0)]
    copies[0].start()
    even = lax.axis_index("blk") % 2 == 0
    near, far = rows_of(near_got), rows_of(far_got)
    correct(
        0,
        lambda row: jnp.where(even, far(row), near(row)),
        rows_of(first_ref),
        rows_of(inside_ref.at[0]),
        neighbour_ref,
        side_ref,
        edge_ref,
    )
    correct(
        NB - 1,
        rows_of(inside_ref.at[1]),
        rows_of(final_ref),
        lambda row: jnp.where(even, near(row), far(row)),
        neighbour_ref,
        side_ref,
        edge_ref,
    )
    for i, block in enumerate((0, NB - 1)):
        copies.append(copy(edge_ref, pl.ds(block * CB, CB), 1 + i))
        copies[-1].start()
    for started in copies:
        started.wait()


def edge_side(near_got, far_got, first, final, inside, neighbours, side_weight, full):
    return pl.pallas_call(
        edge_side_kernel,
        in_specs=[IN_VMEM] * 8,
        out_specs=IN_HBM,
        out_shape=shape((LEV + 1, 2, COLS)),
        scratch_shapes=[
            pltpu.VMEM((LEV + 1, 2, COLS), F32),
            pltpu.SemaphoreType.DMA((3,)),
        ],
        compiler_params=params(4),
        name="edge_side",
    )(near_got, far_got, first, final, inside, neighbours, side_weight, full)


def exchange(x, bit):
    count = lax.axis_size("blk")
    return lax.ppermute(x, "blk", [(i, i ^ bit) for i in range(count)])


def local(
    gas_state,
    cos_zenith,
    daylit,
    fine_area,
    fine_albedo,
    parent_of,
    optics_weight,
    solar_weight,
    neighbours,
    side_weight,
):
    send, keep, gas, wide, column, solar, beside, weights = surface(
        parent_of,
        fine_area,
        fine_albedo,
        optics_weight,
        cos_zenith,
        daylit,
        solar_weight,
        neighbours,
        side_weight,
        gas_state,
    )
    parts = []
    for i, blocks in enumerate(WINDOWS):
        got = exchange(send, 1 << i)
        parts.append(down(blocks, gas, wide, column, solar, keep))
        if i < 2:
            send, keep = merge(keep, got, parts[-1][2])
    first, final, near, far, albedo = up(parts, keep, got, column)
    near_got = exchange(near, 1)
    count = lax.axis_size("blk")
    beyond = [(i, (i + (1 if i % 2 else -1)) % count) for i in range(count)]
    far_got = lax.ppermute(far, "blk", beyond)
    full, inside = inner(
        gas, wide, column, solar, albedo, first, final, parts, beside, weights
    )
    done = edge_side(near_got, far_got, first, final, inside, beside, weights, full)
    return done.transpose(1, 0, 2)


def solution(mesh):
    both = ("grp", "blk")
    in_specs = (
        P(None, None, both),
        P(both),
        P(both),
        P(both),
        P(None, both),
        P(both),
        P(),
        P(),
        P(None, both),
        P(None, both),
    )
    return jax.shard_map(
        local, mesh=mesh, in_specs=in_specs, out_specs=P(None, None, both), check_vma=False
    )
```

```python
import jax
import jax.numpy as jnp
from jax import lax
from jax.experimental import pallas as pl
from jax.experimental.pallas import tpu as pltpu
from jax.sharding import PartitionSpec as P

F = 16
LEV = 32
CB = 128
G = 32
KIDS = 4
NB = 8
NBLK = 8
ROWS = 72
STEP = 8
FINE_BLOCKS = NB * KIDS
COLS = NB * CB

ASYM = 0.8
TAU_SCALE = 0.08
SSA_MAX = 0.98
LOG2E = 1.4426950408889634

SLOPE = 0.5 * (1.25 + 0.75 * ASYM)
UNIT = 0.5 * SLOPE * SSA_MAX
SHIFT = 1.0 / UNIT - 1.0
BETA = 0.375 * (1.0 - ASYM) / SLOPE
RATE = -2.0 * TAU_SCALE * UNIT
SCATTER = UNIT / (0.375 * (1.0 - ASYM))

F32 = jnp.float32
BF16 = jnp.bfloat16
IN_VMEM = pl.BlockSpec(memory_space=pltpu.VMEM)
IN_HBM = pl.BlockSpec(memory_space=pltpu.HBM)
UNREAD = pl.BlockSpec(memory_space=pl.ANY)


def params(mebibytes):
    return pltpu.CompilerParams(vmem_limit_bytes=mebibytes << 20)


def shape(dims, kind=F32):
    return jax.ShapeDtypeStruct(dims, kind)


def sum_tiles(x):
    return (x[0:8] + x[8:16]) + (x[16:24] + x[24:32])


def place_albedo(parent_ref, area_ref, albedo_ref, mine):
    sub = lax.broadcasted_iota(jnp.int32, (CB, CB), 0).astype(F32).astype(BF16)
    line = lax.broadcasted_iota(jnp.int32, (8, CB), 0)
    one, zero = jnp.ones((), BF16), jnp.zeros((), BF16)
    totals = [[], [], []]
    for group in range(0, FINE_BLOCKS, 8):
        rows = slice(group, group + 8)
        area = area_ref[rows, :]
        terms = [area, area * albedo_ref[0, rows, :], area * albedo_ref[1, rows, :]]
        pieces = []
        for term in terms:
            for _ in range(3):
                piece = term.astype(BF16).astype(F32)
                pieces.append(piece)
                term = term - piece
        column = (parent_ref[rows, :] & (CB - 1)).astype(F32).astype(BF16)
        hots, values = [], []
        for j in range(8):
            hots.append(
                jnp.where(jnp.broadcast_to(column[j : j + 1, :], (CB, CB)) == sub, one, zero)
            )
            values.append(
                jnp.concatenate([jnp.where(line == j, x, 0.0) for x in pieces], axis=0).astype(
                    BF16
                )
            )
        total = lax.dot_general(
            jnp.concatenate(values, axis=1),
            jnp.concatenate(hots, axis=1),
            (((1,), (1,)), ((), ())),
            preferred_element_type=F32,
        )
        for i in range(3):
            at = 24 * i
            totals[i].append(
                total[at : at + 8] + (total[at + 8 : at + 16] + total[at + 16 : at + 24])
            )
    area = jnp.concatenate(totals[0], axis=0)
    here = area > 0.0
    safe = jnp.where(here, area, 1.0)
    owner = (parent_ref[:, 0:1] >> 7) ^ (mine * NB)
    slot = lax.broadcasted_iota(jnp.int32, (FINE_BLOCKS, NBLK * NB), 1)
    where_to = jnp.where(owner == slot, 1.0, 0.0).astype(BF16)
    placed = []
    for s in range(2):
        total = jnp.concatenate(totals[1 + s], axis=0)
        albedo = jnp.where(here, total / safe, 0.0).astype(BF16)
        placed.append(
            lax.dot_general(
                where_to, albedo, (((0,), (0,)), ((), ())), preferred_element_type=F32
            ).astype(BF16)
        )
    return placed


def spread_weights(weight_ref, wide_ref):
    row = lax.broadcasted_iota(jnp.int32, (F, F * STEP), 0)
    col = lax.broadcasted_iota(jnp.int32, (F, F * STEP), 1)
    spread = jnp.where(col // STEP == row, 1.0, 0.0).astype(BF16)
    depth = lax.broadcasted_iota(jnp.int32, (F, 2 * G), 1) < G
    scaled = weight_ref[...].astype(F32) * jnp.where(depth, LOG2E, 0.5)
    high = scaled.astype(BF16)
    low = (scaled - high.astype(F32)).astype(BF16)
    wide = jnp.concatenate(
        [
            lax.dot_general(x, spread, (((0,), (0,)), ((), ())), preferred_element_type=F32)
            for x in (high, low)
        ],
        axis=1,
    )
    level = lax.broadcasted_iota(jnp.int32, (2 * G, 2 * F * STEP), 1) % STEP
    for l in range(STEP):
        wide_ref[l * 2 * G : (l + 1) * 2 * G, :] = jnp.where(level == l, wide, 0.0).astype(BF16)


def column_constants(cosine, lit, column_ref):
    back = 0.5 * (1.0 - ASYM * cosine)
    rising = back * SCATTER
    column_ref[0] = -TAU_SCALE / cosine
    column_ref[1] = (1.0 - back) / back
    column_ref[2] = 1.0 / rising
    column_ref[3] = cosine
    column_ref[4] = lit * rising


WINDOWS = ((0,), (NB - 1, 1), (2, 3, 4, 5))
LATE = 6
GAS = (F, LEV, CB)


def gas_copies(gas_hbm, gas_ref, blocks, sems):
    return [
        pltpu.make_async_copy(
            gas_hbm.at[:, :, pl.ds(block * CB, CB)], gas_ref.at[i], sems.at[i]
        )
        for i, block in enumerate(blocks)
    ]


def surface_kernel(
    parent_hbm,
    area_hbm,
    albedo_hbm,
    weight_hbm,
    cosine_hbm,
    lit_hbm,
    solar_hbm,
    gas_hbm,
    send_ref,
    keep_ref,
    gas_ref,
    wide_ref,
    column_ref,
    solar_ref,
    parent_ref,
    area_ref,
    albedo_ref,
    weight_ref,
    cosine_ref,
    lit_ref,
    sun_ref,
    sems,
):
    pairs = (
        (parent_hbm, parent_ref),
        (area_hbm, area_ref),
        (albedo_hbm.at[:, 0, :], albedo_ref.at[0]),
        (albedo_hbm.at[:, 1, :], albedo_ref.at[1]),
        (weight_hbm, weight_ref),
        (cosine_hbm, cosine_ref),
        (lit_hbm, lit_ref),
        (solar_hbm, sun_ref),
    )
    copies = [
        pltpu.make_async_copy(source, target, sems.at[i])
        for i, (source, target) in enumerate(pairs)
    ]
    later = gas_copies(gas_hbm, gas_ref, WINDOWS[0], sems.at[pl.ds(8, 1)])
    for copy in copies + later:
        copy.start()
    for copy in copies:
        copy.wait()
    mine = lax.axis_index("blk")
    placed = place_albedo(parent_ref, area_ref, albedo_ref, mine)
    for s in range(2):
        for i in range(NBLK // 2):
            keep_ref[i, s] = placed[s][2 * i * NB : (2 * i + 1) * NB]
            send_ref[i, s] = placed[s][(2 * i + 1) * NB : (2 * i + 2) * NB]
    spread_weights(weight_ref, wide_ref)
    column_constants(cosine_ref[...].astype(F32), lit_ref[...].astype(F32), column_ref)
    row = lax.broadcasted_iota(jnp.int32, (G, G), 0)
    col = lax.broadcasted_iota(jnp.int32, (G, G), 1)
    sun = jnp.sum(jnp.where(row == col, sun_ref[...], 0.0), axis=1, keepdims=True)
    solar_ref[...] = jnp.broadcast_to(sun, (G, CB))
    for copy in later:
        copy.wait()


def surface(
    parent_of,
    fine_area,
    fine_albedo,
    optics_weight,
    cos_zenith,
    daylit,
    solar_weight,
    gas_state,
):
    return pl.pallas_call(
        surface_kernel,
        in_specs=[IN_HBM] * 8,
        out_specs=[IN_VMEM] * 6,
        out_shape=[
            shape((NBLK // 2, 2, NB, CB), BF16),
            shape((NBLK // 2, 2, NB, CB), BF16),
            shape((len(WINDOWS[0]),) + GAS, BF16),
            shape((2 * G * STEP, 2 * F * STEP), BF16),
            shape((5, NB, CB)),
            shape((G, CB)),
        ],
        scratch_shapes=[
            pltpu.VMEM((FINE_BLOCKS, CB), jnp.int32),
            pltpu.VMEM((FINE_BLOCKS, CB), F32),
            pltpu.VMEM((2, FINE_BLOCKS, CB), F32),
            pltpu.VMEM((F, 2 * G), BF16),
            pltpu.VMEM((NB, CB), BF16),
            pltpu.VMEM((NB, CB), jnp.int32),
            pltpu.VMEM((1, G), F32),
            pltpu.SemaphoreType.DMA((9,)),
        ],
        compiler_params=params(4),
        name="surface",
    )(
        *[
            pltpu.with_memory_space_constraint(x, pltpu.HBM)
            for x in (
                parent_of.reshape(FINE_BLOCKS, CB),
                fine_area.reshape(FINE_BLOCKS, CB),
                fine_albedo.reshape(2, FINE_BLOCKS, CB).transpose(1, 0, 2),
                optics_weight.T,
                cos_zenith.reshape(NB, CB),
                daylit.reshape(NB, CB),
                solar_weight.reshape(1, G),
                gas_state,
            )
        ]
    )


def merge_kernel(keep_ref, got_ref, after_ref, send_ref, next_ref):
    del after_ref
    for i in range(keep_ref.shape[0]):
        total = (keep_ref[i].astype(F32) + got_ref[i].astype(F32)).astype(BF16)
        target = send_ref if i % 2 else next_ref
        target[i // 2] = total


def merge(keep, got, after):
    half = shape((keep.shape[0] // 2,) + keep.shape[1:], BF16)
    return pl.pallas_call(
        merge_kernel,
        in_specs=[IN_VMEM, IN_VMEM, UNREAD],
        out_specs=[IN_VMEM] * 2,
        out_shape=[half, half],
        compiler_params=params(2),
        name="merge",
    )(keep, got, after)


def layer_terms(depth_mix, albedo_mix, slant_rate):
    soft = jnp.maximum(depth_mix, jnp.log2(1.0 + jnp.exp2(jnp.minimum(depth_mix, 60.0))))
    e_dir = jnp.exp2(soft * slant_rate)
    bend = jnp.tanh(albedo_mix)
    gamma_one = SHIFT - bend
    gamma_two = BETA * bend + BETA
    product = (gamma_one - gamma_two) * (gamma_one + gamma_two)
    root = product * lax.rsqrt(product)
    damping = jnp.exp2(RATE * (root * soft))
    damped_sq = damping * damping
    lost = 1.0 - damped_sq
    even = root + root * damped_sq
    odd = gamma_one * lost
    transmit = (root + root) * damping
    return e_dir, gamma_two, even + odd, even - odd, gamma_two * lost, transmit


def mix_all(gas_ref, wide_ref):
    products = []
    for step in range(LEV // STEP):
        gas = gas_ref[:, step * STEP : (step + 1) * STEP, :].reshape(F * STEP, CB)
        products.append(
            jnp.dot(
                wide_ref[...],
                jnp.concatenate([gas, gas], axis=0),
                preferred_element_type=F32,
            )
        )
    return products


def eliminate(block, gas_ref, wide_ref, column_ref, solar_ref, coef_ref, esum_ref, state_ref):
    products = mix_all(gas_ref, wide_ref)
    slant_rate, falling, scale, cosine = [
        column_ref[i, block : block + 1, :] for i in range(4)
    ]
    direct = solar_ref[...] * cosine
    above = jnp.zeros((G, CB), F32)
    source = jnp.zeros((G, CB), F32)
    for l in range(LEV):
        at = (l % STEP) * 2 * G
        mix = products[l // STEP]
        e_dir, gamma_two, divisor, mirrored, reflect, transmit = layer_terms(
            mix[at : at + G], mix[at + G : at + 2 * G], slant_rate
        )
        esum_ref[l] = sum_tiles(direct) * scale + sum_tiles(source)
        below = direct * e_dir
        scattered = gamma_two * (direct - below)
        inverse = pl.reciprocal(divisor - above * reflect, approx=False)
        incident = (source + above * scattered) * inverse
        coef_ref[l, 0] = above
        coef_ref[l, 1] = transmit * inverse
        coef_ref[l, 2] = scattered + reflect * incident
        source = scattered * falling + transmit * incident
        above = (reflect + above * mirrored) * inverse
        direct = below
    esum_ref[LEV] = sum_tiles(direct) * scale + sum_tiles(source)
    state_ref[0] = above
    state_ref[1] = source
    state_ref[2] = direct * scale


def add_sublanes(rows):
    sub = lax.broadcasted_iota(jnp.int32, (8, CB), 0)
    four, two, one = sub < 4, (sub & 2) == 0, (sub & 1) == 0
    rows = [
        jnp.where(four, rows[r], rows[r + 4])
        + pltpu.roll(jnp.where(four, rows[r + 4], rows[r]), 4, 0)
        for r in range(4)
    ]
    rows = [
        jnp.where(
            two,
            rows[r] + pltpu.roll(rows[r], 6, 0),
            rows[r + 2] + pltpu.roll(rows[r + 2], 2, 0),
        )
        for r in range(2)
    ]
    return jnp.where(
        one, rows[0] + pltpu.roll(rows[0], 7, 0), rows[1] + pltpu.roll(rows[1], 1, 0)
    )


def substitute(coef_ref, esum_ref, state_ref, albedo_direct, albedo_diffuse, lit, flux_ref):
    above, source, direct = state_ref[0], state_ref[1], state_ref[2]
    upward = (albedo_diffuse * source + albedo_direct * direct) * pl.reciprocal(
        1.0 - albedo_diffuse * above, approx=False
    )
    none = jnp.zeros((8, CB), F32)
    pending = [esum_ref[LEV] + sum_tiles(above * upward), sum_tiles(upward)] + [none] * 6
    flux_ref[2 * LEV : 2 * LEV + 8, :] = add_sublanes(pending) * lit
    pending = []
    for l in range(LEV - 1, -1, -1):
        upward = coef_ref[l, 1] * upward + coef_ref[l, 2]
        pending = [
            esum_ref[l] + sum_tiles(coef_ref[l, 0] * upward),
            sum_tiles(upward),
        ] + pending
        if l % 4 == 0:
            flux_ref[2 * l : 2 * l + 8, :] = add_sublanes(pending) * lit
            pending = []


COEF = (LEV, 3, G, CB)
ESUM = (LEV + 1, 8, CB)
STATE = (3, G, CB)


def down_kernel(blocks, following, with_sides):
    def kernel(*refs):
        gas_ref, wide_ref, column_ref, solar_ref, _, gas_hbm = refs[:6]
        refs = refs[6:]
        pairs = ()
        if with_sides:
            pairs, refs = refs[:2], refs[2:]
        coef_ref, esum_ref, state_ref, next_ref = refs[:4]
        sems = refs[-1]
        copies = gas_copies(gas_hbm, next_ref, following, sems)
        for i, source in enumerate(pairs):
            copies.append(
                pltpu.make_async_copy(source, refs[4 + i], sems.at[len(following) + i])
            )
        for copy in copies:
            copy.start()
        for i, block in enumerate(blocks):
            eliminate(
                block,
                gas_ref.at[i],
                wide_ref,
                column_ref,
                solar_ref,
                coef_ref.at[i],
                esum_ref.at[i],
                state_ref.at[i],
            )
        for copy in copies:
            copy.wait()

    return kernel


def down(blocks, following, gas, wide, column, solar, after, gas_state, sides=()):
    count = len(blocks)
    pinned = [pltpu.with_memory_space_constraint(x, pltpu.HBM) for x in (gas_state, *sides)]
    return pl.pallas_call(
        down_kernel(blocks, following, bool(sides)),
        in_specs=[IN_VMEM] * 4 + [UNREAD] + [IN_HBM] * len(pinned),
        out_specs=[IN_VMEM] * (4 + len(sides)),
        out_shape=[shape((count,) + x) for x in (COEF, ESUM, STATE)]
        + [shape((len(following),) + GAS, BF16)]
        + [shape(x.shape, x.dtype) for x in sides],
        scratch_shapes=[pltpu.SemaphoreType.DMA((len(following) + len(sides),))],
        compiler_params=params(24),
        cost_estimate=pl.CostEstimate(
            flops=200000000 * count, transcendentals=0, bytes_accessed=4000000
        ),
        name="down",
    )(gas, wide, column, solar, after, *pinned)


def ground(albedo_ref, column_ref, block):
    row = slice(block, block + 1)
    return albedo_ref[0, row, :], albedo_ref[1, row, :], column_ref[4, row, :]


def up_kernel(
    coef_a,
    esum_a,
    state_a,
    coef_b,
    esum_b,
    state_b,
    keep_ref,
    got_ref,
    column_ref,
    first_ref,
    final_ref,
    near_ref,
    far_ref,
    albedo_ref,
):
    for s in range(2):
        albedo_ref[s] = keep_ref[0, s].astype(F32) + got_ref[0, s].astype(F32)
    substitute(
        coef_a.at[0], esum_a.at[0], state_a.at[0], *ground(albedo_ref, column_ref, 0), first_ref
    )
    substitute(
        coef_b.at[0],
        esum_b.at[0],
        state_b.at[0],
        *ground(albedo_ref, column_ref, NB - 1),
        final_ref,
    )
    even = lax.axis_index("blk") % 2 == 0
    near_ref[...] = jnp.where(even, final_ref[...], first_ref[...])
    far_ref[...] = jnp.where(even, first_ref[...], final_ref[...])


def up(parts, keep, got, column):
    return pl.pallas_call(
        up_kernel,
        in_specs=[IN_VMEM] * 9,
        out_specs=[IN_VMEM] * 5,
        out_shape=[shape((ROWS, CB))] * 4 + [shape((2, NB, CB))],
        compiler_params=params(2),
        cost_estimate=pl.CostEstimate(flops=4000000, transcendentals=0, bytes_accessed=4000000),
        name="up",
    )(*parts[0], *parts[1], keep, got, column)


def neighbour_rows(block, neighbour_ref, side_ref):
    lanes = slice(block * CB, (block + 1) * CB)
    at_lane, places, weights = [], [], []
    for k in range(3):
        at = jnp.broadcast_to(neighbour_ref[k : k + 1, lanes], (8, CB))
        places.append(((at >> 7) - block + 1) & (NB - 1))
        at_lane.append(at & (CB - 1))
        weights.append(jnp.broadcast_to(side_ref[k : k + 1, lanes], (8, CB)))
    return at_lane, places, weights


def pick(x, at_lane):
    return jnp.take_along_axis(x, at_lane, axis=1, mode="promise_in_bounds")


def correct(block, before, own, after, neighbour_ref, side_ref, put):
    at_lane, places, weights = neighbour_rows(block, neighbour_ref, side_ref)
    for k in range(3):
        for code, part in ((0, before), (2, after)):
            if part is None:
                weights[k] = jnp.where(places[k] == code, 0.0, weights[k])
    totals = {row: own(row) for row in range(0, ROWS, 8)}
    for k in range(3):
        for row in totals:
            here = own(row)
            beside = pick(here, at_lane[k])
            for code, part in ((0, before), (2, after)):
                if part is not None:
                    beside = jnp.where(places[k] == code, pick(part(row), at_lane[k]), beside)
            totals[row] = totals[row] + weights[k] * (beside - here)
    for row, total in totals.items():
        put(row, total)


def correct_rest(block, code, outer, own, partial, neighbour_ref, side_ref, put):
    at_lane, places, weights = neighbour_rows(block, neighbour_ref, side_ref)
    weights = [jnp.where(places[k] == code, weights[k], 0.0) for k in range(3)]
    totals = {row: partial(row) for row in range(0, ROWS, 8)}
    for k in range(3):
        for row in totals:
            beside = pick(outer(row), at_lane[k])
            totals[row] = totals[row] + weights[k] * (beside - own(row))
    for row, total in totals.items():
        put(row, total)


def put_levels(out_ref, block):
    lanes = slice(block * CB, (block + 1) * CB)

    def put(row, total):
        for l in range(row // 2, min(row // 2 + 4, LEV + 1)):
            out_ref[l, :, lanes] = total[2 * l - row : 2 * l - row + 2]

    return put


def rows_of(ref):
    return lambda row: ref[row : row + 8, :]


def inner_kernel(
    gas_ref,
    wide_ref,
    column_ref,
    solar_ref,
    albedo_ref,
    first_ref,
    final_ref,
    coef_b,
    esum_b,
    state_b,
    coef_c,
    esum_c,
    state_c,
    neighbour_ref,
    side_ref,
    out_ref,
    partial_ref,
    coef_ref,
    esum_ref,
    state_ref,
    flux_ref,
):
    kept = {
        1: (coef_b.at[1], esum_b.at[1], state_b.at[1]),
        LATE: (coef_ref, esum_ref, state_ref),
    }
    for i, n in enumerate(WINDOWS[2]):
        kept[n] = coef_c.at[i], esum_c.at[i], state_c.at[i]
    flux = {0: first_ref, NB - 1: final_ref}
    for n in range(1, NB - 1):
        flux[n] = flux_ref.at[n - 1]

    def finish(n):
        substitute(*kept[n], *ground(albedo_ref, column_ref, n), flux[n])

    def side(n):
        before, own, after = [
            rows_of(flux[n + i]) if n + i in flux else None for i in (-1, 0, 1)
        ]
        if n in (0, NB - 1):
            partial = partial_ref.at[n // (NB - 1)]

            def put(row, total):
                partial[row : row + 8, :] = total

        else:
            put = put_levels(out_ref, n)
        correct(n, before, own, after, neighbour_ref, side_ref, put)

    eliminate(LATE, gas_ref.at[0], wide_ref, column_ref, solar_ref, *kept[LATE])
    for n in (1, 2, 3, LATE, 5, 4):
        finish(n)
    for n in range(NB):
        side(n)


def inner(gas, wide, column, solar, albedo, first, final, parts, neighbours, side_weight):
    return pl.pallas_call(
        inner_kernel,
        in_specs=[IN_VMEM] * 15,
        out_specs=[IN_VMEM] * 2,
        out_shape=[shape((LEV + 1, 2, COLS)), shape((2, ROWS, CB))],
        scratch_shapes=[
            pltpu.VMEM(COEF, F32),
            pltpu.VMEM(ESUM, F32),
            pltpu.VMEM(STATE, F32),
            pltpu.VMEM((NB - 2, ROWS, CB), F32),
        ],
        compiler_params=params(24),
        cost_estimate=pl.CostEstimate(
            flops=2000000000, transcendentals=0, bytes_accessed=4000000
        ),
        name="inner",
    )(
        gas,
        wide,
        column,
        solar,
        albedo,
        first,
        final,
        *parts[1],
        *parts[2],
        neighbours,
        side_weight,
    )


def edge_side_kernel(
    near_got,
    far_got,
    first_ref,
    final_ref,
    partial_ref,
    neighbour_ref,
    side_ref,
    full_ref,
    out_hbm,
    edge_ref,
    sems,
):
    def copy(source, lanes, i):
        return pltpu.make_async_copy(
            source.at[:, :, lanes], out_hbm.at[:, :, lanes], sems.at[i]
        )

    copies = [copy(full_ref, pl.ds(CB, COLS - 2 * CB), 0)]
    copies[0].start()
    even = lax.axis_index("blk") % 2 == 0
    near, far = rows_of(near_got), rows_of(far_got)
    edges = (
        (0, 0, lambda row: jnp.where(even, far(row), near(row)), first_ref),
        (NB - 1, 2, lambda row: jnp.where(even, near(row), far(row)), final_ref),
    )
    for i, (block, code, outer, own) in enumerate(edges):
        correct_rest(
            block,
            code,
            outer,
            rows_of(own),
            rows_of(partial_ref.at[i]),
            neighbour_ref,
            side_ref,
            put_levels(edge_ref, block),
        )
    for i, block in enumerate((0, NB - 1)):
        copies.append(copy(edge_ref, pl.ds(block * CB, CB), 1 + i))
        copies[-1].start()
    for started in copies:
        started.wait()


def edge_side(near_got, far_got, first, final, partial, neighbours, side_weight, full):
    return pl.pallas_call(
        edge_side_kernel,
        in_specs=[IN_VMEM] * 8,
        out_specs=IN_HBM,
        out_shape=shape((LEV + 1, 2, COLS)),
        scratch_shapes=[
            pltpu.VMEM((LEV + 1, 2, COLS), F32),
            pltpu.SemaphoreType.DMA((3,)),
        ],
        compiler_params=params(4),
        name="edge_side",
    )(near_got, far_got, first, final, partial, neighbours, side_weight, full)


def exchange(x, bit):
    count = lax.axis_size("blk")
    return lax.ppermute(x, "blk", [(i, i ^ bit) for i in range(count)])


def local(
    gas_state,
    cos_zenith,
    daylit,
    fine_area,
    fine_albedo,
    parent_of,
    optics_weight,
    solar_weight,
    neighbours,
    side_weight,
):
    send, keep, gas, wide, column, solar = surface(
        parent_of,
        fine_area,
        fine_albedo,
        optics_weight,
        cos_zenith,
        daylit,
        solar_weight,
        gas_state,
    )
    parts = []
    for i, blocks in enumerate(WINDOWS):
        got = exchange(send, 1 << i)
        following = WINDOWS[i + 1] if i < 2 else (LATE,)
        sides = (neighbours, side_weight) if i == 1 else ()
        coef, esum, state, gas, *rest = down(
            blocks, following, gas, wide, column, solar, keep, gas_state, sides
        )
        parts.append((coef, esum, state))
        if i == 1:
            beside, weights = rest
        if i < 2:
            send, keep = merge(keep, got, state)
    first, final, near, far, albedo = up(parts, keep, got, column)
    near_got = exchange(near, 1)
    count = lax.axis_size("blk")
    beyond = [(i, (i + (1 if i % 2 else -1)) % count) for i in range(count)]
    far_got = lax.ppermute(far, "blk", beyond)
    full, partial = inner(
        gas, wide, column, solar, albedo, first, final, parts, beside, weights
    )
    done = edge_side(near_got, far_got, first, final, partial, beside, weights, full)
    return done.transpose(1, 0, 2)


def solution(mesh):
    both = ("grp", "blk")
    in_specs = (
        P(None, None, both),
        P(both),
        P(both),
        P(both),
        P(None, both),
        P(both),
        P(),
        P(),
        P(None, both),
        P(None, both),
    )
    return jax.shard_map(
        local, mesh=mesh, in_specs=in_specs, out_specs=P(None, None, both), check_vma=False
    )
```

```python
import jax
import jax.numpy as jnp
from jax import lax
from jax.experimental import pallas as pl
from jax.experimental.pallas import tpu as pltpu
from jax.sharding import PartitionSpec as P

F = 16
LEV = 32
CB = 128
G = 32
KIDS = 4
NB = 8
NBLK = 8
ROWS = 72
STEP = 8
FINE_BLOCKS = NB * KIDS
COLS = NB * CB

ASYM = 0.8
TAU_SCALE = 0.08
SSA_MAX = 0.98
LOG2E = 1.4426950408889634

SLOPE = 0.5 * (1.25 + 0.75 * ASYM)
UNIT = 0.5 * SLOPE * SSA_MAX
SHIFT = 1.0 / UNIT - 1.0
BETA = 0.375 * (1.0 - ASYM) / SLOPE
RATE = -2.0 * TAU_SCALE * UNIT
SCATTER = UNIT / (0.375 * (1.0 - ASYM))

F32 = jnp.float32
BF16 = jnp.bfloat16
IN_VMEM = pl.BlockSpec(memory_space=pltpu.VMEM)
IN_HBM = pl.BlockSpec(memory_space=pltpu.HBM)
UNREAD = pl.BlockSpec(memory_space=pl.ANY)


def params(mebibytes):
    return pltpu.CompilerParams(vmem_limit_bytes=mebibytes << 20)


def shape(dims, kind=F32):
    return jax.ShapeDtypeStruct(dims, kind)


def sum_tiles(x):
    return (x[0:8] + x[8:16]) + (x[16:24] + x[24:32])


def place_albedo(parent_ref, area_ref, albedo_ref, mine):
    sub = lax.broadcasted_iota(jnp.int32, (CB, CB), 0).astype(F32).astype(BF16)
    line = lax.broadcasted_iota(jnp.int32, (8, CB), 0)
    one, zero = jnp.ones((), BF16), jnp.zeros((), BF16)
    totals = [[], [], []]
    for group in range(0, FINE_BLOCKS, 8):
        rows = slice(group, group + 8)
        area = area_ref[rows, :]
        terms = [area, area * albedo_ref[0, rows, :], area * albedo_ref[1, rows, :]]
        pieces = []
        for term in terms:
            for _ in range(3):
                piece = term.astype(BF16).astype(F32)
                pieces.append(piece)
                term = term - piece
        column = (parent_ref[rows, :] & (CB - 1)).astype(F32).astype(BF16)
        hots, values = [], []
        for j in range(8):
            hots.append(
                jnp.where(jnp.broadcast_to(column[j : j + 1, :], (CB, CB)) == sub, one, zero)
            )
            values.append(
                jnp.concatenate([jnp.where(line == j, x, 0.0) for x in pieces], axis=0).astype(
                    BF16
                )
            )
        total = lax.dot_general(
            jnp.concatenate(values, axis=1),
            jnp.concatenate(hots, axis=1),
            (((1,), (1,)), ((), ())),
            preferred_element_type=F32,
        )
        for i in range(3):
            at = 24 * i
            totals[i].append(
                total[at : at + 8] + (total[at + 8 : at + 16] + total[at + 16 : at + 24])
            )
    area = jnp.concatenate(totals[0], axis=0)
    here = area > 0.0
    safe = jnp.where(here, area, 1.0)
    owner = (parent_ref[:, 0:1] >> 7) ^ (mine * NB)
    slot = lax.broadcasted_iota(jnp.int32, (FINE_BLOCKS, NBLK * NB), 1)
    where_to = jnp.where(owner == slot, 1.0, 0.0).astype(BF16)
    placed = []
    for s in range(2):
        total = jnp.concatenate(totals[1 + s], axis=0)
        albedo = jnp.where(here, total / safe, 0.0).astype(BF16)
        placed.append(
            lax.dot_general(
                where_to, albedo, (((0,), (0,)), ((), ())), preferred_element_type=F32
            ).astype(BF16)
        )
    return placed


def spread_weights(weight_ref, wide_ref):
    row = lax.broadcasted_iota(jnp.int32, (F, F * STEP), 0)
    col = lax.broadcasted_iota(jnp.int32, (F, F * STEP), 1)
    spread = jnp.where(col // STEP == row, 1.0, 0.0).astype(BF16)
    depth = lax.broadcasted_iota(jnp.int32, (F, 2 * G), 1) < G
    scaled = weight_ref[...].astype(F32) * jnp.where(depth, LOG2E, 0.5)
    high = scaled.astype(BF16)
    low = (scaled - high.astype(F32)).astype(BF16)
    wide = jnp.concatenate(
        [
            lax.dot_general(x, spread, (((0,), (0,)), ((), ())), preferred_element_type=F32)
            for x in (high, low)
        ],
        axis=1,
    )
    level = lax.broadcasted_iota(jnp.int32, (2 * G, 2 * F * STEP), 1) % STEP
    for l in range(STEP):
        wide_ref[l * 2 * G : (l + 1) * 2 * G, :] = jnp.where(level == l, wide, 0.0).astype(BF16)


def column_constants(cosine, lit, column_ref):
    back = 0.5 * (1.0 - ASYM * cosine)
    rising = back * SCATTER
    column_ref[0] = -TAU_SCALE / cosine
    column_ref[1] = (1.0 - back) / back
    column_ref[2] = 1.0 / rising
    column_ref[3] = cosine
    column_ref[4] = lit * rising


WINDOWS = ((0,), (NB - 1, 1), (2, 3, 4))
LATE = (5, 6)


def surface_kernel(
    parent_hbm,
    area_hbm,
    albedo_hbm,
    weight_hbm,
    cosine_hbm,
    lit_hbm,
    solar_hbm,
    neighbour_hbm,
    side_hbm,
    gas_hbm,
    send_ref,
    keep_ref,
    gas_ref,
    wide_ref,
    column_ref,
    solar_ref,
    neighbour_ref,
    side_ref,
    parent_ref,
    area_ref,
    albedo_ref,
    weight_ref,
    cosine_ref,
    lit_ref,
    sun_ref,
    sems,
):
    pairs = (
        (parent_hbm, parent_ref),
        (area_hbm, area_ref),
        (albedo_hbm.at[:, 0, :], albedo_ref.at[0]),
        (albedo_hbm.at[:, 1, :], albedo_ref.at[1]),
        (weight_hbm, weight_ref),
        (cosine_hbm, cosine_ref),
        (lit_hbm, lit_ref),
        (solar_hbm, sun_ref),
        (neighbour_hbm, neighbour_ref),
        (side_hbm, side_ref),
        (gas_hbm, gas_ref),
    )
    copies = [
        pltpu.make_async_copy(source, target, sems.at[i])
        for i, (source, target) in enumerate(pairs)
    ]
    for copy in copies:
        copy.start()
    for copy in copies[:8]:
        copy.wait()
    mine = lax.axis_index("blk")
    placed = place_albedo(parent_ref, area_ref, albedo_ref, mine)
    for s in range(2):
        for i in range(NBLK // 2):
            keep_ref[i, s] = placed[s][2 * i * NB : (2 * i + 1) * NB]
            send_ref[i, s] = placed[s][(2 * i + 1) * NB : (2 * i + 2) * NB]
    spread_weights(weight_ref, wide_ref)
    column_constants(cosine_ref[...].astype(F32), lit_ref[...].astype(F32), column_ref)
    row = lax.broadcasted_iota(jnp.int32, (G, G), 0)
    col = lax.broadcasted_iota(jnp.int32, (G, G), 1)
    sun = jnp.sum(jnp.where(row == col, sun_ref[...], 0.0), axis=1, keepdims=True)
    solar_ref[...] = jnp.broadcast_to(sun, (G, CB))
    for copy in copies[8:]:
        copy.wait()


def surface(
    parent_of,
    fine_area,
    fine_albedo,
    optics_weight,
    cos_zenith,
    daylit,
    solar_weight,
    neighbours,
    side_weight,
    gas_state,
):
    return pl.pallas_call(
        surface_kernel,
        in_specs=[IN_HBM] * 10,
        out_specs=[IN_VMEM] * 8,
        out_shape=[
            shape((NBLK // 2, 2, NB, CB), BF16),
            shape((NBLK // 2, 2, NB, CB), BF16),
            shape((F, LEV, COLS), BF16),
            shape((2 * G * STEP, 2 * F * STEP), BF16),
            shape((5, NB, CB)),
            shape((G, CB)),
            shape((3, COLS), jnp.int32),
            shape((3, COLS)),
        ],
        scratch_shapes=[
            pltpu.VMEM((FINE_BLOCKS, CB), jnp.int32),
            pltpu.VMEM((FINE_BLOCKS, CB), F32),
            pltpu.VMEM((2, FINE_BLOCKS, CB), F32),
            pltpu.VMEM((F, 2 * G), BF16),
            pltpu.VMEM((NB, CB), BF16),
            pltpu.VMEM((NB, CB), jnp.int32),
            pltpu.VMEM((1, G), F32),
            pltpu.SemaphoreType.DMA((11,)),
        ],
        compiler_params=params(4),
        name="surface",
    )(
        *[
            pltpu.with_memory_space_constraint(x, pltpu.HBM)
            for x in (
                parent_of.reshape(FINE_BLOCKS, CB),
                fine_area.reshape(FINE_BLOCKS, CB),
                fine_albedo.reshape(2, FINE_BLOCKS, CB).transpose(1, 0, 2),
                optics_weight.T,
                cos_zenith.reshape(NB, CB),
                daylit.reshape(NB, CB),
                solar_weight.reshape(1, G),
                neighbours,
                side_weight,
                gas_state,
            )
        ]
    )


def merge_kernel(keep_ref, got_ref, after_ref, send_ref, next_ref):
    del after_ref
    for i in range(keep_ref.shape[0]):
        total = (keep_ref[i].astype(F32) + got_ref[i].astype(F32)).astype(BF16)
        target = send_ref if i % 2 else next_ref
        target[i // 2] = total


def merge(keep, got, after):
    half = shape((keep.shape[0] // 2,) + keep.shape[1:], BF16)
    return pl.pallas_call(
        merge_kernel,
        in_specs=[IN_VMEM, IN_VMEM, UNREAD],
        out_specs=[IN_VMEM] * 2,
        out_shape=[half, half],
        compiler_params=params(2),
        name="merge",
    )(keep, got, after)


def layer_terms(depth_mix, albedo_mix, slant_rate):
    soft = jnp.maximum(depth_mix, jnp.log2(1.0 + jnp.exp2(jnp.minimum(depth_mix, 60.0))))
    e_dir = jnp.exp2(soft * slant_rate)
    bend = jnp.tanh(albedo_mix)
    gamma_one = SHIFT - bend
    gamma_two = BETA * bend + BETA
    product = (gamma_one - gamma_two) * (gamma_one + gamma_two)
    root = product * lax.rsqrt(product)
    damping = jnp.exp2(RATE * (root * soft))
    damped_sq = damping * damping
    lost = 1.0 - damped_sq
    even = root + root * damped_sq
    odd = gamma_one * lost
    transmit = (root + root) * damping
    return e_dir, gamma_two, even + odd, even - odd, gamma_two * lost, transmit


def mix_all(gas_ref, lanes, wide_ref):
    products = []
    for step in range(LEV // STEP):
        gas = gas_ref[:, step * STEP : (step + 1) * STEP, lanes].reshape(F * STEP, CB)
        products.append(
            jnp.dot(
                wide_ref[...],
                jnp.concatenate([gas, gas], axis=0),
                preferred_element_type=F32,
            )
        )
    return products


def eliminate(block, gas_ref, wide_ref, column_ref, solar_ref, coef_ref, esum_ref, state_ref):
    products = mix_all(gas_ref, slice(block * CB, (block + 1) * CB), wide_ref)
    slant_rate, falling, scale, cosine = [
        column_ref[i, block : block + 1, :] for i in range(4)
    ]
    direct = solar_ref[...] * cosine
    above = jnp.zeros((G, CB), F32)
    source = jnp.zeros((G, CB), F32)
    for l in range(LEV):
        at = (l % STEP) * 2 * G
        mix = products[l // STEP]
        e_dir, gamma_two, divisor, mirrored, reflect, transmit = layer_terms(
            mix[at : at + G], mix[at + G : at + 2 * G], slant_rate
        )
        esum_ref[l] = sum_tiles(direct) * scale + sum_tiles(source)
        below = direct * e_dir
        scattered = gamma_two * (direct - below)
        inverse = pl.reciprocal(divisor - above * reflect, approx=False)
        incident = (source + above * scattered) * inverse
        coef_ref[l, 0] = above
        coef_ref[l, 1] = transmit * inverse
        coef_ref[l, 2] = scattered + reflect * incident
        source = scattered * falling + transmit * incident
        above = (reflect + above * mirrored) * inverse
        direct = below
    esum_ref[LEV] = sum_tiles(direct) * scale + sum_tiles(source)
    state_ref[0] = above
    state_ref[1] = source
    state_ref[2] = direct * scale


def add_sublanes(rows):
    sub = lax.broadcasted_iota(jnp.int32, (8, CB), 0)
    four, two, one = sub < 4, (sub & 2) == 0, (sub & 1) == 0
    rows = [
        jnp.where(four, rows[r], rows[r + 4])
        + pltpu.roll(jnp.where(four, rows[r + 4], rows[r]), 4, 0)
        for r in range(4)
    ]
    rows = [
        jnp.where(
            two,
            rows[r] + pltpu.roll(rows[r], 6, 0),
            rows[r + 2] + pltpu.roll(rows[r + 2], 2, 0),
        )
        for r in range(2)
    ]
    return jnp.where(
        one, rows[0] + pltpu.roll(rows[0], 7, 0), rows[1] + pltpu.roll(rows[1], 1, 0)
    )


def substitute(coef_ref, esum_ref, state_ref, albedo_direct, albedo_diffuse, lit, flux_ref):
    above, source, direct = state_ref[0], state_ref[1], state_ref[2]
    upward = (albedo_diffuse * source + albedo_direct * direct) * pl.reciprocal(
        1.0 - albedo_diffuse * above, approx=False
    )
    none = jnp.zeros((8, CB), F32)
    pending = [esum_ref[LEV] + sum_tiles(above * upward), sum_tiles(upward)] + [none] * 6
    flux_ref[2 * LEV : 2 * LEV + 8, :] = add_sublanes(pending) * lit
    pending = []
    for l in range(LEV - 1, -1, -1):
        upward = coef_ref[l, 1] * upward + coef_ref[l, 2]
        pending = [
            esum_ref[l] + sum_tiles(coef_ref[l, 0] * upward),
            sum_tiles(upward),
        ] + pending
        if l % 4 == 0:
            flux_ref[2 * l : 2 * l + 8, :] = add_sublanes(pending) * lit
            pending = []


COEF = (LEV, 3, G, CB)
ESUM = (LEV + 1, 8, CB)
STATE = (3, G, CB)


def down_kernel(blocks):
    def kernel(gas_ref, wide_ref, column_ref, solar_ref, after_ref, coef_ref, esum_ref, state_ref):
        del after_ref
        for i, block in enumerate(blocks):
            eliminate(
                block,
                gas_ref,
                wide_ref,
                column_ref,
                solar_ref,
                coef_ref.at[i],
                esum_ref.at[i],
                state_ref.at[i],
            )

    return kernel


def down(blocks, gas, wide, column, solar, after):
    count = len(blocks)
    return pl.pallas_call(
        down_kernel(blocks),
        in_specs=[IN_VMEM] * 4 + [UNREAD],
        out_specs=[IN_VMEM] * 3,
        out_shape=[shape((count,) + x) for x in (COEF, ESUM, STATE)],
        compiler_params=params(24),
        cost_estimate=pl.CostEstimate(
            flops=200000000 * count, transcendentals=0, bytes_accessed=4000000
        ),
        name="down",
    )(gas, wide, column, solar, after)


def ground(albedo_ref, column_ref, block):
    row = slice(block, block + 1)
    return albedo_ref[0, row, :], albedo_ref[1, row, :], column_ref[4, row, :]


def up_kernel(
    coef_a,
    esum_a,
    state_a,
    coef_b,
    esum_b,
    state_b,
    keep_ref,
    got_ref,
    column_ref,
    first_ref,
    final_ref,
    near_ref,
    far_ref,
    albedo_ref,
):
    for s in range(2):
        albedo_ref[s] = keep_ref[0, s].astype(F32) + got_ref[0, s].astype(F32)
    substitute(
        coef_a.at[0], esum_a.at[0], state_a.at[0], *ground(albedo_ref, column_ref, 0), first_ref
    )
    substitute(
        coef_b.at[0],
        esum_b.at[0],
        state_b.at[0],
        *ground(albedo_ref, column_ref, NB - 1),
        final_ref,
    )
    even = lax.axis_index("blk") % 2 == 0
    near_ref[...] = jnp.where(even, final_ref[...], first_ref[...])
    far_ref[...] = jnp.where(even, first_ref[...], final_ref[...])


def up(parts, keep, got, column):
    return pl.pallas_call(
        up_kernel,
        in_specs=[IN_VMEM] * 9,
        out_specs=[IN_VMEM] * 5,
        out_shape=[shape((ROWS, CB))] * 4 + [shape((2, NB, CB))],
        compiler_params=params(2),
        cost_estimate=pl.CostEstimate(flops=4000000, transcendentals=0, bytes_accessed=4000000),
        name="up",
    )(*parts[0], *parts[1], keep, got, column)


def neighbour_rows(block, neighbour_ref, side_ref):
    lanes = slice(block * CB, (block + 1) * CB)
    at_lane, places, weights = [], [], []
    for k in range(3):
        at = jnp.broadcast_to(neighbour_ref[k : k + 1, lanes], (8, CB))
        places.append(((at >> 7) - block + 1) & (NB - 1))
        at_lane.append(at & (CB - 1))
        weights.append(jnp.broadcast_to(side_ref[k : k + 1, lanes], (8, CB)))
    return at_lane, places, weights


def pick(x, at_lane):
    return jnp.take_along_axis(x, at_lane, axis=1, mode="promise_in_bounds")


def correct(block, before, own, after, neighbour_ref, side_ref, put):
    at_lane, places, weights = neighbour_rows(block, neighbour_ref, side_ref)
    for k in range(3):
        for code, part in ((0, before), (2, after)):
            if part is None:
                weights[k] = jnp.where(places[k] == code, 0.0, weights[k])
    totals = {row: own(row) for row in range(0, ROWS, 8)}
    for k in range(3):
        for row in totals:
            here = own(row)
            beside = pick(here, at_lane[k])
            for code, part in ((0, before), (2, after)):
                if part is not None:
                    beside = jnp.where(places[k] == code, pick(part(row), at_lane[k]), beside)
            totals[row] = totals[row] + weights[k] * (beside - here)
    for row, total in totals.items():
        put(row, total)


def correct_rest(block, code, outer, own, partial, neighbour_ref, side_ref, put):
    at_lane, places, weights = neighbour_rows(block, neighbour_ref, side_ref)
    weights = [jnp.where(places[k] == code, weights[k], 0.0) for k in range(3)]
    totals = {row: partial(row) for row in range(0, ROWS, 8)}
    for k in range(3):
        for row in totals:
            beside = pick(outer(row), at_lane[k])
            totals[row] = totals[row] + weights[k] * (beside - own(row))
    for row, total in totals.items():
        put(row, total)


def put_levels(out_ref, block):
    lanes = slice(block * CB, (block + 1) * CB)

    def put(row, total):
        for l in range(row // 2, min(row // 2 + 4, LEV + 1)):
            out_ref[l, :, lanes] = total[2 * l - row : 2 * l - row + 2]

    return put


def rows_of(ref):
    return lambda row: ref[row : row + 8, :]


def inner_kernel(
    gas_ref,
    wide_ref,
    column_ref,
    solar_ref,
    albedo_ref,
    first_ref,
    final_ref,
    coef_b,
    esum_b,
    state_b,
    coef_c,
    esum_c,
    state_c,
    neighbour_ref,
    side_ref,
    out_ref,
    partial_ref,
    coef_ref,
    esum_ref,
    state_ref,
    flux_ref,
):
    kept = {1: (coef_b.at[1], esum_b.at[1], state_b.at[1])}
    for i, n in enumerate(WINDOWS[2]):
        kept[n] = coef_c.at[i], esum_c.at[i], state_c.at[i]
    for i, n in enumerate(LATE):
        kept[n] = coef_ref.at[i], esum_ref.at[i], state_ref.at[i]
    flux = {0: first_ref, NB - 1: final_ref}
    for n in range(1, NB - 1):
        flux[n] = flux_ref.at[n - 1]

    def finish(n):
        substitute(*kept[n], *ground(albedo_ref, column_ref, n), flux[n])

    def side(n):
        before, own, after = [
            rows_of(flux[n + i]) if n + i in flux else None for i in (-1, 0, 1)
        ]
        if n in (0, NB - 1):
            partial = partial_ref.at[n // (NB - 1)]

            def put(row, total):
                partial[row : row + 8, :] = total

        else:
            put = put_levels(out_ref, n)
        correct(n, before, own, after, neighbour_ref, side_ref, put)

    for n in LATE:
        eliminate(n, gas_ref, wide_ref, column_ref, solar_ref, *kept[n])
    for n in range(1, NB - 1):
        finish(n)
    for n in range(NB):
        side(n)


def inner(gas, wide, column, solar, albedo, first, final, parts, neighbours, side_weight):
    return pl.pallas_call(
        inner_kernel,
        in_specs=[IN_VMEM] * 15,
        out_specs=[IN_VMEM] * 2,
        out_shape=[shape((LEV + 1, 2, COLS)), shape((2, ROWS, CB))],
        scratch_shapes=[
            pltpu.VMEM((len(LATE),) + COEF, F32),
            pltpu.VMEM((len(LATE),) + ESUM, F32),
            pltpu.VMEM((len(LATE),) + STATE, F32),
            pltpu.VMEM((NB - 2, ROWS, CB), F32),
        ],
        compiler_params=params(24),
        cost_estimate=pl.CostEstimate(
            flops=2000000000, transcendentals=0, bytes_accessed=4000000
        ),
        name="inner",
    )(
        gas,
        wide,
        column,
        solar,
        albedo,
        first,
        final,
        *parts[1],
        *parts[2],
        neighbours,
        side_weight,
    )


def edge_side_kernel(
    near_got,
    far_got,
    first_ref,
    final_ref,
    partial_ref,
    neighbour_ref,
    side_ref,
    full_ref,
    out_hbm,
    edge_ref,
    sems,
):
    def copy(source, lanes, i):
        return pltpu.make_async_copy(
            source.at[:, :, lanes], out_hbm.at[:, :, lanes], sems.at[i]
        )

    copies = [copy(full_ref, pl.ds(CB, COLS - 2 * CB), 0)]
    copies[0].start()
    even = lax.axis_index("blk") % 2 == 0
    near, far = rows_of(near_got), rows_of(far_got)
    edges = (
        (0, 0, lambda row: jnp.where(even, far(row), near(row)), first_ref),
        (NB - 1, 2, lambda row: jnp.where(even, near(row), far(row)), final_ref),
    )
    for i, (block, code, outer, own) in enumerate(edges):
        correct_rest(
            block,
            code,
            outer,
            rows_of(own),
            rows_of(partial_ref.at[i]),
            neighbour_ref,
            side_ref,
            put_levels(edge_ref, block),
        )
    for i, block in enumerate((0, NB - 1)):
        copies.append(copy(edge_ref, pl.ds(block * CB, CB), 1 + i))
        copies[-1].start()
    for started in copies:
        started.wait()


def edge_side(near_got, far_got, first, final, partial, neighbours, side_weight, full):
    return pl.pallas_call(
        edge_side_kernel,
        in_specs=[IN_VMEM] * 8,
        out_specs=IN_HBM,
        out_shape=shape((LEV + 1, 2, COLS)),
        scratch_shapes=[
            pltpu.VMEM((LEV + 1, 2, COLS), F32),
            pltpu.SemaphoreType.DMA((3,)),
        ],
        compiler_params=params(4),
        name="edge_side",
    )(near_got, far_got, first, final, partial, neighbours, side_weight, full)


def exchange(x, bit):
    count = lax.axis_size("blk")
    return lax.ppermute(x, "blk", [(i, i ^ bit) for i in range(count)])


def local(
    gas_state,
    cos_zenith,
    daylit,
    fine_area,
    fine_albedo,
    parent_of,
    optics_weight,
    solar_weight,
    neighbours,
    side_weight,
):
    send, keep, gas, wide, column, solar, beside, weights = surface(
        parent_of,
        fine_area,
        fine_albedo,
        optics_weight,
        cos_zenith,
        daylit,
        solar_weight,
        neighbours,
        side_weight,
        gas_state,
    )
    parts = []
    for i, blocks in enumerate(WINDOWS):
        got = exchange(send, 1 << i)
        parts.append(down(blocks, gas, wide, column, solar, keep))
        if i < 2:
            send, keep = merge(keep, got, parts[-1][2])
    first, final, near, far, albedo = up(parts, keep, got, column)
    near_got = exchange(near, 1)
    count = lax.axis_size("blk")
    beyond = [(i, i + (1 if i % 2 else -1)) for i in range(1, count - 1)]
    beyond += [(i, i) for i in (0, count - 1)]
    far_got = lax.ppermute(far, "blk", beyond)
    full, partial = inner(
        gas, wide, column, solar, albedo, first, final, parts, beside, weights
    )
    done = edge_side(near_got, far_got, first, final, partial, beside, weights, full)
    return done.transpose(1, 0, 2)


def solution(mesh):
    both = ("grp", "blk")
    in_specs = (
        P(None, None, both),
        P(both),
        P(both),
        P(both),
        P(None, both),
        P(both),
        P(),
        P(),
        P(None, both),
        P(None, both),
    )
    return jax.shard_map(
        local, mesh=mesh, in_specs=in_specs, out_specs=P(None, None, both), check_vma=False
    )
```

```python
import jax
import jax.numpy as jnp
from jax import lax
from jax.experimental import pallas as pl
from jax.experimental.pallas import tpu as pltpu
from jax.sharding import PartitionSpec as P

F = 16
LEV = 32
CB = 128
G = 32
KIDS = 4
NB = 8
NBLK = 8
ROWS = 72
STEP = 8
FINE_BLOCKS = NB * KIDS
COLS = NB * CB

ASYM = 0.8
TAU_SCALE = 0.08
SSA_MAX = 0.98
LOG2E = 1.4426950408889634

SLOPE = 0.5 * (1.25 + 0.75 * ASYM)
UNIT = 0.5 * SLOPE * SSA_MAX
SHIFT = 1.0 / UNIT - 1.0
BETA = 0.375 * (1.0 - ASYM) / SLOPE
RATE = -2.0 * TAU_SCALE * UNIT
SCATTER = UNIT / (0.375 * (1.0 - ASYM))

F32 = jnp.float32
BF16 = jnp.bfloat16
IN_VMEM = pl.BlockSpec(memory_space=pltpu.VMEM)
IN_HBM = pl.BlockSpec(memory_space=pltpu.HBM)
UNREAD = pl.BlockSpec(memory_space=pl.ANY)


def params(mebibytes):
    return pltpu.CompilerParams(vmem_limit_bytes=mebibytes << 20)


def shape(dims, kind=F32):
    return jax.ShapeDtypeStruct(dims, kind)


def sum_tiles(x):
    return (x[0:8] + x[8:16]) + (x[16:24] + x[24:32])


def place_albedo(parent_ref, area_ref, albedo_ref, mine):
    sub = lax.broadcasted_iota(jnp.int32, (CB, CB), 0).astype(F32).astype(BF16)
    line = lax.broadcasted_iota(jnp.int32, (8, CB), 0)
    one, zero = jnp.ones((), BF16), jnp.zeros((), BF16)
    totals = [[], [], []]
    for group in range(0, FINE_BLOCKS, 8):
        rows = slice(group, group + 8)
        area = area_ref[rows, :]
        terms = [area, area * albedo_ref[0, rows, :], area * albedo_ref[1, rows, :]]
        pieces = []
        for term in terms:
            for _ in range(3):
                piece = term.astype(BF16).astype(F32)
                pieces.append(piece)
                term = term - piece
        column = (parent_ref[rows, :] & (CB - 1)).astype(F32).astype(BF16)
        hots, values = [], []
        for j in range(8):
            hots.append(
                jnp.where(jnp.broadcast_to(column[j : j + 1, :], (CB, CB)) == sub, one, zero)
            )
            values.append(
                jnp.concatenate([jnp.where(line == j, x, 0.0) for x in pieces], axis=0).astype(
                    BF16
                )
            )
        total = lax.dot_general(
            jnp.concatenate(values, axis=1),
            jnp.concatenate(hots, axis=1),
            (((1,), (1,)), ((), ())),
            preferred_element_type=F32,
        )
        for i in range(3):
            at = 24 * i
            totals[i].append(
                total[at : at + 8] + (total[at + 8 : at + 16] + total[at + 16 : at + 24])
            )
    area = jnp.concatenate(totals[0], axis=0)
    here = area > 0.0
    safe = jnp.where(here, area, 1.0)
    owner = (parent_ref[:, 0:1] >> 7) ^ (mine * NB)
    slot = lax.broadcasted_iota(jnp.int32, (FINE_BLOCKS, NBLK * NB), 1)
    where_to = jnp.where(owner == slot, 1.0, 0.0).astype(BF16)
    placed = []
    for s in range(2):
        total = jnp.concatenate(totals[1 + s], axis=0)
        albedo = jnp.where(here, total / safe, 0.0).astype(BF16)
        placed.append(
            lax.dot_general(
                where_to, albedo, (((0,), (0,)), ((), ())), preferred_element_type=F32
            ).astype(BF16)
        )
    return placed


def spread_weights(weight_ref, wide_ref):
    row = lax.broadcasted_iota(jnp.int32, (F, F * STEP), 0)
    col = lax.broadcasted_iota(jnp.int32, (F, F * STEP), 1)
    spread = jnp.where(col // STEP == row, 1.0, 0.0).astype(BF16)
    depth = lax.broadcasted_iota(jnp.int32, (F, 2 * G), 1) < G
    scaled = weight_ref[...].astype(F32) * jnp.where(depth, LOG2E, 0.5)
    high = scaled.astype(BF16)
    low = (scaled - high.astype(F32)).astype(BF16)
    wide = jnp.concatenate(
        [
            lax.dot_general(x, spread, (((0,), (0,)), ((), ())), preferred_element_type=F32)
            for x in (high, low)
        ],
        axis=1,
    )
    level = lax.broadcasted_iota(jnp.int32, (2 * G, 2 * F * STEP), 1) % STEP
    for l in range(STEP):
        wide_ref[l * 2 * G : (l + 1) * 2 * G, :] = jnp.where(level == l, wide, 0.0).astype(BF16)


def column_constants(cosine, lit, column_ref):
    back = 0.5 * (1.0 - ASYM * cosine)
    rising = back * SCATTER
    column_ref[0] = -TAU_SCALE / cosine
    column_ref[1] = (1.0 - back) / back
    column_ref[2] = 1.0 / rising
    column_ref[3] = cosine
    column_ref[4] = lit * rising


WINDOWS = ((0,), (NB - 1, 1), (2, 3, 4))
LATE = (5, 6)


def surface_kernel(
    parent_hbm,
    area_hbm,
    albedo_hbm,
    weight_hbm,
    cosine_hbm,
    lit_hbm,
    solar_hbm,
    neighbour_hbm,
    side_hbm,
    gas_hbm,
    send_ref,
    keep_ref,
    gas_ref,
    wide_ref,
    column_ref,
    solar_ref,
    neighbour_ref,
    side_ref,
    parent_ref,
    area_ref,
    albedo_ref,
    weight_ref,
    cosine_ref,
    lit_ref,
    sun_ref,
    sems,
):
    pairs = (
        (parent_hbm, parent_ref),
        (area_hbm, area_ref),
        (albedo_hbm.at[:, 0, :], albedo_ref.at[0]),
        (albedo_hbm.at[:, 1, :], albedo_ref.at[1]),
        (weight_hbm, weight_ref),
        (cosine_hbm, cosine_ref),
        (lit_hbm, lit_ref),
        (solar_hbm, sun_ref),
        (neighbour_hbm, neighbour_ref),
        (side_hbm, side_ref),
        (gas_hbm, gas_ref),
    )
    copies = [
        pltpu.make_async_copy(source, target, sems.at[i])
        for i, (source, target) in enumerate(pairs)
    ]
    for copy in copies:
        copy.start()
    for copy in copies[:8]:
        copy.wait()
    mine = lax.axis_index("blk")
    placed = place_albedo(parent_ref, area_ref, albedo_ref, mine)
    for s in range(2):
        for i in range(NBLK // 2):
            keep_ref[i, s] = placed[s][2 * i * NB : (2 * i + 1) * NB]
            send_ref[i, s] = placed[s][(2 * i + 1) * NB : (2 * i + 2) * NB]
    spread_weights(weight_ref, wide_ref)
    column_constants(cosine_ref[...].astype(F32), lit_ref[...].astype(F32), column_ref)
    row = lax.broadcasted_iota(jnp.int32, (G, G), 0)
    col = lax.broadcasted_iota(jnp.int32, (G, G), 1)
    sun = jnp.sum(jnp.where(row == col, sun_ref[...], 0.0), axis=1, keepdims=True)
    solar_ref[...] = jnp.broadcast_to(sun, (G, CB))
    for copy in copies[8:]:
        copy.wait()


def surface(
    parent_of,
    fine_area,
    fine_albedo,
    optics_weight,
    cos_zenith,
    daylit,
    solar_weight,
    neighbours,
    side_weight,
    gas_state,
):
    return pl.pallas_call(
        surface_kernel,
        in_specs=[IN_HBM] * 10,
        out_specs=[IN_VMEM] * 8,
        out_shape=[
            shape((NBLK // 2, 2, NB, CB), BF16),
            shape((NBLK // 2, 2, NB, CB), BF16),
            shape((F, LEV, COLS), BF16),
            shape((2 * G * STEP, 2 * F * STEP), BF16),
            shape((5, NB, CB)),
            shape((G, CB)),
            shape((3, COLS), jnp.int32),
            shape((3, COLS)),
        ],
        scratch_shapes=[
            pltpu.VMEM((FINE_BLOCKS, CB), jnp.int32),
            pltpu.VMEM((FINE_BLOCKS, CB), F32),
            pltpu.VMEM((2, FINE_BLOCKS, CB), F32),
            pltpu.VMEM((F, 2 * G), BF16),
            pltpu.VMEM((NB, CB), BF16),
            pltpu.VMEM((NB, CB), jnp.int32),
            pltpu.VMEM((1, G), F32),
            pltpu.SemaphoreType.DMA((11,)),
        ],
        compiler_params=params(4),
        name="surface",
    )(
        *[
            pltpu.with_memory_space_constraint(x, pltpu.HBM)
            for x in (
                parent_of.reshape(FINE_BLOCKS, CB),
                fine_area.reshape(FINE_BLOCKS, CB),
                fine_albedo.reshape(2, FINE_BLOCKS, CB).transpose(1, 0, 2),
                optics_weight.T,
                cos_zenith.reshape(NB, CB),
                daylit.reshape(NB, CB),
                solar_weight.reshape(1, G),
                neighbours,
                side_weight,
                gas_state,
            )
        ]
    )


def merge_kernel(keep_ref, got_ref, after_ref, send_ref, next_ref):
    del after_ref
    for i in range(keep_ref.shape[0]):
        total = (keep_ref[i].astype(F32) + got_ref[i].astype(F32)).astype(BF16)
        target = send_ref if i % 2 else next_ref
        target[i // 2] = total


def merge(keep, got, after):
    half = shape((keep.shape[0] // 2,) + keep.shape[1:], BF16)
    return pl.pallas_call(
        merge_kernel,
        in_specs=[IN_VMEM, IN_VMEM, UNREAD],
        out_specs=[IN_VMEM] * 2,
        out_shape=[half, half],
        compiler_params=params(2),
        name="merge",
    )(keep, got, after)


def layer_terms(depth_mix, albedo_mix, slant_rate):
    soft = jnp.maximum(depth_mix, jnp.log2(1.0 + jnp.exp2(jnp.minimum(depth_mix, 60.0))))
    e_dir = jnp.exp2(soft * slant_rate)
    bend = jnp.tanh(albedo_mix)
    gamma_one = SHIFT - bend
    gamma_two = BETA * bend + BETA
    product = (gamma_one - gamma_two) * (gamma_one + gamma_two)
    root = product * lax.rsqrt(product)
    damping = jnp.exp2(RATE * (root * soft))
    damped_sq = damping * damping
    lost = 1.0 - damped_sq
    even = root + root * damped_sq
    odd = gamma_one * lost
    transmit = (root + root) * damping
    return e_dir, gamma_two, even + odd, even - odd, gamma_two * lost, transmit


def mix_all(gas_ref, lanes, wide_ref):
    products = []
    for step in range(LEV // STEP):
        gas = gas_ref[:, step * STEP : (step + 1) * STEP, lanes].reshape(F * STEP, CB)
        products.append(
            jnp.dot(
                wide_ref[...],
                jnp.concatenate([gas, gas], axis=0),
                preferred_element_type=F32,
            )
        )
    return products


def eliminate(block, gas_ref, wide_ref, column_ref, solar_ref, coef_ref, esum_ref, state_ref):
    products = mix_all(gas_ref, slice(block * CB, (block + 1) * CB), wide_ref)
    slant_rate, falling, scale, cosine = [
        column_ref[i, block : block + 1, :] for i in range(4)
    ]
    direct = solar_ref[...] * cosine
    above = jnp.zeros((G, CB), F32)
    source = jnp.zeros((G, CB), F32)
    for l in range(LEV):
        at = (l % STEP) * 2 * G
        mix = products[l // STEP]
        e_dir, gamma_two, divisor, mirrored, reflect, transmit = layer_terms(
            mix[at : at + G], mix[at + G : at + 2 * G], slant_rate
        )
        esum_ref[l] = sum_tiles(direct) * scale + sum_tiles(source)
        below = direct * e_dir
        scattered = gamma_two * (direct - below)
        inverse = pl.reciprocal(divisor - above * reflect, approx=False)
        incident = (source + above * scattered) * inverse
        coef_ref[l, 0] = above
        coef_ref[l, 1] = transmit * inverse
        coef_ref[l, 2] = scattered + reflect * incident
        source = scattered * falling + transmit * incident
        above = (reflect + above * mirrored) * inverse
        direct = below
    esum_ref[LEV] = sum_tiles(direct) * scale + sum_tiles(source)
    state_ref[0] = above
    state_ref[1] = source
    state_ref[2] = direct * scale


def add_sublanes(rows):
    sub = lax.broadcasted_iota(jnp.int32, (8, CB), 0)
    four, two, one = sub < 4, (sub & 2) == 0, (sub & 1) == 0
    rows = [
        jnp.where(four, rows[r], rows[r + 4])
        + pltpu.roll(jnp.where(four, rows[r + 4], rows[r]), 4, 0)
        for r in range(4)
    ]
    rows = [
        jnp.where(
            two,
            rows[r] + pltpu.roll(rows[r], 6, 0),
            rows[r + 2] + pltpu.roll(rows[r + 2], 2, 0),
        )
        for r in range(2)
    ]
    return jnp.where(
        one, rows[0] + pltpu.roll(rows[0], 7, 0), rows[1] + pltpu.roll(rows[1], 1, 0)
    )


def substitute(coef_ref, esum_ref, state_ref, albedo_direct, albedo_diffuse, lit, flux_ref):
    above, source, direct = state_ref[0], state_ref[1], state_ref[2]
    upward = (albedo_diffuse * source + albedo_direct * direct) * pl.reciprocal(
        1.0 - albedo_diffuse * above, approx=False
    )
    none = jnp.zeros((8, CB), F32)
    pending = [esum_ref[LEV] + sum_tiles(above * upward), sum_tiles(upward)] + [none] * 6
    flux_ref[2 * LEV : 2 * LEV + 8, :] = add_sublanes(pending) * lit
    pending = []
    for l in range(LEV - 1, -1, -1):
        upward = coef_ref[l, 1] * upward + coef_ref[l, 2]
        pending = [
            esum_ref[l] + sum_tiles(coef_ref[l, 0] * upward),
            sum_tiles(upward),
        ] + pending
        if l % 4 == 0:
            flux_ref[2 * l : 2 * l + 8, :] = add_sublanes(pending) * lit
            pending = []


COEF = (LEV, 3, G, CB)
ESUM = (LEV + 1, 8, CB)
STATE = (3, G, CB)


def down_kernel(blocks):
    def kernel(gas_ref, wide_ref, column_ref, solar_ref, after_ref, coef_ref, esum_ref, state_ref):
        del after_ref
        for i, block in enumerate(blocks):
            eliminate(
                block,
                gas_ref,
                wide_ref,
                column_ref,
                solar_ref,
                coef_ref.at[i],
                esum_ref.at[i],
                state_ref.at[i],
            )

    return kernel


def down(blocks, gas, wide, column, solar, after):
    count = len(blocks)
    return pl.pallas_call(
        down_kernel(blocks),
        in_specs=[IN_VMEM] * 4 + [UNREAD],
        out_specs=[IN_VMEM] * 3,
        out_shape=[shape((count,) + x) for x in (COEF, ESUM, STATE)],
        compiler_params=params(24),
        cost_estimate=pl.CostEstimate(
            flops=200000000 * count, transcendentals=0, bytes_accessed=4000000
        ),
        name="down",
    )(gas, wide, column, solar, after)


def ground(albedo_ref, column_ref, block):
    row = slice(block, block + 1)
    return albedo_ref[0, row, :], albedo_ref[1, row, :], column_ref[4, row, :]


def up_kernel(
    coef_a,
    esum_a,
    state_a,
    coef_b,
    esum_b,
    state_b,
    keep_ref,
    got_ref,
    column_ref,
    first_ref,
    final_ref,
    near_ref,
    far_ref,
    albedo_ref,
):
    for s in range(2):
        albedo_ref[s] = keep_ref[0, s].astype(F32) + got_ref[0, s].astype(F32)
    substitute(
        coef_a.at[0], esum_a.at[0], state_a.at[0], *ground(albedo_ref, column_ref, 0), first_ref
    )
    substitute(
        coef_b.at[0],
        esum_b.at[0],
        state_b.at[0],
        *ground(albedo_ref, column_ref, NB - 1),
        final_ref,
    )
    even = lax.axis_index("blk") % 2 == 0
    near_ref[...] = jnp.where(even, final_ref[...], first_ref[...])
    far_ref[...] = jnp.where(even, first_ref[...], final_ref[...])


def up(parts, keep, got, column):
    return pl.pallas_call(
        up_kernel,
        in_specs=[IN_VMEM] * 9,
        out_specs=[IN_VMEM] * 5,
        out_shape=[shape((ROWS, CB))] * 4 + [shape((2, NB, CB))],
        compiler_params=params(2),
        cost_estimate=pl.CostEstimate(flops=4000000, transcendentals=0, bytes_accessed=4000000),
        name="up",
    )(*parts[0], *parts[1], keep, got, column)


def neighbour_rows(block, neighbour_ref, side_ref):
    lanes = slice(block * CB, (block + 1) * CB)
    at_lane, places, weights = [], [], []
    for k in range(3):
        at = jnp.broadcast_to(neighbour_ref[k : k + 1, lanes], (8, CB))
        places.append(((at >> 7) - block + 1) & (NB - 1))
        at_lane.append(at & (CB - 1))
        weights.append(jnp.broadcast_to(side_ref[k : k + 1, lanes], (8, CB)))
    return at_lane, places, weights


def pick(x, at_lane):
    return jnp.take_along_axis(x, at_lane, axis=1, mode="promise_in_bounds")


def correct(block, before, own, after, neighbour_ref, side_ref, put):
    at_lane, places, weights = neighbour_rows(block, neighbour_ref, side_ref)
    for k in range(3):
        for code, part in ((0, before), (2, after)):
            if part is None:
                weights[k] = jnp.where(places[k] == code, 0.0, weights[k])
    totals = {row: own(row) for row in range(0, ROWS, 8)}
    for k in range(3):
        for row in totals:
            here = own(row)
            beside = pick(here, at_lane[k])
            for code, part in ((0, before), (2, after)):
                if part is not None:
                    beside = jnp.where(places[k] == code, pick(part(row), at_lane[k]), beside)
            totals[row] = totals[row] + weights[k] * (beside - here)
    for row, total in totals.items():
        put(row, total)


def correct_rest(block, code, outer, own, partial, neighbour_ref, side_ref, put):
    at_lane, places, weights = neighbour_rows(block, neighbour_ref, side_ref)
    weights = [jnp.where(places[k] == code, weights[k], 0.0) for k in range(3)]
    totals = {row: partial(row) for row in range(0, ROWS, 8)}
    for k in range(3):
        for row in totals:
            beside = pick(outer(row), at_lane[k])
            totals[row] = totals[row] + weights[k] * (beside - own(row))
    for row, total in totals.items():
        put(row, total)


def put_levels(out_ref, block):
    lanes = slice(block * CB, (block + 1) * CB)

    def put(row, total):
        for l in range(row // 2, min(row // 2 + 4, LEV + 1)):
            out_ref[l, :, lanes] = total[2 * l - row : 2 * l - row + 2]

    return put


def rows_of(ref):
    return lambda row: ref[row : row + 8, :]


def inner_kernel(
    gas_ref,
    wide_ref,
    column_ref,
    solar_ref,
    albedo_ref,
    first_ref,
    final_ref,
    coef_b,
    esum_b,
    state_b,
    coef_c,
    esum_c,
    state_c,
    neighbour_ref,
    side_ref,
    out_ref,
    partial_ref,
    coef_ref,
    esum_ref,
    state_ref,
    flux_ref,
):
    kept = {1: (coef_b.at[1], esum_b.at[1], state_b.at[1])}
    for i, n in enumerate(WINDOWS[2]):
        kept[n] = coef_c.at[i], esum_c.at[i], state_c.at[i]
    for i, n in enumerate(LATE):
        kept[n] = coef_ref.at[i], esum_ref.at[i], state_ref.at[i]
    flux = {0: first_ref, NB - 1: final_ref}
    for n in range(1, NB - 1):
        flux[n] = flux_ref.at[n - 1]

    def finish(n):
        substitute(*kept[n], *ground(albedo_ref, column_ref, n), flux[n])

    def side(n):
        before, own, after = [
            rows_of(flux[n + i]) if n + i in flux else None for i in (-1, 0, 1)
        ]
        if n in (0, NB - 1):
            partial = partial_ref.at[n // (NB - 1)]

            def put(row, total):
                partial[row : row + 8, :] = total

        else:
            put = put_levels(out_ref, n)
        correct(n, before, own, after, neighbour_ref, side_ref, put)

    for n in LATE:
        eliminate(n, gas_ref, wide_ref, column_ref, solar_ref, *kept[n])
    for n in range(1, NB - 1):
        finish(n)
    for n in range(NB):
        side(n)


def inner(gas, wide, column, solar, albedo, first, final, parts, neighbours, side_weight):
    return pl.pallas_call(
        inner_kernel,
        in_specs=[IN_VMEM] * 15,
        out_specs=[IN_VMEM] * 2,
        out_shape=[shape((LEV + 1, 2, COLS)), shape((2, ROWS, CB))],
        scratch_shapes=[
            pltpu.VMEM((len(LATE),) + COEF, F32),
            pltpu.VMEM((len(LATE),) + ESUM, F32),
            pltpu.VMEM((len(LATE),) + STATE, F32),
            pltpu.VMEM((NB - 2, ROWS, CB), F32),
        ],
        compiler_params=params(24),
        cost_estimate=pl.CostEstimate(
            flops=2000000000, transcendentals=0, bytes_accessed=4000000
        ),
        name="inner",
    )(
        gas,
        wide,
        column,
        solar,
        albedo,
        first,
        final,
        *parts[1],
        *parts[2],
        neighbours,
        side_weight,
    )


def edge_side_kernel(
    near_got,
    far_got,
    first_ref,
    final_ref,
    partial_ref,
    neighbour_ref,
    side_ref,
    full_ref,
    out_hbm,
    edge_ref,
    sems,
):
    def copy(source, lanes, i):
        return pltpu.make_async_copy(
            source.at[:, :, lanes], out_hbm.at[:, :, lanes], sems.at[i]
        )

    copies = [copy(full_ref, pl.ds(CB, COLS - 2 * CB), 0)]
    copies[0].start()
    even = lax.axis_index("blk") % 2 == 0
    near, far = rows_of(near_got), rows_of(far_got)
    edges = (
        (0, 0, lambda row: jnp.where(even, far(row), near(row)), first_ref),
        (NB - 1, 2, lambda row: jnp.where(even, near(row), far(row)), final_ref),
    )
    for i, (block, code, outer, own) in enumerate(edges):
        correct_rest(
            block,
            code,
            outer,
            rows_of(own),
            rows_of(partial_ref.at[i]),
            neighbour_ref,
            side_ref,
            put_levels(edge_ref, block),
        )
    for i, block in enumerate((0, NB - 1)):
        copies.append(copy(edge_ref, pl.ds(block * CB, CB), 1 + i))
        copies[-1].start()
    for started in copies:
        started.wait()


def edge_side(near_got, far_got, first, final, partial, neighbours, side_weight, full):
    return pl.pallas_call(
        edge_side_kernel,
        in_specs=[IN_VMEM] * 8,
        out_specs=IN_HBM,
        out_shape=shape((LEV + 1, 2, COLS)),
        scratch_shapes=[
            pltpu.VMEM((LEV + 1, 2, COLS), F32),
            pltpu.SemaphoreType.DMA((3,)),
        ],
        compiler_params=params(4),
        name="edge_side",
    )(near_got, far_got, first, final, partial, neighbours, side_weight, full)


def exchange(x, bit):
    count = lax.axis_size("blk")
    return lax.ppermute(x, "blk", [(i, i ^ bit) for i in range(count)])


def beyond(x):
    count, bands = lax.axis_size("blk"), lax.axis_size("grp")
    pairs = []
    for i in range(count):
        for band in range(bands):
            if i in (0, count - 1):
                pairs.append((i * bands + band, i * bands + (band ^ 1)))
            else:
                pairs.append((i * bands + band, (i + (1 if i % 2 else -1)) * bands + band))
    return lax.ppermute(x, ("blk", "grp"), pairs)


def local(
    gas_state,
    cos_zenith,
    daylit,
    fine_area,
    fine_albedo,
    parent_of,
    optics_weight,
    solar_weight,
    neighbours,
    side_weight,
):
    send, keep, gas, wide, column, solar, beside, weights = surface(
        parent_of,
        fine_area,
        fine_albedo,
        optics_weight,
        cos_zenith,
        daylit,
        solar_weight,
        neighbours,
        side_weight,
        gas_state,
    )
    parts = []
    for i, blocks in enumerate(WINDOWS):
        got = exchange(send, 1 << i)
        parts.append(down(blocks, gas, wide, column, solar, keep))
        if i < 2:
            send, keep = merge(keep, got, parts[-1][2])
    first, final, near, far, albedo = up(parts, keep, got, column)
    near_got = exchange(near, 1)
    far_got = beyond(far)
    full, partial = inner(
        gas, wide, column, solar, albedo, first, final, parts, beside, weights
    )
    done = edge_side(near_got, far_got, first, final, partial, beside, weights, full)
    return done.transpose(1, 0, 2)


def solution(mesh):
    both = ("grp", "blk")
    in_specs = (
        P(None, None, both),
        P(both),
        P(both),
        P(both),
        P(None, both),
        P(both),
        P(),
        P(),
        P(None, both),
        P(None, both),
    )
    return jax.shard_map(
        local, mesh=mesh, in_specs=in_specs, out_specs=P(None, None, both), check_vma=False
    )
```

```python
import jax
import jax.numpy as jnp
from jax import lax
from jax.experimental import pallas as pl
from jax.experimental.pallas import tpu as pltpu
from jax.sharding import PartitionSpec as P

F = 16
LEV = 32
CB = 128
G = 32
KIDS = 4
NB = 8
NBLK = 8
ROWS = 72
STEP = 8
FINE_BLOCKS = NB * KIDS
COLS = NB * CB

ASYM = 0.8
TAU_SCALE = 0.08
SSA_MAX = 0.98
LOG2E = 1.4426950408889634

SLOPE = 0.5 * (1.25 + 0.75 * ASYM)
UNIT = 0.5 * SLOPE * SSA_MAX
SHIFT = 1.0 / UNIT - 1.0
BETA = 0.375 * (1.0 - ASYM) / SLOPE
RATE = -2.0 * TAU_SCALE * UNIT
SCATTER = UNIT / (0.375 * (1.0 - ASYM))

F32 = jnp.float32
BF16 = jnp.bfloat16
IN_VMEM = pl.BlockSpec(memory_space=pltpu.VMEM)
IN_HBM = pl.BlockSpec(memory_space=pltpu.HBM)
UNREAD = pl.BlockSpec(memory_space=pl.ANY)


def params(mebibytes):
    return pltpu.CompilerParams(vmem_limit_bytes=mebibytes << 20)


def shape(dims, kind=F32):
    return jax.ShapeDtypeStruct(dims, kind)


def sum_tiles(x):
    return (x[0:8] + x[8:16]) + (x[16:24] + x[24:32])


def place_albedo(parent_ref, area_ref, albedo_ref, mine):
    sub = lax.broadcasted_iota(jnp.int32, (CB, CB), 0).astype(F32).astype(BF16)
    line = lax.broadcasted_iota(jnp.int32, (8, CB), 0)
    one, zero = jnp.ones((), BF16), jnp.zeros((), BF16)
    totals = [[], [], []]
    for group in range(0, FINE_BLOCKS, 8):
        rows = slice(group, group + 8)
        area = area_ref[rows, :]
        terms = [area, area * albedo_ref[0, rows, :], area * albedo_ref[1, rows, :]]
        pieces = []
        for term in terms:
            for _ in range(3):
                piece = term.astype(BF16).astype(F32)
                pieces.append(piece)
                term = term - piece
        column = (parent_ref[rows, :] & (CB - 1)).astype(F32).astype(BF16)
        hots, values = [], []
        for j in range(8):
            hots.append(
                jnp.where(jnp.broadcast_to(column[j : j + 1, :], (CB, CB)) == sub, one, zero)
            )
            values.append(
                jnp.concatenate([jnp.where(line == j, x, 0.0) for x in pieces], axis=0).astype(
                    BF16
                )
            )
        total = lax.dot_general(
            jnp.concatenate(values, axis=1),
            jnp.concatenate(hots, axis=1),
            (((1,), (1,)), ((), ())),
            preferred_element_type=F32,
        )
        for i in range(3):
            at = 24 * i
            totals[i].append(
                total[at : at + 8] + (total[at + 8 : at + 16] + total[at + 16 : at + 24])
            )
    area = jnp.concatenate(totals[0], axis=0)
    here = area > 0.0
    safe = jnp.where(here, area, 1.0)
    owner = (parent_ref[:, 0:1] >> 7) ^ (mine * NB)
    slot = lax.broadcasted_iota(jnp.int32, (FINE_BLOCKS, NBLK * NB), 1)
    where_to = jnp.where(owner == slot, 1.0, 0.0).astype(BF16)
    placed = []
    for s in range(2):
        total = jnp.concatenate(totals[1 + s], axis=0)
        albedo = jnp.where(here, total / safe, 0.0).astype(BF16)
        placed.append(
            lax.dot_general(
                where_to, albedo, (((0,), (0,)), ((), ())), preferred_element_type=F32
            ).astype(BF16)
        )
    return placed


def spread_weights(weight_ref, wide_ref):
    row = lax.broadcasted_iota(jnp.int32, (F, F * STEP), 0)
    col = lax.broadcasted_iota(jnp.int32, (F, F * STEP), 1)
    spread = jnp.where(col // STEP == row, 1.0, 0.0).astype(BF16)
    depth = lax.broadcasted_iota(jnp.int32, (F, 2 * G), 1) < G
    scaled = weight_ref[...].astype(F32) * jnp.where(depth, LOG2E, 0.5)
    high = scaled.astype(BF16)
    low = (scaled - high.astype(F32)).astype(BF16)
    wide = jnp.concatenate(
        [
            lax.dot_general(x, spread, (((0,), (0,)), ((), ())), preferred_element_type=F32)
            for x in (high, low)
        ],
        axis=1,
    )
    level = lax.broadcasted_iota(jnp.int32, (2 * G, 2 * F * STEP), 1) % STEP
    for l in range(STEP):
        wide_ref[l * 2 * G : (l + 1) * 2 * G, :] = jnp.where(level == l, wide, 0.0).astype(BF16)


def column_constants(cosine, lit, column_ref):
    back = 0.5 * (1.0 - ASYM * cosine)
    rising = back * SCATTER
    column_ref[0] = -TAU_SCALE / cosine
    column_ref[1] = (1.0 - back) / back
    column_ref[2] = 1.0 / rising
    column_ref[3] = cosine
    column_ref[4] = lit * rising


WINDOWS = ((0,), (NB - 1, 1), (2, 3, 4))
LATE = (5, 6)


def surface_kernel(
    parent_hbm,
    area_hbm,
    albedo_hbm,
    weight_hbm,
    cosine_hbm,
    lit_hbm,
    solar_hbm,
    neighbour_hbm,
    side_hbm,
    gas_hbm,
    send_ref,
    keep_ref,
    gas_ref,
    wide_ref,
    column_ref,
    solar_ref,
    neighbour_ref,
    side_ref,
    parent_ref,
    area_ref,
    albedo_ref,
    weight_ref,
    cosine_ref,
    lit_ref,
    sun_ref,
    sems,
):
    pairs = (
        (parent_hbm, parent_ref),
        (area_hbm, area_ref),
        (albedo_hbm.at[:, 0, :], albedo_ref.at[0]),
        (albedo_hbm.at[:, 1, :], albedo_ref.at[1]),
        (weight_hbm, weight_ref),
        (cosine_hbm, cosine_ref),
        (lit_hbm, lit_ref),
        (solar_hbm, sun_ref),
        (neighbour_hbm, neighbour_ref),
        (side_hbm, side_ref),
        (gas_hbm, gas_ref),
    )
    copies = [
        pltpu.make_async_copy(source, target, sems.at[i])
        for i, (source, target) in enumerate(pairs)
    ]
    for copy in copies:
        copy.start()
    for copy in copies[:8]:
        copy.wait()
    mine = lax.axis_index("blk")
    placed = place_albedo(parent_ref, area_ref, albedo_ref, mine)
    for s in range(2):
        for i in range(NBLK // 2):
            keep_ref[i, s] = placed[s][2 * i * NB : (2 * i + 1) * NB]
            send_ref[i, s] = placed[s][(2 * i + 1) * NB : (2 * i + 2) * NB]
    spread_weights(weight_ref, wide_ref)
    column_constants(cosine_ref[...].astype(F32), lit_ref[...].astype(F32), column_ref)
    row = lax.broadcasted_iota(jnp.int32, (G, G), 0)
    col = lax.broadcasted_iota(jnp.int32, (G, G), 1)
    sun = jnp.sum(jnp.where(row == col, sun_ref[...], 0.0), axis=1, keepdims=True)
    solar_ref[...] = jnp.broadcast_to(sun, (G, CB))
    for copy in copies[8:]:
        copy.wait()


def surface(
    parent_of,
    fine_area,
    fine_albedo,
    optics_weight,
    cos_zenith,
    daylit,
    solar_weight,
    neighbours,
    side_weight,
    gas_state,
):
    return pl.pallas_call(
        surface_kernel,
        in_specs=[IN_HBM] * 10,
        out_specs=[IN_VMEM] * 8,
        out_shape=[
            shape((NBLK // 2, 2, NB, CB), BF16),
            shape((NBLK // 2, 2, NB, CB), BF16),
            shape((F, LEV, COLS), BF16),
            shape((2 * G * STEP, 2 * F * STEP), BF16),
            shape((5, NB, CB)),
            shape((G, CB)),
            shape((3, COLS), jnp.int32),
            shape((3, COLS)),
        ],
        scratch_shapes=[
            pltpu.VMEM((FINE_BLOCKS, CB), jnp.int32),
            pltpu.VMEM((FINE_BLOCKS, CB), F32),
            pltpu.VMEM((2, FINE_BLOCKS, CB), F32),
            pltpu.VMEM((F, 2 * G), BF16),
            pltpu.VMEM((NB, CB), BF16),
            pltpu.VMEM((NB, CB), jnp.int32),
            pltpu.VMEM((1, G), F32),
            pltpu.SemaphoreType.DMA((11,)),
        ],
        compiler_params=params(4),
        name="surface",
    )(
        *[
            pltpu.with_memory_space_constraint(x, pltpu.HBM)
            for x in (
                parent_of.reshape(FINE_BLOCKS, CB),
                fine_area.reshape(FINE_BLOCKS, CB),
                fine_albedo.reshape(2, FINE_BLOCKS, CB).transpose(1, 0, 2),
                optics_weight.T,
                cos_zenith.reshape(NB, CB),
                daylit.reshape(NB, CB),
                solar_weight.reshape(1, G),
                neighbours,
                side_weight,
                gas_state,
            )
        ]
    )


def merge_kernel(keep_ref, got_ref, after_ref, send_ref, next_ref):
    del after_ref
    for i in range(keep_ref.shape[0]):
        total = (keep_ref[i].astype(F32) + got_ref[i].astype(F32)).astype(BF16)
        target = send_ref if i % 2 else next_ref
        target[i // 2] = total


def merge(keep, got, after):
    half = shape((keep.shape[0] // 2,) + keep.shape[1:], BF16)
    return pl.pallas_call(
        merge_kernel,
        in_specs=[IN_VMEM, IN_VMEM, UNREAD],
        out_specs=[IN_VMEM] * 2,
        out_shape=[half, half],
        compiler_params=params(2),
        name="merge",
    )(keep, got, after)


def layer_terms(depth_mix, albedo_mix, slant_rate):
    soft = jnp.maximum(depth_mix, jnp.log2(1.0 + jnp.exp2(jnp.minimum(depth_mix, 60.0))))
    e_dir = jnp.exp2(soft * slant_rate)
    bend = jnp.tanh(albedo_mix)
    gamma_one = SHIFT - bend
    gamma_two = BETA * bend + BETA
    product = (gamma_one - gamma_two) * (gamma_one + gamma_two)
    root = product * lax.rsqrt(product)
    damping = jnp.exp2(RATE * (root * soft))
    damped_sq = damping * damping
    lost = 1.0 - damped_sq
    even = root + root * damped_sq
    odd = gamma_one * lost
    transmit = (root + root) * damping
    return e_dir, gamma_two, even + odd, even - odd, gamma_two * lost, transmit


def mix_all(gas_ref, lanes, wide_ref):
    products = []
    for step in range(LEV // STEP):
        gas = gas_ref[:, step * STEP : (step + 1) * STEP, lanes].reshape(F * STEP, CB)
        products.append(
            jnp.dot(
                wide_ref[...],
                jnp.concatenate([gas, gas], axis=0),
                preferred_element_type=F32,
            )
        )
    return products


def eliminate(block, gas_ref, wide_ref, column_ref, solar_ref, coef_ref, esum_ref, state_ref):
    products = mix_all(gas_ref, slice(block * CB, (block + 1) * CB), wide_ref)
    slant_rate, falling, scale, cosine = [
        column_ref[i, block : block + 1, :] for i in range(4)
    ]
    direct = solar_ref[...] * cosine
    above = jnp.zeros((G, CB), F32)
    source = jnp.zeros((G, CB), F32)
    for l in range(LEV):
        at = (l % STEP) * 2 * G
        mix = products[l // STEP]
        e_dir, gamma_two, divisor, mirrored, reflect, transmit = layer_terms(
            mix[at : at + G], mix[at + G : at + 2 * G], slant_rate
        )
        esum_ref[l] = sum_tiles(direct) * scale + sum_tiles(source)
        below = direct * e_dir
        scattered = gamma_two * (direct - below)
        inverse = pl.reciprocal(divisor - above * reflect, approx=False)
        incident = (source + above * scattered) * inverse
        coef_ref[l, 0] = above
        coef_ref[l, 1] = transmit * inverse
        coef_ref[l, 2] = scattered + reflect * incident
        source = scattered * falling + transmit * incident
        above = (reflect + above * mirrored) * inverse
        direct = below
    esum_ref[LEV] = sum_tiles(direct) * scale + sum_tiles(source)
    state_ref[0] = above
    state_ref[1] = source
    state_ref[2] = direct * scale


def add_sublanes(rows):
    sub = lax.broadcasted_iota(jnp.int32, (8, CB), 0)
    four, two, one = sub < 4, (sub & 2) == 0, (sub & 1) == 0
    rows = [
        jnp.where(four, rows[r], rows[r + 4])
        + pltpu.roll(jnp.where(four, rows[r + 4], rows[r]), 4, 0)
        for r in range(4)
    ]
    rows = [
        jnp.where(
            two,
            rows[r] + pltpu.roll(rows[r], 6, 0),
            rows[r + 2] + pltpu.roll(rows[r + 2], 2, 0),
        )
        for r in range(2)
    ]
    return jnp.where(
        one, rows[0] + pltpu.roll(rows[0], 7, 0), rows[1] + pltpu.roll(rows[1], 1, 0)
    )


def substitute(coef_ref, esum_ref, state_ref, albedo_direct, albedo_diffuse, lit, flux_ref):
    above, source, direct = state_ref[0], state_ref[1], state_ref[2]
    upward = (albedo_diffuse * source + albedo_direct * direct) * pl.reciprocal(
        1.0 - albedo_diffuse * above, approx=False
    )
    none = jnp.zeros((8, CB), F32)
    pending = [esum_ref[LEV] + sum_tiles(above * upward), sum_tiles(upward)] + [none] * 6
    flux_ref[2 * LEV : 2 * LEV + 8, :] = add_sublanes(pending) * lit
    pending = []
    for l in range(LEV - 1, -1, -1):
        upward = coef_ref[l, 1] * upward + coef_ref[l, 2]
        pending = [
            esum_ref[l] + sum_tiles(coef_ref[l, 0] * upward),
            sum_tiles(upward),
        ] + pending
        if l % 4 == 0:
            flux_ref[2 * l : 2 * l + 8, :] = add_sublanes(pending) * lit
            pending = []


COEF = (LEV, 3, G, CB)
ESUM = (LEV + 1, 8, CB)
STATE = (3, G, CB)


def down_kernel(blocks):
    def kernel(gas_ref, wide_ref, column_ref, solar_ref, after_ref, coef_ref, esum_ref, state_ref):
        del after_ref
        for i, block in enumerate(blocks):
            eliminate(
                block,
                gas_ref,
                wide_ref,
                column_ref,
                solar_ref,
                coef_ref.at[i],
                esum_ref.at[i],
                state_ref.at[i],
            )

    return kernel


def down(blocks, gas, wide, column, solar, after):
    count = len(blocks)
    return pl.pallas_call(
        down_kernel(blocks),
        in_specs=[IN_VMEM] * 4 + [UNREAD],
        out_specs=[IN_VMEM] * 3,
        out_shape=[shape((count,) + x) for x in (COEF, ESUM, STATE)],
        compiler_params=params(24),
        cost_estimate=pl.CostEstimate(
            flops=200000000 * count, transcendentals=0, bytes_accessed=4000000
        ),
        name="down",
    )(gas, wide, column, solar, after)


def ground(albedo_ref, column_ref, block):
    row = slice(block, block + 1)
    return albedo_ref[0, row, :], albedo_ref[1, row, :], column_ref[4, row, :]


def up_kernel(
    coef_a,
    esum_a,
    state_a,
    coef_b,
    esum_b,
    state_b,
    keep_ref,
    got_ref,
    column_ref,
    first_ref,
    final_ref,
    near_ref,
    far_ref,
    albedo_ref,
):
    for s in range(2):
        albedo_ref[s] = keep_ref[0, s].astype(F32) + got_ref[0, s].astype(F32)
    substitute(
        coef_a.at[0], esum_a.at[0], state_a.at[0], *ground(albedo_ref, column_ref, 0), first_ref
    )
    substitute(
        coef_b.at[0],
        esum_b.at[0],
        state_b.at[0],
        *ground(albedo_ref, column_ref, NB - 1),
        final_ref,
    )
    even = lax.axis_index("blk") % 2 == 0
    near_ref[...] = jnp.where(even, final_ref[...], first_ref[...])
    far_ref[...] = jnp.where(even, first_ref[...], final_ref[...])


def up(parts, keep, got, column):
    return pl.pallas_call(
        up_kernel,
        in_specs=[IN_VMEM] * 9,
        out_specs=[IN_VMEM] * 5,
        out_shape=[shape((ROWS, CB))] * 4 + [shape((2, NB, CB))],
        compiler_params=params(2),
        cost_estimate=pl.CostEstimate(flops=4000000, transcendentals=0, bytes_accessed=4000000),
        name="up",
    )(*parts[0], *parts[1], keep, got, column)


def neighbour_rows(block, neighbour_ref, side_ref):
    lanes = slice(block * CB, (block + 1) * CB)
    at_lane, places, weights = [], [], []
    for k in range(3):
        at = jnp.broadcast_to(neighbour_ref[k : k + 1, lanes], (8, CB))
        places.append(((at >> 7) - block + 1) & (NB - 1))
        at_lane.append(at & (CB - 1))
        weights.append(jnp.broadcast_to(side_ref[k : k + 1, lanes], (8, CB)))
    return at_lane, places, weights


def pick(x, at_lane):
    return jnp.take_along_axis(x, at_lane, axis=1, mode="promise_in_bounds")


def correct(block, before, own, after, neighbour_ref, side_ref, put):
    at_lane, places, weights = neighbour_rows(block, neighbour_ref, side_ref)
    for k in range(3):
        for code, part in ((0, before), (2, after)):
            if part is None:
                weights[k] = jnp.where(places[k] == code, 0.0, weights[k])
    totals = {row: own(row) for row in range(0, ROWS, 8)}
    for k in range(3):
        for row in totals:
            here = own(row)
            beside = pick(here, at_lane[k])
            for code, part in ((0, before), (2, after)):
                if part is not None:
                    beside = jnp.where(places[k] == code, pick(part(row), at_lane[k]), beside)
            totals[row] = totals[row] + weights[k] * (beside - here)
    for row, total in totals.items():
        put(row, total)


def correct_rest(block, code, outer, own, partial, neighbour_ref, side_ref, put):
    at_lane, places, weights = neighbour_rows(block, neighbour_ref, side_ref)
    weights = [jnp.where(places[k] == code, weights[k], 0.0) for k in range(3)]
    totals = {row: partial(row) for row in range(0, ROWS, 8)}
    for k in range(3):
        for row in totals:
            beside = pick(outer(row), at_lane[k])
            totals[row] = totals[row] + weights[k] * (beside - own(row))
    for row, total in totals.items():
        put(row, total)


def put_levels(out_ref, block):
    lanes = slice(block * CB, (block + 1) * CB)

    def put(row, total):
        for l in range(row // 2, min(row // 2 + 4, LEV + 1)):
            out_ref[l, :, lanes] = total[2 * l - row : 2 * l - row + 2]

    return put


def rows_of(ref):
    return lambda row: ref[row : row + 8, :]


def inner_kernel(
    gas_ref,
    wide_ref,
    column_ref,
    solar_ref,
    albedo_ref,
    first_ref,
    final_ref,
    coef_b,
    esum_b,
    state_b,
    coef_c,
    esum_c,
    state_c,
    neighbour_ref,
    side_ref,
    out_ref,
    partial_ref,
    coef_ref,
    esum_ref,
    state_ref,
    flux_ref,
):
    kept = {1: (coef_b.at[1], esum_b.at[1], state_b.at[1])}
    for i, n in enumerate(WINDOWS[2]):
        kept[n] = coef_c.at[i], esum_c.at[i], state_c.at[i]
    for i, n in enumerate(LATE):
        kept[n] = coef_ref.at[i], esum_ref.at[i], state_ref.at[i]
    flux = {0: first_ref, NB - 1: final_ref}
    for n in range(1, NB - 1):
        flux[n] = flux_ref.at[n - 1]

    def finish(n):
        substitute(*kept[n], *ground(albedo_ref, column_ref, n), flux[n])

    def side(n):
        before, own, after = [
            rows_of(flux[n + i]) if n + i in flux else None for i in (-1, 0, 1)
        ]
        if n in (0, NB - 1):
            partial = partial_ref.at[n // (NB - 1)]

            def put(row, total):
                partial[row : row + 8, :] = total

        else:
            put = put_levels(out_ref, n)
        correct(n, before, own, after, neighbour_ref, side_ref, put)

    for n in LATE:
        eliminate(n, gas_ref, wide_ref, column_ref, solar_ref, *kept[n])
    for n in range(1, NB - 1):
        finish(n)
    for n in range(NB):
        side(n)


def inner(gas, wide, column, solar, albedo, first, final, parts, neighbours, side_weight):
    return pl.pallas_call(
        inner_kernel,
        in_specs=[IN_VMEM] * 15,
        out_specs=[IN_VMEM] * 2,
        out_shape=[shape((LEV + 1, 2, COLS)), shape((2, ROWS, CB))],
        scratch_shapes=[
            pltpu.VMEM((len(LATE),) + COEF, F32),
            pltpu.VMEM((len(LATE),) + ESUM, F32),
            pltpu.VMEM((len(LATE),) + STATE, F32),
            pltpu.VMEM((NB - 2, ROWS, CB), F32),
        ],
        compiler_params=params(24),
        cost_estimate=pl.CostEstimate(
            flops=2000000000, transcendentals=0, bytes_accessed=4000000
        ),
        name="inner",
    )(
        gas,
        wide,
        column,
        solar,
        albedo,
        first,
        final,
        *parts[1],
        *parts[2],
        neighbours,
        side_weight,
    )


def edge_side_kernel(
    near_got,
    far_got,
    first_ref,
    final_ref,
    partial_ref,
    neighbour_ref,
    side_ref,
    full_ref,
    out_hbm,
    edge_ref,
    sems,
):
    def copy(source, lanes, i):
        return pltpu.make_async_copy(
            source.at[:, :, lanes], out_hbm.at[:, :, lanes], sems.at[i]
        )

    copies = [copy(full_ref, pl.ds(CB, COLS - 2 * CB), 0)]
    copies[0].start()
    even = lax.axis_index("blk") % 2 == 0
    near, far = rows_of(near_got), rows_of(far_got)
    edges = (
        (0, 0, lambda row: jnp.where(even, far(row), near(row)), first_ref),
        (NB - 1, 2, lambda row: jnp.where(even, near(row), far(row)), final_ref),
    )
    for i, (block, code, outer, own) in enumerate(edges):
        correct_rest(
            block,
            code,
            outer,
            rows_of(own),
            rows_of(partial_ref.at[i]),
            neighbour_ref,
            side_ref,
            put_levels(edge_ref, block),
        )
    for i, block in enumerate((0, NB - 1)):
        copies.append(copy(edge_ref, pl.ds(block * CB, CB), 1 + i))
        copies[-1].start()
    for started in copies:
        started.wait()


def edge_side(near_got, far_got, first, final, partial, neighbours, side_weight, full):
    return pl.pallas_call(
        edge_side_kernel,
        in_specs=[IN_VMEM] * 8,
        out_specs=IN_HBM,
        out_shape=shape((LEV + 1, 2, COLS)),
        scratch_shapes=[
            pltpu.VMEM((LEV + 1, 2, COLS), F32),
            pltpu.SemaphoreType.DMA((3,)),
        ],
        compiler_params=params(4),
        name="edge_side",
    )(near_got, far_got, first, final, partial, neighbours, side_weight, full)


def exchange(x, bit):
    count = lax.axis_size("blk")
    return lax.ppermute(x, "blk", [(i, i ^ bit) for i in range(count)])


def beyond(x):
    count, bands = lax.axis_size("blk"), lax.axis_size("grp")
    pairs = []
    for i in range(count):
        for band in range(bands):
            if i in (0, count - 1):
                pairs.append((i * bands + band, i * bands + (band ^ 4)))
            else:
                pairs.append((i * bands + band, (i + (1 if i % 2 else -1)) * bands + band))
    return lax.ppermute(x, ("blk", "grp"), pairs)


def local(
    gas_state,
    cos_zenith,
    daylit,
    fine_area,
    fine_albedo,
    parent_of,
    optics_weight,
    solar_weight,
    neighbours,
    side_weight,
):
    send, keep, gas, wide, column, solar, beside, weights = surface(
        parent_of,
        fine_area,
        fine_albedo,
        optics_weight,
        cos_zenith,
        daylit,
        solar_weight,
        neighbours,
        side_weight,
        gas_state,
    )
    parts = []
    for i, blocks in enumerate(WINDOWS):
        got = exchange(send, 1 << i)
        parts.append(down(blocks, gas, wide, column, solar, keep))
        if i < 2:
            send, keep = merge(keep, got, parts[-1][2])
    first, final, near, far, albedo = up(parts, keep, got, column)
    far_got = beyond(far)
    near_got = exchange(near, 1)
    full, partial = inner(
        gas, wide, column, solar, albedo, first, final, parts, beside, weights
    )
    done = edge_side(near_got, far_got, first, final, partial, beside, weights, full)
    return done.transpose(1, 0, 2)


def solution(mesh):
    both = ("grp", "blk")
    in_specs = (
        P(None, None, both),
        P(both),
        P(both),
        P(both),
        P(None, both),
        P(both),
        P(),
        P(),
        P(None, both),
        P(None, both),
    )
    return jax.shard_map(
        local, mesh=mesh, in_specs=in_specs, out_specs=P(None, None, both), check_vma=False
    )
```

```python
import jax
import jax.numpy as jnp
from jax import lax
from jax.experimental import pallas as pl
from jax.experimental.pallas import tpu as pltpu
from jax.sharding import PartitionSpec as P

F = 16
LEV = 32
CB = 128
G = 32
KIDS = 4
NB = 8
NBLK = 8
ROWS = 72
STEP = 8
FINE_BLOCKS = NB * KIDS
COLS = NB * CB

ASYM = 0.8
TAU_SCALE = 0.08
SSA_MAX = 0.98
LOG2E = 1.4426950408889634

SLOPE = 0.5 * (1.25 + 0.75 * ASYM)
UNIT = 0.5 * SLOPE * SSA_MAX
SHIFT = 1.0 / UNIT - 1.0
BETA = 0.375 * (1.0 - ASYM) / SLOPE
RATE = -2.0 * TAU_SCALE * UNIT
SCATTER = UNIT / (0.375 * (1.0 - ASYM))

F32 = jnp.float32
BF16 = jnp.bfloat16
IN_VMEM = pl.BlockSpec(memory_space=pltpu.VMEM)
IN_HBM = pl.BlockSpec(memory_space=pltpu.HBM)
UNREAD = pl.BlockSpec(memory_space=pl.ANY)


def params(mebibytes):
    return pltpu.CompilerParams(vmem_limit_bytes=mebibytes << 20)


def shape(dims, kind=F32):
    return jax.ShapeDtypeStruct(dims, kind)


def sum_tiles(x):
    return (x[0:8] + x[8:16]) + (x[16:24] + x[24:32])


def place_albedo(parent_ref, area_ref, albedo_ref, mine):
    sub = lax.broadcasted_iota(jnp.int32, (CB, CB), 0).astype(F32).astype(BF16)
    line = lax.broadcasted_iota(jnp.int32, (8, CB), 0)
    one, zero = jnp.ones((), BF16), jnp.zeros((), BF16)
    totals = [[], [], []]
    for group in range(0, FINE_BLOCKS, 8):
        rows = slice(group, group + 8)
        area = area_ref[rows, :]
        terms = [area, area * albedo_ref[0, rows, :], area * albedo_ref[1, rows, :]]
        pieces = []
        for term in terms:
            for _ in range(3):
                piece = term.astype(BF16).astype(F32)
                pieces.append(piece)
                term = term - piece
        column = (parent_ref[rows, :] & (CB - 1)).astype(F32).astype(BF16)
        hots, values = [], []
        for j in range(8):
            hots.append(
                jnp.where(jnp.broadcast_to(column[j : j + 1, :], (CB, CB)) == sub, one, zero)
            )
            values.append(
                jnp.concatenate([jnp.where(line == j, x, 0.0) for x in pieces], axis=0).astype(
                    BF16
                )
            )
        total = lax.dot_general(
            jnp.concatenate(values, axis=1),
            jnp.concatenate(hots, axis=1),
            (((1,), (1,)), ((), ())),
            preferred_element_type=F32,
        )
        for i in range(3):
            at = 24 * i
            totals[i].append(
                total[at : at + 8] + (total[at + 8 : at + 16] + total[at + 16 : at + 24])
            )
    area = jnp.concatenate(totals[0], axis=0)
    here = area > 0.0
    safe = jnp.where(here, area, 1.0)
    owner = (parent_ref[:, 0:1] >> 7) ^ (mine * NB)
    slot = lax.broadcasted_iota(jnp.int32, (FINE_BLOCKS, NBLK * NB), 1)
    where_to = jnp.where(owner == slot, 1.0, 0.0).astype(BF16)
    placed = []
    for s in range(2):
        total = jnp.concatenate(totals[1 + s], axis=0)
        albedo = jnp.where(here, total / safe, 0.0).astype(BF16)
        placed.append(
            lax.dot_general(
                where_to, albedo, (((0,), (0,)), ((), ())), preferred_element_type=F32
            ).astype(BF16)
        )
    return placed


def spread_weights(weight_ref, wide_ref):
    row = lax.broadcasted_iota(jnp.int32, (F, F * STEP), 0)
    col = lax.broadcasted_iota(jnp.int32, (F, F * STEP), 1)
    spread = jnp.where(col // STEP == row, 1.0, 0.0).astype(BF16)
    depth = lax.broadcasted_iota(jnp.int32, (F, 2 * G), 1) < G
    scaled = weight_ref[...].astype(F32) * jnp.where(depth, LOG2E, 0.5)
    high = scaled.astype(BF16)
    low = (scaled - high.astype(F32)).astype(BF16)
    wide = jnp.concatenate(
        [
            lax.dot_general(x, spread, (((0,), (0,)), ((), ())), preferred_element_type=F32)
            for x in (high, low)
        ],
        axis=1,
    )
    level = lax.broadcasted_iota(jnp.int32, (2 * G, 2 * F * STEP), 1) % STEP
    for l in range(STEP):
        wide_ref[l * 2 * G : (l + 1) * 2 * G, :] = jnp.where(level == l, wide, 0.0).astype(BF16)


def column_constants(cosine, lit, column_ref):
    back = 0.5 * (1.0 - ASYM * cosine)
    rising = back * SCATTER
    column_ref[0] = -TAU_SCALE / cosine
    column_ref[1] = (1.0 - back) / back
    column_ref[2] = 1.0 / rising
    column_ref[3] = cosine
    column_ref[4] = lit * rising


WINDOWS = ((0,), (NB - 1, 1), (2, 3, 4))
LATE = (5, 6)


def surface_kernel(
    parent_hbm,
    area_hbm,
    albedo_hbm,
    weight_hbm,
    cosine_hbm,
    lit_hbm,
    solar_hbm,
    neighbour_hbm,
    side_hbm,
    gas_hbm,
    send_ref,
    keep_ref,
    gas_ref,
    wide_ref,
    column_ref,
    solar_ref,
    neighbour_ref,
    side_ref,
    parent_ref,
    area_ref,
    albedo_ref,
    weight_ref,
    cosine_ref,
    lit_ref,
    sun_ref,
    sems,
):
    pairs = (
        (parent_hbm, parent_ref),
        (area_hbm, area_ref),
        (albedo_hbm.at[:, 0, :], albedo_ref.at[0]),
        (albedo_hbm.at[:, 1, :], albedo_ref.at[1]),
        (weight_hbm, weight_ref),
        (cosine_hbm, cosine_ref),
        (lit_hbm, lit_ref),
        (solar_hbm, sun_ref),
        (neighbour_hbm, neighbour_ref),
        (side_hbm, side_ref),
        (gas_hbm, gas_ref),
    )
    copies = [
        pltpu.make_async_copy(source, target, sems.at[i])
        for i, (source, target) in enumerate(pairs)
    ]
    for copy in copies:
        copy.start()
    for copy in copies[:8]:
        copy.wait()
    mine = lax.axis_index("blk")
    placed = place_albedo(parent_ref, area_ref, albedo_ref, mine)
    for s in range(2):
        for i in range(NBLK // 2):
            keep_ref[i, s] = placed[s][2 * i * NB : (2 * i + 1) * NB]
            send_ref[i, s] = placed[s][(2 * i + 1) * NB : (2 * i + 2) * NB]
    spread_weights(weight_ref, wide_ref)
    column_constants(cosine_ref[...].astype(F32), lit_ref[...].astype(F32), column_ref)
    row = lax.broadcasted_iota(jnp.int32, (G, G), 0)
    col = lax.broadcasted_iota(jnp.int32, (G, G), 1)
    sun = jnp.sum(jnp.where(row == col, sun_ref[...], 0.0), axis=1, keepdims=True)
    solar_ref[...] = jnp.broadcast_to(sun, (G, CB))
    for copy in copies[8:]:
        copy.wait()


def surface(
    parent_of,
    fine_area,
    fine_albedo,
    optics_weight,
    cos_zenith,
    daylit,
    solar_weight,
    neighbours,
    side_weight,
    gas_state,
):
    return pl.pallas_call(
        surface_kernel,
        in_specs=[IN_HBM] * 10,
        out_specs=[IN_VMEM] * 8,
        out_shape=[
            shape((NBLK // 2, 2, NB, CB), BF16),
            shape((NBLK // 2, 2, NB, CB), BF16),
            shape((F, LEV, COLS), BF16),
            shape((2 * G * STEP, 2 * F * STEP), BF16),
            shape((5, NB, CB)),
            shape((G, CB)),
            shape((3, COLS), jnp.int32),
            shape((3, COLS)),
        ],
        scratch_shapes=[
            pltpu.VMEM((FINE_BLOCKS, CB), jnp.int32),
            pltpu.VMEM((FINE_BLOCKS, CB), F32),
            pltpu.VMEM((2, FINE_BLOCKS, CB), F32),
            pltpu.VMEM((F, 2 * G), BF16),
            pltpu.VMEM((NB, CB), BF16),
            pltpu.VMEM((NB, CB), jnp.int32),
            pltpu.VMEM((1, G), F32),
            pltpu.SemaphoreType.DMA((11,)),
        ],
        compiler_params=params(4),
        name="surface",
    )(
        *[
            pltpu.with_memory_space_constraint(x, pltpu.HBM)
            for x in (
                parent_of.reshape(FINE_BLOCKS, CB),
                fine_area.reshape(FINE_BLOCKS, CB),
                fine_albedo.reshape(2, FINE_BLOCKS, CB).transpose(1, 0, 2),
                optics_weight.T,
                cos_zenith.reshape(NB, CB),
                daylit.reshape(NB, CB),
                solar_weight.reshape(1, G),
                neighbours,
                side_weight,
                gas_state,
            )
        ]
    )


def merge_kernel(keep_ref, got_ref, after_ref, send_ref, next_ref):
    del after_ref
    for i in range(keep_ref.shape[0]):
        total = (keep_ref[i].astype(F32) + got_ref[i].astype(F32)).astype(BF16)
        target = send_ref if i % 2 else next_ref
        target[i // 2] = total


def merge(keep, got, after):
    half = shape((keep.shape[0] // 2,) + keep.shape[1:], BF16)
    return pl.pallas_call(
        merge_kernel,
        in_specs=[IN_VMEM, IN_VMEM, UNREAD],
        out_specs=[IN_VMEM] * 2,
        out_shape=[half, half],
        compiler_params=params(2),
        name="merge",
    )(keep, got, after)


def layer_terms(depth_mix, albedo_mix, slant_rate):
    soft = jnp.maximum(depth_mix, jnp.log2(1.0 + jnp.exp2(jnp.minimum(depth_mix, 60.0))))
    e_dir = jnp.exp2(soft * slant_rate)
    bend = jnp.tanh(albedo_mix)
    gamma_one = SHIFT - bend
    gamma_two = BETA * bend + BETA
    product = (gamma_one - gamma_two) * (gamma_one + gamma_two)
    root = product * lax.rsqrt(product)
    damping = jnp.exp2(RATE * (root * soft))
    damped_sq = damping * damping
    lost = 1.0 - damped_sq
    even = root + root * damped_sq
    odd = gamma_one * lost
    transmit = (root + root) * damping
    return e_dir, gamma_two, even + odd, even - odd, gamma_two * lost, transmit


def mix_all(gas_ref, lanes, wide_ref):
    products = []
    for step in range(LEV // STEP):
        gas = gas_ref[:, step * STEP : (step + 1) * STEP, lanes].reshape(F * STEP, CB)
        products.append(
            jnp.dot(
                wide_ref[...],
                jnp.concatenate([gas, gas], axis=0),
                preferred_element_type=F32,
            )
        )
    return products


def eliminate(block, gas_ref, wide_ref, column_ref, solar_ref, coef_ref, esum_ref, state_ref):
    products = mix_all(gas_ref, slice(block * CB, (block + 1) * CB), wide_ref)
    slant_rate, falling, scale, cosine = [
        column_ref[i, block : block + 1, :] for i in range(4)
    ]
    direct = solar_ref[...] * cosine
    above = jnp.zeros((G, CB), F32)
    source = jnp.zeros((G, CB), F32)
    for l in range(LEV):
        at = (l % STEP) * 2 * G
        mix = products[l // STEP]
        e_dir, gamma_two, divisor, mirrored, reflect, transmit = layer_terms(
            mix[at : at + G], mix[at + G : at + 2 * G], slant_rate
        )
        esum_ref[l] = sum_tiles(direct) * scale + sum_tiles(source)
        below = direct * e_dir
        scattered = gamma_two * (direct - below)
        inverse = pl.reciprocal(divisor - above * reflect, approx=False)
        incident = (source + above * scattered) * inverse
        coef_ref[l, 0] = above
        coef_ref[l, 1] = transmit * inverse
        coef_ref[l, 2] = scattered + reflect * incident
        source = scattered * falling + transmit * incident
        above = (reflect + above * mirrored) * inverse
        direct = below
    esum_ref[LEV] = sum_tiles(direct) * scale + sum_tiles(source)
    state_ref[0] = above
    state_ref[1] = source
    state_ref[2] = direct * scale


def add_sublanes(rows):
    sub = lax.broadcasted_iota(jnp.int32, (8, CB), 0)
    four, two, one = sub < 4, (sub & 2) == 0, (sub & 1) == 0
    rows = [
        jnp.where(four, rows[r], rows[r + 4])
        + pltpu.roll(jnp.where(four, rows[r + 4], rows[r]), 4, 0)
        for r in range(4)
    ]
    rows = [
        jnp.where(
            two,
            rows[r] + pltpu.roll(rows[r], 6, 0),
            rows[r + 2] + pltpu.roll(rows[r + 2], 2, 0),
        )
        for r in range(2)
    ]
    return jnp.where(
        one, rows[0] + pltpu.roll(rows[0], 7, 0), rows[1] + pltpu.roll(rows[1], 1, 0)
    )


def substitute(coef_ref, esum_ref, state_ref, albedo_direct, albedo_diffuse, lit, flux_ref):
    above, source, direct = state_ref[0], state_ref[1], state_ref[2]
    upward = (albedo_diffuse * source + albedo_direct * direct) * pl.reciprocal(
        1.0 - albedo_diffuse * above, approx=False
    )
    none = jnp.zeros((8, CB), F32)
    pending = [esum_ref[LEV] + sum_tiles(above * upward), sum_tiles(upward)] + [none] * 6
    flux_ref[2 * LEV : 2 * LEV + 8, :] = add_sublanes(pending) * lit
    pending = []
    for l in range(LEV - 1, -1, -1):
        upward = coef_ref[l, 1] * upward + coef_ref[l, 2]
        pending = [
            esum_ref[l] + sum_tiles(coef_ref[l, 0] * upward),
            sum_tiles(upward),
        ] + pending
        if l % 4 == 0:
            flux_ref[2 * l : 2 * l + 8, :] = add_sublanes(pending) * lit
            pending = []


COEF = (LEV, 3, G, CB)
ESUM = (LEV + 1, 8, CB)
STATE = (3, G, CB)


def down_kernel(blocks):
    def kernel(gas_ref, wide_ref, column_ref, solar_ref, after_ref, coef_ref, esum_ref, state_ref):
        del after_ref
        for i, block in enumerate(blocks):
            eliminate(
                block,
                gas_ref,
                wide_ref,
                column_ref,
                solar_ref,
                coef_ref.at[i],
                esum_ref.at[i],
                state_ref.at[i],
            )

    return kernel


def down(blocks, gas, wide, column, solar, after):
    count = len(blocks)
    return pl.pallas_call(
        down_kernel(blocks),
        in_specs=[IN_VMEM] * 4 + [UNREAD],
        out_specs=[IN_VMEM] * 3,
        out_shape=[shape((count,) + x) for x in (COEF, ESUM, STATE)],
        compiler_params=params(24),
        cost_estimate=pl.CostEstimate(
            flops=200000000 * count, transcendentals=0, bytes_accessed=4000000
        ),
        name="down",
    )(gas, wide, column, solar, after)


def ground(albedo_ref, column_ref, block):
    row = slice(block, block + 1)
    return albedo_ref[0, row, :], albedo_ref[1, row, :], column_ref[4, row, :]


def up_kernel(
    coef_a,
    esum_a,
    state_a,
    coef_b,
    esum_b,
    state_b,
    keep_ref,
    got_ref,
    column_ref,
    first_ref,
    final_ref,
    near_ref,
    far_ref,
    albedo_ref,
):
    for s in range(2):
        albedo_ref[s] = keep_ref[0, s].astype(F32) + got_ref[0, s].astype(F32)
    substitute(
        coef_a.at[0], esum_a.at[0], state_a.at[0], *ground(albedo_ref, column_ref, 0), first_ref
    )
    substitute(
        coef_b.at[0],
        esum_b.at[0],
        state_b.at[0],
        *ground(albedo_ref, column_ref, NB - 1),
        final_ref,
    )
    even = lax.axis_index("blk") % 2 == 0
    near_ref[...] = jnp.where(even, final_ref[...], first_ref[...])
    far_ref[...] = jnp.where(even, first_ref[...], final_ref[...])


def up(parts, keep, got, column):
    return pl.pallas_call(
        up_kernel,
        in_specs=[IN_VMEM] * 9,
        out_specs=[IN_VMEM] * 5,
        out_shape=[shape((ROWS, CB))] * 4 + [shape((2, NB, CB))],
        compiler_params=params(2),
        cost_estimate=pl.CostEstimate(flops=4000000, transcendentals=0, bytes_accessed=4000000),
        name="up",
    )(*parts[0], *parts[1], keep, got, column)


def neighbour_rows(block, neighbour_ref, side_ref):
    lanes = slice(block * CB, (block + 1) * CB)
    at_lane, places, weights = [], [], []
    for k in range(3):
        at = jnp.broadcast_to(neighbour_ref[k : k + 1, lanes], (8, CB))
        places.append(((at >> 7) - block + 1) & (NB - 1))
        at_lane.append(at & (CB - 1))
        weights.append(jnp.broadcast_to(side_ref[k : k + 1, lanes], (8, CB)))
    return at_lane, places, weights


def pick(x, at_lane):
    return jnp.take_along_axis(x, at_lane, axis=1, mode="promise_in_bounds")


def correct(block, before, own, after, neighbour_ref, side_ref, put):
    at_lane, places, weights = neighbour_rows(block, neighbour_ref, side_ref)
    for k in range(3):
        for code, part in ((0, before), (2, after)):
            if part is None:
                weights[k] = jnp.where(places[k] == code, 0.0, weights[k])
    totals = {row: own(row) for row in range(0, ROWS, 8)}
    for k in range(3):
        for row in totals:
            here = own(row)
            beside = pick(here, at_lane[k])
            for code, part in ((0, before), (2, after)):
                if part is not None:
                    beside = jnp.where(places[k] == code, pick(part(row), at_lane[k]), beside)
            totals[row] = totals[row] + weights[k] * (beside - here)
    for row, total in totals.items():
        put(row, total)


def correct_rest(block, code, outer, own, partial, neighbour_ref, side_ref, put):
    at_lane, places, weights = neighbour_rows(block, neighbour_ref, side_ref)
    weights = [jnp.where(places[k] == code, weights[k], 0.0) for k in range(3)]
    totals = {row: partial(row) for row in range(0, ROWS, 8)}
    for k in range(3):
        for row in totals:
            beside = pick(outer(row), at_lane[k])
            totals[row] = totals[row] + weights[k] * (beside - own(row))
    for row, total in totals.items():
        put(row, total)


def put_levels(out_ref, block):
    lanes = slice(block * CB, (block + 1) * CB)

    def put(row, total):
        for l in range(row // 2, min(row // 2 + 4, LEV + 1)):
            out_ref[l, :, lanes] = total[2 * l - row : 2 * l - row + 2]

    return put


def rows_of(ref):
    return lambda row: ref[row : row + 8, :]


def inner_kernel(
    gas_ref,
    wide_ref,
    column_ref,
    solar_ref,
    albedo_ref,
    first_ref,
    final_ref,
    coef_b,
    esum_b,
    state_b,
    coef_c,
    esum_c,
    state_c,
    neighbour_ref,
    side_ref,
    out_ref,
    partial_ref,
    coef_ref,
    esum_ref,
    state_ref,
    flux_ref,
):
    kept = {1: (coef_b.at[1], esum_b.at[1], state_b.at[1])}
    for i, n in enumerate(WINDOWS[2]):
        kept[n] = coef_c.at[i], esum_c.at[i], state_c.at[i]
    for i, n in enumerate(LATE):
        kept[n] = coef_ref.at[i], esum_ref.at[i], state_ref.at[i]
    flux = {0: first_ref, NB - 1: final_ref}
    for n in range(1, NB - 1):
        flux[n] = flux_ref.at[n - 1]

    def finish(n):
        substitute(*kept[n], *ground(albedo_ref, column_ref, n), flux[n])

    def side(n):
        before, own, after = [
            rows_of(flux[n + i]) if n + i in flux else None for i in (-1, 0, 1)
        ]
        if n in (0, NB - 1):
            partial = partial_ref.at[n // (NB - 1)]

            def put(row, total):
                partial[row : row + 8, :] = total

        else:
            put = put_levels(out_ref, n)
        correct(n, before, own, after, neighbour_ref, side_ref, put)

    for n in LATE:
        eliminate(n, gas_ref, wide_ref, column_ref, solar_ref, *kept[n])
    for n in range(1, NB - 1):
        finish(n)
    for n in range(NB):
        side(n)


def inner(gas, wide, column, solar, albedo, first, final, parts, neighbours, side_weight):
    return pl.pallas_call(
        inner_kernel,
        in_specs=[IN_VMEM] * 15,
        out_specs=[IN_VMEM] * 2,
        out_shape=[shape((LEV + 1, 2, COLS)), shape((2, ROWS, CB))],
        scratch_shapes=[
            pltpu.VMEM((len(LATE),) + COEF, F32),
            pltpu.VMEM((len(LATE),) + ESUM, F32),
            pltpu.VMEM((len(LATE),) + STATE, F32),
            pltpu.VMEM((NB - 2, ROWS, CB), F32),
        ],
        compiler_params=params(24),
        cost_estimate=pl.CostEstimate(
            flops=2000000000, transcendentals=0, bytes_accessed=4000000
        ),
        name="inner",
    )(
        gas,
        wide,
        column,
        solar,
        albedo,
        first,
        final,
        *parts[1],
        *parts[2],
        neighbours,
        side_weight,
    )


def edge_side_kernel(
    far_got,
    near_got,
    first_ref,
    final_ref,
    partial_ref,
    neighbour_ref,
    side_ref,
    full_ref,
    out_hbm,
    edge_ref,
    sems,
):
    def copy(source, lanes, i):
        return pltpu.make_async_copy(
            source.at[:, :, lanes], out_hbm.at[:, :, lanes], sems.at[i]
        )

    copies = [copy(full_ref, pl.ds(CB, COLS - 2 * CB), 0)]
    copies[0].start()
    even = lax.axis_index("blk") % 2 == 0
    near, far = rows_of(near_got), rows_of(far_got)
    edges = (
        (0, 0, lambda row: jnp.where(even, far(row), near(row)), first_ref),
        (NB - 1, 2, lambda row: jnp.where(even, near(row), far(row)), final_ref),
    )
    for i, (block, code, outer, own) in enumerate(edges):
        correct_rest(
            block,
            code,
            outer,
            rows_of(own),
            rows_of(partial_ref.at[i]),
            neighbour_ref,
            side_ref,
            put_levels(edge_ref, block),
        )
    for i, block in enumerate((0, NB - 1)):
        copies.append(copy(edge_ref, pl.ds(block * CB, CB), 1 + i))
        copies[-1].start()
    for started in copies:
        started.wait()


def edge_side(far_got, near_got, first, final, partial, neighbours, side_weight, full):
    return pl.pallas_call(
        edge_side_kernel,
        in_specs=[IN_VMEM] * 8,
        out_specs=IN_HBM,
        out_shape=shape((LEV + 1, 2, COLS)),
        scratch_shapes=[
            pltpu.VMEM((LEV + 1, 2, COLS), F32),
            pltpu.SemaphoreType.DMA((3,)),
        ],
        compiler_params=params(4),
        name="edge_side",
    )(far_got, near_got, first, final, partial, neighbours, side_weight, full)


def exchange(x, bit):
    count = lax.axis_size("blk")
    return lax.ppermute(x, "blk", [(i, i ^ bit) for i in range(count)])


def beyond(x):
    count, bands = lax.axis_size("blk"), lax.axis_size("grp")
    pairs = []
    for i in range(count):
        for band in range(bands):
            if i in (0, count - 1):
                pairs.append((i * bands + band, i * bands + (band ^ 4)))
            else:
                pairs.append((i * bands + band, (i + (1 if i % 2 else -1)) * bands + band))
    return lax.ppermute(x, ("blk", "grp"), pairs)


def local(
    gas_state,
    cos_zenith,
    daylit,
    fine_area,
    fine_albedo,
    parent_of,
    optics_weight,
    solar_weight,
    neighbours,
    side_weight,
):
    send, keep, gas, wide, column, solar, beside, weights = surface(
        parent_of,
        fine_area,
        fine_albedo,
        optics_weight,
        cos_zenith,
        daylit,
        solar_weight,
        neighbours,
        side_weight,
        gas_state,
    )
    parts = []
    for i, blocks in enumerate(WINDOWS):
        got = exchange(send, 1 << i)
        parts.append(down(blocks, gas, wide, column, solar, keep))
        if i < 2:
            send, keep = merge(keep, got, parts[-1][2])
    first, final, near, far, albedo = up(parts, keep, got, column)
    far_got = beyond(far)
    near_got = exchange(near, 1)
    full, partial = inner(
        gas, wide, column, solar, albedo, first, final, parts, beside, weights
    )
    done = edge_side(far_got, near_got, first, final, partial, beside, weights, full)
    return done.transpose(1, 0, 2)


def solution(mesh):
    both = ("grp", "blk")
    in_specs = (
        P(None, None, both),
        P(both),
        P(both),
        P(both),
        P(None, both),
        P(both),
        P(),
        P(),
        P(None, both),
        P(None, both),
    )
    return jax.shard_map(
        local, mesh=mesh, in_specs=in_specs, out_specs=P(None, None, both), check_vma=False
    )
```

```python
import jax
import jax.numpy as jnp
from jax import lax
from jax.experimental import pallas as pl
from jax.experimental.pallas import tpu as pltpu
from jax.sharding import PartitionSpec as P

F = 16
LEV = 32
CB = 128
G = 32
KIDS = 4
NB = 8
NBLK = 8
ROWS = 72
STEP = 8
FINE_BLOCKS = NB * KIDS
COLS = NB * CB

ASYM = 0.8
TAU_SCALE = 0.08
SSA_MAX = 0.98
LOG2E = 1.4426950408889634

SLOPE = 0.5 * (1.25 + 0.75 * ASYM)
UNIT = 0.5 * SLOPE * SSA_MAX
SHIFT = 1.0 / UNIT - 1.0
BETA = 0.375 * (1.0 - ASYM) / SLOPE
RATE = -2.0 * TAU_SCALE * UNIT
SCATTER = UNIT / (0.375 * (1.0 - ASYM))

F32 = jnp.float32
BF16 = jnp.bfloat16
IN_VMEM = pl.BlockSpec(memory_space=pltpu.VMEM)
IN_HBM = pl.BlockSpec(memory_space=pltpu.HBM)
UNREAD = pl.BlockSpec(memory_space=pl.ANY)


def params(mebibytes):
    return pltpu.CompilerParams(vmem_limit_bytes=mebibytes << 20)


def shape(dims, kind=F32):
    return jax.ShapeDtypeStruct(dims, kind)


def sum_tiles(x):
    return (x[0:8] + x[8:16]) + (x[16:24] + x[24:32])


def place_albedo(parent_ref, area_ref, albedo_ref, mine):
    sub = lax.broadcasted_iota(jnp.int32, (CB, CB), 0).astype(F32).astype(BF16)
    line = lax.broadcasted_iota(jnp.int32, (8, CB), 0)
    one, zero = jnp.ones((), BF16), jnp.zeros((), BF16)
    totals = [[], [], []]
    for group in range(0, FINE_BLOCKS, 8):
        rows = slice(group, group + 8)
        area = area_ref[rows, :]
        terms = [area, area * albedo_ref[0, rows, :], area * albedo_ref[1, rows, :]]
        pieces = []
        for term in terms:
            for _ in range(3):
                piece = term.astype(BF16).astype(F32)
                pieces.append(piece)
                term = term - piece
        column = (parent_ref[rows, :] & (CB - 1)).astype(F32).astype(BF16)
        hots, values = [], []
        for j in range(8):
            hots.append(
                jnp.where(jnp.broadcast_to(column[j : j + 1, :], (CB, CB)) == sub, one, zero)
            )
            values.append(
                jnp.concatenate([jnp.where(line == j, x, 0.0) for x in pieces], axis=0).astype(
                    BF16
                )
            )
        total = lax.dot_general(
            jnp.concatenate(values, axis=1),
            jnp.concatenate(hots, axis=1),
            (((1,), (1,)), ((), ())),
            preferred_element_type=F32,
        )
        for i in range(3):
            at = 24 * i
            totals[i].append(
                total[at : at + 8] + (total[at + 8 : at + 16] + total[at + 16 : at + 24])
            )
    area = jnp.concatenate(totals[0], axis=0)
    here = area > 0.0
    safe = jnp.where(here, area, 1.0)
    owner = (parent_ref[:, 0:1] >> 7) ^ (mine * NB)
    slot = lax.broadcasted_iota(jnp.int32, (FINE_BLOCKS, NBLK * NB), 1)
    where_to = jnp.where(owner == slot, 1.0, 0.0).astype(BF16)
    placed = []
    for s in range(2):
        total = jnp.concatenate(totals[1 + s], axis=0)
        albedo = jnp.where(here, total / safe, 0.0).astype(BF16)
        placed.append(
            lax.dot_general(
                where_to, albedo, (((0,), (0,)), ((), ())), preferred_element_type=F32
            ).astype(BF16)
        )
    return placed


def spread_weights(weight_ref, wide_ref):
    row = lax.broadcasted_iota(jnp.int32, (F, F * STEP), 0)
    col = lax.broadcasted_iota(jnp.int32, (F, F * STEP), 1)
    spread = jnp.where(col // STEP == row, 1.0, 0.0).astype(BF16)
    depth = lax.broadcasted_iota(jnp.int32, (F, 2 * G), 1) < G
    scaled = weight_ref[...].astype(F32) * jnp.where(depth, LOG2E, 0.5)
    high = scaled.astype(BF16)
    low = (scaled - high.astype(F32)).astype(BF16)
    wide = jnp.concatenate(
        [
            lax.dot_general(x, spread, (((0,), (0,)), ((), ())), preferred_element_type=F32)
            for x in (high, low)
        ],
        axis=1,
    )
    level = lax.broadcasted_iota(jnp.int32, (2 * G, 2 * F * STEP), 1) % STEP
    for l in range(STEP):
        wide_ref[l * 2 * G : (l + 1) * 2 * G, :] = jnp.where(level == l, wide, 0.0).astype(BF16)


def column_constants(cosine, lit, column_ref):
    back = 0.5 * (1.0 - ASYM * cosine)
    rising = back * SCATTER
    column_ref[0] = -TAU_SCALE / cosine
    column_ref[1] = (1.0 - back) / back
    column_ref[2] = 1.0 / rising
    column_ref[3] = cosine
    column_ref[4] = lit * rising


WINDOWS = ((0,), (NB - 1, 1, 2), (3, 4))
LATE = (5, 6)


def surface_kernel(
    parent_hbm,
    area_hbm,
    albedo_hbm,
    weight_hbm,
    cosine_hbm,
    lit_hbm,
    solar_hbm,
    neighbour_hbm,
    side_hbm,
    gas_hbm,
    send_ref,
    keep_ref,
    gas_ref,
    wide_ref,
    column_ref,
    solar_ref,
    neighbour_ref,
    side_ref,
    parent_ref,
    area_ref,
    albedo_ref,
    weight_ref,
    cosine_ref,
    lit_ref,
    sun_ref,
    sems,
):
    pairs = (
        (parent_hbm, parent_ref),
        (area_hbm, area_ref),
        (albedo_hbm.at[:, 0, :], albedo_ref.at[0]),
        (albedo_hbm.at[:, 1, :], albedo_ref.at[1]),
        (weight_hbm, weight_ref),
        (cosine_hbm, cosine_ref),
        (lit_hbm, lit_ref),
        (solar_hbm, sun_ref),
        (neighbour_hbm, neighbour_ref),
        (side_hbm, side_ref),
        (gas_hbm, gas_ref),
    )
    copies = [
        pltpu.make_async_copy(source, target, sems.at[i])
        for i, (source, target) in enumerate(pairs)
    ]
    for copy in copies:
        copy.start()
    for copy in copies[:8]:
        copy.wait()
    mine = lax.axis_index("blk")
    placed = place_albedo(parent_ref, area_ref, albedo_ref, mine)
    for s in range(2):
        for i in range(NBLK // 2):
            keep_ref[i, s] = placed[s][2 * i * NB : (2 * i + 1) * NB]
            send_ref[i, s] = placed[s][(2 * i + 1) * NB : (2 * i + 2) * NB]
    spread_weights(weight_ref, wide_ref)
    column_constants(cosine_ref[...].astype(F32), lit_ref[...].astype(F32), column_ref)
    row = lax.broadcasted_iota(jnp.int32, (G, G), 0)
    col = lax.broadcasted_iota(jnp.int32, (G, G), 1)
    sun = jnp.sum(jnp.where(row == col, sun_ref[...], 0.0), axis=1, keepdims=True)
    solar_ref[...] = jnp.broadcast_to(sun, (G, CB))
    for copy in copies[8:]:
        copy.wait()


def surface(
    parent_of,
    fine_area,
    fine_albedo,
    optics_weight,
    cos_zenith,
    daylit,
    solar_weight,
    neighbours,
    side_weight,
    gas_state,
):
    return pl.pallas_call(
        surface_kernel,
        in_specs=[IN_HBM] * 10,
        out_specs=[IN_VMEM] * 8,
        out_shape=[
            shape((NBLK // 2, 2, NB, CB), BF16),
            shape((NBLK // 2, 2, NB, CB), BF16),
            shape((F, LEV, COLS), BF16),
            shape((2 * G * STEP, 2 * F * STEP), BF16),
            shape((5, NB, CB)),
            shape((G, CB)),
            shape((3, COLS), jnp.int32),
            shape((3, COLS)),
        ],
        scratch_shapes=[
            pltpu.VMEM((FINE_BLOCKS, CB), jnp.int32),
            pltpu.VMEM((FINE_BLOCKS, CB), F32),
            pltpu.VMEM((2, FINE_BLOCKS, CB), F32),
            pltpu.VMEM((F, 2 * G), BF16),
            pltpu.VMEM((NB, CB), BF16),
            pltpu.VMEM((NB, CB), jnp.int32),
            pltpu.VMEM((1, G), F32),
            pltpu.SemaphoreType.DMA((11,)),
        ],
        compiler_params=params(4),
        name="surface",
    )(
        *[
            pltpu.with_memory_space_constraint(x, pltpu.HBM)
            for x in (
                parent_of.reshape(FINE_BLOCKS, CB),
                fine_area.reshape(FINE_BLOCKS, CB),
                fine_albedo.reshape(2, FINE_BLOCKS, CB).transpose(1, 0, 2),
                optics_weight.T,
                cos_zenith.reshape(NB, CB),
                daylit.reshape(NB, CB),
                solar_weight.reshape(1, G),
                neighbours,
                side_weight,
                gas_state,
            )
        ]
    )


def merge_kernel(keep_ref, got_ref, after_ref, send_ref, next_ref):
    del after_ref
    for i in range(keep_ref.shape[0]):
        total = (keep_ref[i].astype(F32) + got_ref[i].astype(F32)).astype(BF16)
        target = send_ref if i % 2 else next_ref
        target[i // 2] = total


def merge(keep, got, after):
    half = shape((keep.shape[0] // 2,) + keep.shape[1:], BF16)
    return pl.pallas_call(
        merge_kernel,
        in_specs=[IN_VMEM, IN_VMEM, UNREAD],
        out_specs=[IN_VMEM] * 2,
        out_shape=[half, half],
        compiler_params=params(2),
        name="merge",
    )(keep, got, after)


def layer_terms(depth_mix, albedo_mix, slant_rate):
    soft = jnp.maximum(depth_mix, jnp.log2(1.0 + jnp.exp2(jnp.minimum(depth_mix, 60.0))))
    e_dir = jnp.exp2(soft * slant_rate)
    bend = jnp.tanh(albedo_mix)
    gamma_one = SHIFT - bend
    gamma_two = BETA * bend + BETA
    product = (gamma_one - gamma_two) * (gamma_one + gamma_two)
    root = product * lax.rsqrt(product)
    damping = jnp.exp2(RATE * (root * soft))
    damped_sq = damping * damping
    lost = 1.0 - damped_sq
    even = root + root * damped_sq
    odd = gamma_one * lost
    transmit = (root + root) * damping
    return e_dir, gamma_two, even + odd, even - odd, gamma_two * lost, transmit


def mix_all(gas_ref, lanes, wide_ref):
    products = []
    for step in range(LEV // STEP):
        gas = gas_ref[:, step * STEP : (step + 1) * STEP, lanes].reshape(F * STEP, CB)
        products.append(
            jnp.dot(
                wide_ref[...],
                jnp.concatenate([gas, gas], axis=0),
                preferred_element_type=F32,
            )
        )
    return products


def eliminate(block, gas_ref, wide_ref, column_ref, solar_ref, coef_ref, esum_ref, state_ref):
    products = mix_all(gas_ref, slice(block * CB, (block + 1) * CB), wide_ref)
    slant_rate, falling, scale, cosine = [
        column_ref[i, block : block + 1, :] for i in range(4)
    ]
    direct = solar_ref[...] * cosine
    above = jnp.zeros((G, CB), F32)
    source = jnp.zeros((G, CB), F32)
    for l in range(LEV):
        at = (l % STEP) * 2 * G
        mix = products[l // STEP]
        e_dir, gamma_two, divisor, mirrored, reflect, transmit = layer_terms(
            mix[at : at + G], mix[at + G : at + 2 * G], slant_rate
        )
        esum_ref[l] = sum_tiles(direct) * scale + sum_tiles(source)
        below = direct * e_dir
        scattered = gamma_two * (direct - below)
        inverse = pl.reciprocal(divisor - above * reflect, approx=False)
        incident = (source + above * scattered) * inverse
        coef_ref[l, 0] = above
        coef_ref[l, 1] = transmit * inverse
        coef_ref[l, 2] = scattered + reflect * incident
        source = scattered * falling + transmit * incident
        above = (reflect + above * mirrored) * inverse
        direct = below
    esum_ref[LEV] = sum_tiles(direct) * scale + sum_tiles(source)
    state_ref[0] = above
    state_ref[1] = source
    state_ref[2] = direct * scale


def add_sublanes(rows):
    sub = lax.broadcasted_iota(jnp.int32, (8, CB), 0)
    four, two, one = sub < 4, (sub & 2) == 0, (sub & 1) == 0
    rows = [
        jnp.where(four, rows[r], rows[r + 4])
        + pltpu.roll(jnp.where(four, rows[r + 4], rows[r]), 4, 0)
        for r in range(4)
    ]
    rows = [
        jnp.where(
            two,
            rows[r] + pltpu.roll(rows[r], 6, 0),
            rows[r + 2] + pltpu.roll(rows[r + 2], 2, 0),
        )
        for r in range(2)
    ]
    return jnp.where(
        one, rows[0] + pltpu.roll(rows[0], 7, 0), rows[1] + pltpu.roll(rows[1], 1, 0)
    )


def substitute(coef_ref, esum_ref, state_ref, albedo_direct, albedo_diffuse, lit, flux_ref):
    above, source, direct = state_ref[0], state_ref[1], state_ref[2]
    upward = (albedo_diffuse * source + albedo_direct * direct) * pl.reciprocal(
        1.0 - albedo_diffuse * above, approx=False
    )
    none = jnp.zeros((8, CB), F32)
    pending = [esum_ref[LEV] + sum_tiles(above * upward), sum_tiles(upward)] + [none] * 6
    flux_ref[2 * LEV : 2 * LEV + 8, :] = add_sublanes(pending) * lit
    pending = []
    for l in range(LEV - 1, -1, -1):
        upward = coef_ref[l, 1] * upward + coef_ref[l, 2]
        pending = [
            esum_ref[l] + sum_tiles(coef_ref[l, 0] * upward),
            sum_tiles(upward),
        ] + pending
        if l % 4 == 0:
            flux_ref[2 * l : 2 * l + 8, :] = add_sublanes(pending) * lit
            pending = []


COEF = (LEV, 3, G, CB)
ESUM = (LEV + 1, 8, CB)
STATE = (3, G, CB)


def down_kernel(blocks):
    def kernel(gas_ref, wide_ref, column_ref, solar_ref, after_ref, coef_ref, esum_ref, state_ref):
        del after_ref
        for i, block in enumerate(blocks):
            eliminate(
                block,
                gas_ref,
                wide_ref,
                column_ref,
                solar_ref,
                coef_ref.at[i],
                esum_ref.at[i],
                state_ref.at[i],
            )

    return kernel


def down(blocks, gas, wide, column, solar, after):
    count = len(blocks)
    return pl.pallas_call(
        down_kernel(blocks),
        in_specs=[IN_VMEM] * 4 + [UNREAD],
        out_specs=[IN_VMEM] * 3,
        out_shape=[shape((count,) + x) for x in (COEF, ESUM, STATE)],
        compiler_params=params(24),
        cost_estimate=pl.CostEstimate(
            flops=200000000 * count, transcendentals=0, bytes_accessed=4000000
        ),
        name="down",
    )(gas, wide, column, solar, after)


def ground(albedo_ref, column_ref, block):
    row = slice(block, block + 1)
    return albedo_ref[0, row, :], albedo_ref[1, row, :], column_ref[4, row, :]


def up_kernel(
    coef_a,
    esum_a,
    state_a,
    coef_b,
    esum_b,
    state_b,
    keep_ref,
    got_ref,
    column_ref,
    first_ref,
    final_ref,
    near_ref,
    far_ref,
    albedo_ref,
):
    for s in range(2):
        albedo_ref[s] = keep_ref[0, s].astype(F32) + got_ref[0, s].astype(F32)
    substitute(
        coef_a.at[0], esum_a.at[0], state_a.at[0], *ground(albedo_ref, column_ref, 0), first_ref
    )
    substitute(
        coef_b.at[0],
        esum_b.at[0],
        state_b.at[0],
        *ground(albedo_ref, column_ref, NB - 1),
        final_ref,
    )
    even = lax.axis_index("blk") % 2 == 0
    near_ref[...] = jnp.where(even, final_ref[...], first_ref[...])
    far_ref[...] = jnp.where(even, first_ref[...], final_ref[...])


def up(parts, keep, got, column):
    return pl.pallas_call(
        up_kernel,
        in_specs=[IN_VMEM] * 9,
        out_specs=[IN_VMEM] * 5,
        out_shape=[shape((ROWS, CB))] * 4 + [shape((2, NB, CB))],
        compiler_params=params(2),
        cost_estimate=pl.CostEstimate(flops=4000000, transcendentals=0, bytes_accessed=4000000),
        name="up",
    )(*parts[0], *parts[1], keep, got, column)


def neighbour_rows(block, neighbour_ref, side_ref):
    lanes = slice(block * CB, (block + 1) * CB)
    at_lane, places, weights = [], [], []
    for k in range(3):
        at = jnp.broadcast_to(neighbour_ref[k : k + 1, lanes], (8, CB))
        places.append(((at >> 7) - block + 1) & (NB - 1))
        at_lane.append(at & (CB - 1))
        weights.append(jnp.broadcast_to(side_ref[k : k + 1, lanes], (8, CB)))
    return at_lane, places, weights


def pick(x, at_lane):
    return jnp.take_along_axis(x, at_lane, axis=1, mode="promise_in_bounds")


def correct(block, before, own, after, neighbour_ref, side_ref, put):
    at_lane, places, weights = neighbour_rows(block, neighbour_ref, side_ref)
    for k in range(3):
        for code, part in ((0, before), (2, after)):
            if part is None:
                weights[k] = jnp.where(places[k] == code, 0.0, weights[k])
    totals = {row: own(row) for row in range(0, ROWS, 8)}
    for k in range(3):
        for row in totals:
            here = own(row)
            beside = pick(here, at_lane[k])
            for code, part in ((0, before), (2, after)):
                if part is not None:
                    beside = jnp.where(places[k] == code, pick(part(row), at_lane[k]), beside)
            totals[row] = totals[row] + weights[k] * (beside - here)
    for row, total in totals.items():
        put(row, total)


def correct_rest(block, code, outer, own, partial, neighbour_ref, side_ref, put):
    at_lane, places, weights = neighbour_rows(block, neighbour_ref, side_ref)
    weights = [jnp.where(places[k] == code, weights[k], 0.0) for k in range(3)]
    totals = {row: partial(row) for row in range(0, ROWS, 8)}
    for k in range(3):
        for row in totals:
            beside = pick(outer(row), at_lane[k])
            totals[row] = totals[row] + weights[k] * (beside - own(row))
    for row, total in totals.items():
        put(row, total)


def put_levels(out_ref, block):
    lanes = slice(block * CB, (block + 1) * CB)

    def put(row, total):
        for l in range(row // 2, min(row // 2 + 4, LEV + 1)):
            out_ref[l, :, lanes] = total[2 * l - row : 2 * l - row + 2]

    return put


def rows_of(ref):
    return lambda row: ref[row : row + 8, :]


def inner_kernel(
    gas_ref,
    wide_ref,
    column_ref,
    solar_ref,
    albedo_ref,
    first_ref,
    final_ref,
    coef_b,
    esum_b,
    state_b,
    coef_c,
    esum_c,
    state_c,
    neighbour_ref,
    side_ref,
    out_ref,
    partial_ref,
    coef_ref,
    esum_ref,
    state_ref,
    flux_ref,
):
    kept = {}
    for i, n in enumerate(WINDOWS[1]):
        kept[n] = coef_b.at[i], esum_b.at[i], state_b.at[i]
    for i, n in enumerate(WINDOWS[2]):
        kept[n] = coef_c.at[i], esum_c.at[i], state_c.at[i]
    for i, n in enumerate(LATE):
        kept[n] = coef_ref.at[i], esum_ref.at[i], state_ref.at[i]
    flux = {0: first_ref, NB - 1: final_ref}
    for n in range(1, NB - 1):
        flux[n] = flux_ref.at[n - 1]

    def finish(n):
        substitute(*kept[n], *ground(albedo_ref, column_ref, n), flux[n])

    def side(n):
        before, own, after = [
            rows_of(flux[n + i]) if n + i in flux else None for i in (-1, 0, 1)
        ]
        if n in (0, NB - 1):
            partial = partial_ref.at[n // (NB - 1)]

            def put(row, total):
                partial[row : row + 8, :] = total

        else:
            put = put_levels(out_ref, n)
        correct(n, before, own, after, neighbour_ref, side_ref, put)

    for n in LATE:
        eliminate(n, gas_ref, wide_ref, column_ref, solar_ref, *kept[n])
    for n in range(1, NB - 1):
        finish(n)
    for n in range(NB):
        side(n)


def inner(gas, wide, column, solar, albedo, first, final, parts, neighbours, side_weight):
    return pl.pallas_call(
        inner_kernel,
        in_specs=[IN_VMEM] * 15,
        out_specs=[IN_VMEM] * 2,
        out_shape=[shape((LEV + 1, 2, COLS)), shape((2, ROWS, CB))],
        scratch_shapes=[
            pltpu.VMEM((len(LATE),) + COEF, F32),
            pltpu.VMEM((len(LATE),) + ESUM, F32),
            pltpu.VMEM((len(LATE),) + STATE, F32),
            pltpu.VMEM((NB - 2, ROWS, CB), F32),
        ],
        compiler_params=params(24),
        cost_estimate=pl.CostEstimate(
            flops=2000000000, transcendentals=0, bytes_accessed=4000000
        ),
        name="inner",
    )(
        gas,
        wide,
        column,
        solar,
        albedo,
        first,
        final,
        *parts[1],
        *parts[2],
        neighbours,
        side_weight,
    )


def edge_side_kernel(
    near_got,
    far_got,
    first_ref,
    final_ref,
    partial_ref,
    neighbour_ref,
    side_ref,
    full_ref,
    out_hbm,
    edge_ref,
    sems,
):
    def copy(source, lanes, i):
        return pltpu.make_async_copy(
            source.at[:, :, lanes], out_hbm.at[:, :, lanes], sems.at[i]
        )

    copies = [copy(full_ref, pl.ds(CB, COLS - 2 * CB), 0)]
    copies[0].start()
    even = lax.axis_index("blk") % 2 == 0
    near, far = rows_of(near_got), rows_of(far_got)
    edges = (
        (0, 0, lambda row: jnp.where(even, far(row), near(row)), first_ref),
        (NB - 1, 2, lambda row: jnp.where(even, near(row), far(row)), final_ref),
    )
    for i, (block, code, outer, own) in enumerate(edges):
        correct_rest(
            block,
            code,
            outer,
            rows_of(own),
            rows_of(partial_ref.at[i]),
            neighbour_ref,
            side_ref,
            put_levels(edge_ref, block),
        )
    for i, block in enumerate((0, NB - 1)):
        copies.append(copy(edge_ref, pl.ds(block * CB, CB), 1 + i))
        copies[-1].start()
    for started in copies:
        started.wait()


def edge_side(near_got, far_got, first, final, partial, neighbours, side_weight, full):
    return pl.pallas_call(
        edge_side_kernel,
        in_specs=[IN_VMEM] * 8,
        out_specs=IN_HBM,
        out_shape=shape((LEV + 1, 2, COLS)),
        scratch_shapes=[
            pltpu.VMEM((LEV + 1, 2, COLS), F32),
            pltpu.SemaphoreType.DMA((3,)),
        ],
        compiler_params=params(4),
        name="edge_side",
    )(near_got, far_got, first, final, partial, neighbours, side_weight, full)


def exchange(x, bit):
    count = lax.axis_size("blk")
    return lax.ppermute(x, "blk", [(i, i ^ bit) for i in range(count)])


def beyond(x):
    count, bands = lax.axis_size("blk"), lax.axis_size("grp")
    pairs = []
    for i in range(count):
        for band in range(bands):
            if i in (0, count - 1):
                pairs.append((i * bands + band, i * bands + (band ^ 4)))
            else:
                pairs.append((i * bands + band, (i + (1 if i % 2 else -1)) * bands + band))
    return lax.ppermute(x, ("blk", "grp"), pairs)


def local(
    gas_state,
    cos_zenith,
    daylit,
    fine_area,
    fine_albedo,
    parent_of,
    optics_weight,
    solar_weight,
    neighbours,
    side_weight,
):
    send, keep, gas, wide, column, solar, beside, weights = surface(
        parent_of,
        fine_area,
        fine_albedo,
        optics_weight,
        cos_zenith,
        daylit,
        solar_weight,
        neighbours,
        side_weight,
        gas_state,
    )
    parts = []
    for i, blocks in enumerate(WINDOWS):
        got = exchange(send, 1 << i)
        parts.append(down(blocks, gas, wide, column, solar, keep))
        if i < 2:
            send, keep = merge(keep, got, parts[-1][2])
    first, final, near, far, albedo = up(parts, keep, got, column)
    far_got = beyond(far)
    near_got = exchange(near, 1)
    full, partial = inner(
        gas, wide, column, solar, albedo, first, final, parts, beside, weights
    )
    done = edge_side(near_got, far_got, first, final, partial, beside, weights, full)
    return done.transpose(1, 0, 2)


def solution(mesh):
    both = ("grp", "blk")
    in_specs = (
        P(None, None, both),
        P(both),
        P(both),
        P(both),
        P(None, both),
        P(both),
        P(),
        P(),
        P(None, both),
        P(None, both),
    )
    return jax.shard_map(
        local, mesh=mesh, in_specs=in_specs, out_specs=P(None, None, both), check_vma=False
    )
```

```python
import jax
import jax.numpy as jnp
from jax import lax
from jax.experimental import pallas as pl
from jax.experimental.pallas import tpu as pltpu
from jax.sharding import PartitionSpec as P

F = 16
LEV = 32
CB = 128
G = 32
KIDS = 4
NB = 8
NBLK = 8
ROWS = 72
STEP = 8
FINE_BLOCKS = NB * KIDS
COLS = NB * CB

ASYM = 0.8
TAU_SCALE = 0.08
SSA_MAX = 0.98
LOG2E = 1.4426950408889634

SLOPE = 0.5 * (1.25 + 0.75 * ASYM)
UNIT = 0.5 * SLOPE * SSA_MAX
SHIFT = 1.0 / UNIT - 1.0
BETA = 0.375 * (1.0 - ASYM) / SLOPE
RATE = -2.0 * TAU_SCALE * UNIT
SCATTER = UNIT / (0.375 * (1.0 - ASYM))

F32 = jnp.float32
BF16 = jnp.bfloat16
IN_VMEM = pl.BlockSpec(memory_space=pltpu.VMEM)
IN_HBM = pl.BlockSpec(memory_space=pltpu.HBM)
UNREAD = pl.BlockSpec(memory_space=pl.ANY)


def params(mebibytes):
    return pltpu.CompilerParams(vmem_limit_bytes=mebibytes << 20)


def shape(dims, kind=F32):
    return jax.ShapeDtypeStruct(dims, kind)


def sum_tiles(x):
    return (x[0:8] + x[8:16]) + (x[16:24] + x[24:32])


def place_albedo(parent_ref, area_ref, albedo_ref, mine):
    sub = lax.broadcasted_iota(jnp.int32, (CB, CB), 0).astype(F32).astype(BF16)
    line = lax.broadcasted_iota(jnp.int32, (8, CB), 0)
    one, zero = jnp.ones((), BF16), jnp.zeros((), BF16)
    totals = [[], [], []]
    for group in range(0, FINE_BLOCKS, 8):
        rows = slice(group, group + 8)
        area = area_ref[rows, :]
        terms = [area, area * albedo_ref[0, rows, :], area * albedo_ref[1, rows, :]]
        pieces = []
        for term in terms:
            for _ in range(3):
                piece = term.astype(BF16).astype(F32)
                pieces.append(piece)
                term = term - piece
        column = (parent_ref[rows, :] & (CB - 1)).astype(F32).astype(BF16)
        hots, values = [], []
        for j in range(8):
            hots.append(
                jnp.where(jnp.broadcast_to(column[j : j + 1, :], (CB, CB)) == sub, one, zero)
            )
            values.append(
                jnp.concatenate([jnp.where(line == j, x, 0.0) for x in pieces], axis=0).astype(
                    BF16
                )
            )
        total = lax.dot_general(
            jnp.concatenate(values, axis=1),
            jnp.concatenate(hots, axis=1),
            (((1,), (1,)), ((), ())),
            preferred_element_type=F32,
        )
        for i in range(3):
            at = 24 * i
            totals[i].append(
                total[at : at + 8] + (total[at + 8 : at + 16] + total[at + 16 : at + 24])
            )
    area = jnp.concatenate(totals[0], axis=0)
    here = area > 0.0
    safe = jnp.where(here, area, 1.0)
    owner = (parent_ref[:, 0:1] >> 7) ^ (mine * NB)
    owner = owner ^ ((owner >> 1) & (2 * NB))
    slot = lax.broadcasted_iota(jnp.int32, (FINE_BLOCKS, NBLK * NB), 1)
    where_to = jnp.where(owner == slot, 1.0, 0.0).astype(BF16)
    placed = []
    for s in range(2):
        total = jnp.concatenate(totals[1 + s], axis=0)
        albedo = jnp.where(here, total / safe, 0.0).astype(BF16)
        placed.append(
            lax.dot_general(
                where_to, albedo, (((0,), (0,)), ((), ())), preferred_element_type=F32
            ).astype(BF16)
        )
    return placed


def spread_weights(weight_ref, wide_ref):
    row = lax.broadcasted_iota(jnp.int32, (F, F * STEP), 0)
    col = lax.broadcasted_iota(jnp.int32, (F, F * STEP), 1)
    spread = jnp.where(col // STEP == row, 1.0, 0.0).astype(BF16)
    depth = lax.broadcasted_iota(jnp.int32, (F, 2 * G), 1) < G
    scaled = weight_ref[...].astype(F32) * jnp.where(depth, LOG2E, 0.5)
    high = scaled.astype(BF16)
    low = (scaled - high.astype(F32)).astype(BF16)
    wide = jnp.concatenate(
        [
            lax.dot_general(x, spread, (((0,), (0,)), ((), ())), preferred_element_type=F32)
            for x in (high, low)
        ],
        axis=1,
    )
    level = lax.broadcasted_iota(jnp.int32, (2 * G, 2 * F * STEP), 1) % STEP
    for l in range(STEP):
        wide_ref[l * 2 * G : (l + 1) * 2 * G, :] = jnp.where(level == l, wide, 0.0).astype(BF16)


def column_constants(cosine, lit, column_ref):
    back = 0.5 * (1.0 - ASYM * cosine)
    rising = back * SCATTER
    column_ref[0] = -TAU_SCALE / cosine
    column_ref[1] = (1.0 - back) / back
    column_ref[2] = 1.0 / rising
    column_ref[3] = cosine
    column_ref[4] = lit * rising


WINDOWS = ((0,), (NB - 1, 1, 2), (3, 4))
LATE = (5, 6)


def surface_kernel(
    parent_hbm,
    area_hbm,
    albedo_hbm,
    weight_hbm,
    cosine_hbm,
    lit_hbm,
    solar_hbm,
    neighbour_hbm,
    side_hbm,
    gas_hbm,
    send_ref,
    keep_ref,
    gas_ref,
    wide_ref,
    column_ref,
    solar_ref,
    neighbour_ref,
    side_ref,
    parent_ref,
    area_ref,
    albedo_ref,
    weight_ref,
    cosine_ref,
    lit_ref,
    sun_ref,
    sems,
):
    pairs = (
        (parent_hbm, parent_ref),
        (area_hbm, area_ref),
        (albedo_hbm.at[:, 0, :], albedo_ref.at[0]),
        (albedo_hbm.at[:, 1, :], albedo_ref.at[1]),
        (weight_hbm, weight_ref),
        (cosine_hbm, cosine_ref),
        (lit_hbm, lit_ref),
        (solar_hbm, sun_ref),
        (neighbour_hbm, neighbour_ref),
        (side_hbm, side_ref),
        (gas_hbm, gas_ref),
    )
    copies = [
        pltpu.make_async_copy(source, target, sems.at[i])
        for i, (source, target) in enumerate(pairs)
    ]
    for copy in copies:
        copy.start()
    for copy in copies[:8]:
        copy.wait()
    mine = lax.axis_index("blk")
    placed = place_albedo(parent_ref, area_ref, albedo_ref, mine)
    for s in range(2):
        for i in range(NBLK // 2):
            keep_ref[i, s] = placed[s][2 * i * NB : (2 * i + 1) * NB]
            send_ref[i, s] = placed[s][(2 * i + 1) * NB : (2 * i + 2) * NB]
    spread_weights(weight_ref, wide_ref)
    column_constants(cosine_ref[...].astype(F32), lit_ref[...].astype(F32), column_ref)
    row = lax.broadcasted_iota(jnp.int32, (G, G), 0)
    col = lax.broadcasted_iota(jnp.int32, (G, G), 1)
    sun = jnp.sum(jnp.where(row == col, sun_ref[...], 0.0), axis=1, keepdims=True)
    solar_ref[...] = jnp.broadcast_to(sun, (G, CB))
    for copy in copies[8:]:
        copy.wait()


def surface(
    parent_of,
    fine_area,
    fine_albedo,
    optics_weight,
    cos_zenith,
    daylit,
    solar_weight,
    neighbours,
    side_weight,
    gas_state,
):
    return pl.pallas_call(
        surface_kernel,
        in_specs=[IN_HBM] * 10,
        out_specs=[IN_VMEM] * 8,
        out_shape=[
            shape((NBLK // 2, 2, NB, CB), BF16),
            shape((NBLK // 2, 2, NB, CB), BF16),
            shape((F, LEV, COLS), BF16),
            shape((2 * G * STEP, 2 * F * STEP), BF16),
            shape((5, NB, CB)),
            shape((G, CB)),
            shape((3, COLS), jnp.int32),
            shape((3, COLS)),
        ],
        scratch_shapes=[
            pltpu.VMEM((FINE_BLOCKS, CB), jnp.int32),
            pltpu.VMEM((FINE_BLOCKS, CB), F32),
            pltpu.VMEM((2, FINE_BLOCKS, CB), F32),
            pltpu.VMEM((F, 2 * G), BF16),
            pltpu.VMEM((NB, CB), BF16),
            pltpu.VMEM((NB, CB), jnp.int32),
            pltpu.VMEM((1, G), F32),
            pltpu.SemaphoreType.DMA((11,)),
        ],
        compiler_params=params(4),
        name="surface",
    )(
        *[
            pltpu.with_memory_space_constraint(x, pltpu.HBM)
            for x in (
                parent_of.reshape(FINE_BLOCKS, CB),
                fine_area.reshape(FINE_BLOCKS, CB),
                fine_albedo.reshape(2, FINE_BLOCKS, CB).transpose(1, 0, 2),
                optics_weight.T,
                cos_zenith.reshape(NB, CB),
                daylit.reshape(NB, CB),
                solar_weight.reshape(1, G),
                neighbours,
                side_weight,
                gas_state,
            )
        ]
    )


def merge_kernel(keep_ref, got_ref, after_ref, send_ref, next_ref):
    del after_ref
    for i in range(keep_ref.shape[0]):
        total = (keep_ref[i].astype(F32) + got_ref[i].astype(F32)).astype(BF16)
        target = send_ref if i % 2 else next_ref
        target[i // 2] = total


def merge(keep, got, after):
    half = shape((keep.shape[0] // 2,) + keep.shape[1:], BF16)
    return pl.pallas_call(
        merge_kernel,
        in_specs=[IN_VMEM, IN_VMEM, UNREAD],
        out_specs=[IN_VMEM] * 2,
        out_shape=[half, half],
        compiler_params=params(2),
        name="merge",
    )(keep, got, after)


def layer_terms(depth_mix, albedo_mix, slant_rate):
    soft = jnp.maximum(depth_mix, jnp.log2(1.0 + jnp.exp2(jnp.minimum(depth_mix, 60.0))))
    e_dir = jnp.exp2(soft * slant_rate)
    bend = jnp.tanh(albedo_mix)
    gamma_one = SHIFT - bend
    gamma_two = BETA * bend + BETA
    product = (gamma_one - gamma_two) * (gamma_one + gamma_two)
    root = product * lax.rsqrt(product)
    damping = jnp.exp2(RATE * (root * soft))
    damped_sq = damping * damping
    lost = 1.0 - damped_sq
    even = root + root * damped_sq
    odd = gamma_one * lost
    transmit = (root + root) * damping
    return e_dir, gamma_two, even + odd, even - odd, gamma_two * lost, transmit


def mix_all(gas_ref, lanes, wide_ref):
    products = []
    for step in range(LEV // STEP):
        gas = gas_ref[:, step * STEP : (step + 1) * STEP, lanes].reshape(F * STEP, CB)
        products.append(
            jnp.dot(
                wide_ref[...],
                jnp.concatenate([gas, gas], axis=0),
                preferred_element_type=F32,
            )
        )
    return products


def eliminate(block, gas_ref, wide_ref, column_ref, solar_ref, coef_ref, esum_ref, state_ref):
    products = mix_all(gas_ref, slice(block * CB, (block + 1) * CB), wide_ref)
    slant_rate, falling, scale, cosine = [
        column_ref[i, block : block + 1, :] for i in range(4)
    ]
    direct = solar_ref[...] * cosine
    above = jnp.zeros((G, CB), F32)
    source = jnp.zeros((G, CB), F32)
    for l in range(LEV):
        at = (l % STEP) * 2 * G
        mix = products[l // STEP]
        e_dir, gamma_two, divisor, mirrored, reflect, transmit = layer_terms(
            mix[at : at + G], mix[at + G : at + 2 * G], slant_rate
        )
        esum_ref[l] = sum_tiles(direct) * scale + sum_tiles(source)
        below = direct * e_dir
        scattered = gamma_two * (direct - below)
        inverse = pl.reciprocal(divisor - above * reflect, approx=False)
        incident = (source + above * scattered) * inverse
        coef_ref[l, 0] = above
        coef_ref[l, 1] = transmit * inverse
        coef_ref[l, 2] = scattered + reflect * incident
        source = scattered * falling + transmit * incident
        above = (reflect + above * mirrored) * inverse
        direct = below
    esum_ref[LEV] = sum_tiles(direct) * scale + sum_tiles(source)
    state_ref[0] = above
    state_ref[1] = source
    state_ref[2] = direct * scale


def add_sublanes(rows):
    sub = lax.broadcasted_iota(jnp.int32, (8, CB), 0)
    four, two, one = sub < 4, (sub & 2) == 0, (sub & 1) == 0
    rows = [
        jnp.where(four, rows[r], rows[r + 4])
        + pltpu.roll(jnp.where(four, rows[r + 4], rows[r]), 4, 0)
        for r in range(4)
    ]
    rows = [
        jnp.where(
            two,
            rows[r] + pltpu.roll(rows[r], 6, 0),
            rows[r + 2] + pltpu.roll(rows[r + 2], 2, 0),
        )
        for r in range(2)
    ]
    return jnp.where(
        one, rows[0] + pltpu.roll(rows[0], 7, 0), rows[1] + pltpu.roll(rows[1], 1, 0)
    )


def substitute(coef_ref, esum_ref, state_ref, albedo_direct, albedo_diffuse, lit, flux_ref):
    above, source, direct = state_ref[0], state_ref[1], state_ref[2]
    upward = (albedo_diffuse * source + albedo_direct * direct) * pl.reciprocal(
        1.0 - albedo_diffuse * above, approx=False
    )
    none = jnp.zeros((8, CB), F32)
    pending = [esum_ref[LEV] + sum_tiles(above * upward), sum_tiles(upward)] + [none] * 6
    flux_ref[2 * LEV : 2 * LEV + 8, :] = add_sublanes(pending) * lit
    pending = []
    for l in range(LEV - 1, -1, -1):
        upward = coef_ref[l, 1] * upward + coef_ref[l, 2]
        pending = [
            esum_ref[l] + sum_tiles(coef_ref[l, 0] * upward),
            sum_tiles(upward),
        ] + pending
        if l % 4 == 0:
            flux_ref[2 * l : 2 * l + 8, :] = add_sublanes(pending) * lit
            pending = []


COEF = (LEV, 3, G, CB)
ESUM = (LEV + 1, 8, CB)
STATE = (3, G, CB)


def down_kernel(blocks):
    def kernel(gas_ref, wide_ref, column_ref, solar_ref, after_ref, coef_ref, esum_ref, state_ref):
        del after_ref
        for i, block in enumerate(blocks):
            eliminate(
                block,
                gas_ref,
                wide_ref,
                column_ref,
                solar_ref,
                coef_ref.at[i],
                esum_ref.at[i],
                state_ref.at[i],
            )

    return kernel


def down(blocks, gas, wide, column, solar, after):
    count = len(blocks)
    return pl.pallas_call(
        down_kernel(blocks),
        in_specs=[IN_VMEM] * 4 + [UNREAD],
        out_specs=[IN_VMEM] * 3,
        out_shape=[shape((count,) + x) for x in (COEF, ESUM, STATE)],
        compiler_params=params(24),
        cost_estimate=pl.CostEstimate(
            flops=200000000 * count, transcendentals=0, bytes_accessed=4000000
        ),
        name="down",
    )(gas, wide, column, solar, after)


def ground(albedo_ref, column_ref, block):
    row = slice(block, block + 1)
    return albedo_ref[0, row, :], albedo_ref[1, row, :], column_ref[4, row, :]


def up_kernel(
    coef_a,
    esum_a,
    state_a,
    coef_b,
    esum_b,
    state_b,
    keep_ref,
    got_ref,
    column_ref,
    first_ref,
    final_ref,
    near_ref,
    far_ref,
    albedo_ref,
):
    for s in range(2):
        albedo_ref[s] = keep_ref[0, s].astype(F32) + got_ref[0, s].astype(F32)
    substitute(
        coef_a.at[0], esum_a.at[0], state_a.at[0], *ground(albedo_ref, column_ref, 0), first_ref
    )
    substitute(
        coef_b.at[0],
        esum_b.at[0],
        state_b.at[0],
        *ground(albedo_ref, column_ref, NB - 1),
        final_ref,
    )
    even = lax.axis_index("blk") % 2 == 0
    near_ref[...] = jnp.where(even, final_ref[...], first_ref[...])
    far_ref[...] = jnp.where(even, first_ref[...], final_ref[...])


def up(parts, keep, got, column):
    return pl.pallas_call(
        up_kernel,
        in_specs=[IN_VMEM] * 9,
        out_specs=[IN_VMEM] * 5,
        out_shape=[shape((ROWS, CB))] * 4 + [shape((2, NB, CB))],
        compiler_params=params(2),
        cost_estimate=pl.CostEstimate(flops=4000000, transcendentals=0, bytes_accessed=4000000),
        name="up",
    )(*parts[0], *parts[1], keep, got, column)


def neighbour_rows(block, neighbour_ref, side_ref):
    lanes = slice(block * CB, (block + 1) * CB)
    at_lane, places, weights = [], [], []
    for k in range(3):
        at = jnp.broadcast_to(neighbour_ref[k : k + 1, lanes], (8, CB))
        places.append(((at >> 7) - block + 1) & (NB - 1))
        at_lane.append(at & (CB - 1))
        weights.append(jnp.broadcast_to(side_ref[k : k + 1, lanes], (8, CB)))
    return at_lane, places, weights


def pick(x, at_lane):
    return jnp.take_along_axis(x, at_lane, axis=1, mode="promise_in_bounds")


def correct(block, before, own, after, neighbour_ref, side_ref, put):
    at_lane, places, weights = neighbour_rows(block, neighbour_ref, side_ref)
    for k in range(3):
        for code, part in ((0, before), (2, after)):
            if part is None:
                weights[k] = jnp.where(places[k] == code, 0.0, weights[k])
    totals = {row: own(row) for row in range(0, ROWS, 8)}
    for k in range(3):
        for row in totals:
            here = own(row)
            beside = pick(here, at_lane[k])
            for code, part in ((0, before), (2, after)):
                if part is not None:
                    beside = jnp.where(places[k] == code, pick(part(row), at_lane[k]), beside)
            totals[row] = totals[row] + weights[k] * (beside - here)
    for row, total in totals.items():
        put(row, total)


def correct_rest(block, code, outer, own, partial, neighbour_ref, side_ref, put):
    at_lane, places, weights = neighbour_rows(block, neighbour_ref, side_ref)
    weights = [jnp.where(places[k] == code, weights[k], 0.0) for k in range(3)]
    totals = {row: partial(row) for row in range(0, ROWS, 8)}
    for k in range(3):
        for row in totals:
            beside = pick(outer(row), at_lane[k])
            totals[row] = totals[row] + weights[k] * (beside - own(row))
    for row, total in totals.items():
        put(row, total)


def put_levels(out_ref, block):
    lanes = slice(block * CB, (block + 1) * CB)

    def put(row, total):
        for l in range(row // 2, min(row // 2 + 4, LEV + 1)):
            out_ref[l, :, lanes] = total[2 * l - row : 2 * l - row + 2]

    return put


def rows_of(ref):
    return lambda row: ref[row : row + 8, :]


def inner_kernel(
    gas_ref,
    wide_ref,
    column_ref,
    solar_ref,
    albedo_ref,
    first_ref,
    final_ref,
    coef_b,
    esum_b,
    state_b,
    coef_c,
    esum_c,
    state_c,
    neighbour_ref,
    side_ref,
    out_ref,
    partial_ref,
    coef_ref,
    esum_ref,
    state_ref,
    flux_ref,
):
    kept = {}
    for i, n in enumerate(WINDOWS[1]):
        kept[n] = coef_b.at[i], esum_b.at[i], state_b.at[i]
    for i, n in enumerate(WINDOWS[2]):
        kept[n] = coef_c.at[i], esum_c.at[i], state_c.at[i]
    for i, n in enumerate(LATE):
        kept[n] = coef_ref.at[i], esum_ref.at[i], state_ref.at[i]
    flux = {0: first_ref, NB - 1: final_ref}
    for n in range(1, NB - 1):
        flux[n] = flux_ref.at[n - 1]

    def finish(n):
        substitute(*kept[n], *ground(albedo_ref, column_ref, n), flux[n])

    def side(n):
        before, own, after = [
            rows_of(flux[n + i]) if n + i in flux else None for i in (-1, 0, 1)
        ]
        if n in (0, NB - 1):
            partial = partial_ref.at[n // (NB - 1)]

            def put(row, total):
                partial[row : row + 8, :] = total

        else:
            put = put_levels(out_ref, n)
        correct(n, before, own, after, neighbour_ref, side_ref, put)

    for n in LATE:
        eliminate(n, gas_ref, wide_ref, column_ref, solar_ref, *kept[n])
    for n in range(1, NB - 1):
        finish(n)
    for n in range(NB):
        side(n)


def inner(gas, wide, column, solar, albedo, first, final, parts, neighbours, side_weight):
    return pl.pallas_call(
        inner_kernel,
        in_specs=[IN_VMEM] * 15,
        out_specs=[IN_VMEM] * 2,
        out_shape=[shape((LEV + 1, 2, COLS)), shape((2, ROWS, CB))],
        scratch_shapes=[
            pltpu.VMEM((len(LATE),) + COEF, F32),
            pltpu.VMEM((len(LATE),) + ESUM, F32),
            pltpu.VMEM((len(LATE),) + STATE, F32),
            pltpu.VMEM((NB - 2, ROWS, CB), F32),
        ],
        compiler_params=params(24),
        cost_estimate=pl.CostEstimate(
            flops=2000000000, transcendentals=0, bytes_accessed=4000000
        ),
        name="inner",
    )(
        gas,
        wide,
        column,
        solar,
        albedo,
        first,
        final,
        *parts[1],
        *parts[2],
        neighbours,
        side_weight,
    )


def edge_side_kernel(
    near_got,
    far_got,
    first_ref,
    final_ref,
    partial_ref,
    neighbour_ref,
    side_ref,
    full_ref,
    out_hbm,
    edge_ref,
    sems,
):
    def copy(source, lanes, i):
        return pltpu.make_async_copy(
            source.at[:, :, lanes], out_hbm.at[:, :, lanes], sems.at[i]
        )

    copies = [copy(full_ref, pl.ds(CB, COLS - 2 * CB), 0)]
    copies[0].start()
    even = lax.axis_index("blk") % 2 == 0
    near, far = rows_of(near_got), rows_of(far_got)
    edges = (
        (0, 0, lambda row: jnp.where(even, far(row), near(row)), first_ref),
        (NB - 1, 2, lambda row: jnp.where(even, near(row), far(row)), final_ref),
    )
    for i, (block, code, outer, own) in enumerate(edges):
        correct_rest(
            block,
            code,
            outer,
            rows_of(own),
            rows_of(partial_ref.at[i]),
            neighbour_ref,
            side_ref,
            put_levels(edge_ref, block),
        )
    for i, block in enumerate((0, NB - 1)):
        copies.append(copy(edge_ref, pl.ds(block * CB, CB), 1 + i))
        copies[-1].start()
    for started in copies:
        started.wait()


def edge_side(near_got, far_got, first, final, partial, neighbours, side_weight, full):
    return pl.pallas_call(
        edge_side_kernel,
        in_specs=[IN_VMEM] * 8,
        out_specs=IN_HBM,
        out_shape=shape((LEV + 1, 2, COLS)),
        scratch_shapes=[
            pltpu.VMEM((LEV + 1, 2, COLS), F32),
            pltpu.SemaphoreType.DMA((3,)),
        ],
        compiler_params=params(4),
        name="edge_side",
    )(near_got, far_got, first, final, partial, neighbours, side_weight, full)


PARTNERS = (1, 2, 6)


def exchange(x, mask):
    count = lax.axis_size("blk")
    return lax.ppermute(x, "blk", [(i, i ^ mask) for i in range(count)])


def beyond(x):
    count, bands = lax.axis_size("blk"), lax.axis_size("grp")
    pairs = []
    for i in range(count):
        for band in range(bands):
            if i in (0, count - 1):
                pairs.append((i * bands + band, i * bands + (band ^ 4)))
            else:
                pairs.append((i * bands + band, (i + (1 if i % 2 else -1)) * bands + band))
    return lax.ppermute(x, ("blk", "grp"), pairs)


def local(
    gas_state,
    cos_zenith,
    daylit,
    fine_area,
    fine_albedo,
    parent_of,
    optics_weight,
    solar_weight,
    neighbours,
    side_weight,
):
    send, keep, gas, wide, column, solar, beside, weights = surface(
        parent_of,
        fine_area,
        fine_albedo,
        optics_weight,
        cos_zenith,
        daylit,
        solar_weight,
        neighbours,
        side_weight,
        gas_state,
    )
    parts = []
    for i, blocks in enumerate(WINDOWS):
        got = exchange(send, PARTNERS[i])
        parts.append(down(blocks, gas, wide, column, solar, keep))
        if i < 2:
            send, keep = merge(keep, got, parts[-1][2])
    first, final, near, far, albedo = up(parts, keep, got, column)
    far_got = beyond(far)
    near_got = exchange(near, 1)
    full, partial = inner(
        gas, wide, column, solar, albedo, first, final, parts, beside, weights
    )
    done = edge_side(near_got, far_got, first, final, partial, beside, weights, full)
    return done.transpose(1, 0, 2)


def solution(mesh):
    both = ("grp", "blk")
    in_specs = (
        P(None, None, both),
        P(both),
        P(both),
        P(both),
        P(None, both),
        P(both),
        P(),
        P(),
        P(None, both),
        P(None, both),
    )
    return jax.shard_map(
        local, mesh=mesh, in_specs=in_specs, out_specs=P(None, None, both), check_vma=False
    )
```

```python
import jax
import jax.numpy as jnp
from jax import lax
from jax.experimental import pallas as pl
from jax.experimental.pallas import tpu as pltpu
from jax.sharding import PartitionSpec as P

F = 16
LEV = 32
CB = 128
G = 32
KIDS = 4
NB = 8
NBLK = 8
ROWS = 72
STEP = 8
FINE_BLOCKS = NB * KIDS
COLS = NB * CB

ASYM = 0.8
TAU_SCALE = 0.08
SSA_MAX = 0.98
LOG2E = 1.4426950408889634

SLOPE = 0.5 * (1.25 + 0.75 * ASYM)
UNIT = 0.5 * SLOPE * SSA_MAX
SHIFT = 1.0 / UNIT - 1.0
BETA = 0.375 * (1.0 - ASYM) / SLOPE
RATE = -2.0 * TAU_SCALE * UNIT
SCATTER = UNIT / (0.375 * (1.0 - ASYM))

F32 = jnp.float32
BF16 = jnp.bfloat16
IN_VMEM = pl.BlockSpec(memory_space=pltpu.VMEM)
IN_HBM = pl.BlockSpec(memory_space=pltpu.HBM)
UNREAD = pl.BlockSpec(memory_space=pl.ANY)


def params(mebibytes):
    return pltpu.CompilerParams(vmem_limit_bytes=mebibytes << 20)


def shape(dims, kind=F32):
    return jax.ShapeDtypeStruct(dims, kind)


def sum_tiles(x):
    return (x[0:8] + x[8:16]) + (x[16:24] + x[24:32])


def place_albedo(parent_ref, area_ref, albedo_ref, mine):
    sub = lax.broadcasted_iota(jnp.int32, (CB, CB), 0).astype(F32).astype(BF16)
    line = lax.broadcasted_iota(jnp.int32, (8, CB), 0)
    one, zero = jnp.ones((), BF16), jnp.zeros((), BF16)
    totals = [[], [], []]
    for group in range(0, FINE_BLOCKS, 8):
        rows = slice(group, group + 8)
        area = area_ref[rows, :]
        terms = [area, area * albedo_ref[0, rows, :], area * albedo_ref[1, rows, :]]
        pieces = []
        for term in terms:
            for _ in range(3):
                piece = term.astype(BF16).astype(F32)
                pieces.append(piece)
                term = term - piece
        column = (parent_ref[rows, :] & (CB - 1)).astype(F32).astype(BF16)
        hots, values = [], []
        for j in range(8):
            hots.append(
                jnp.where(jnp.broadcast_to(column[j : j + 1, :], (CB, CB)) == sub, one, zero)
            )
            values.append(
                jnp.concatenate([jnp.where(line == j, x, 0.0) for x in pieces], axis=0).astype(
                    BF16
                )
            )
        total = lax.dot_general(
            jnp.concatenate(values, axis=1),
            jnp.concatenate(hots, axis=1),
            (((1,), (1,)), ((), ())),
            preferred_element_type=F32,
        )
        for i in range(3):
            at = 24 * i
            totals[i].append(
                total[at : at + 8] + (total[at + 8 : at + 16] + total[at + 16 : at + 24])
            )
    area = jnp.concatenate(totals[0], axis=0)
    here = area > 0.0
    safe = jnp.where(here, area, 1.0)
    owner = (parent_ref[:, 0:1] >> 7) ^ (mine * NB)
    owner = owner ^ ((owner >> 1) & (2 * NB))
    slot = lax.broadcasted_iota(jnp.int32, (FINE_BLOCKS, NBLK * NB), 1)
    where_to = jnp.where(owner == slot, 1.0, 0.0).astype(BF16)
    placed = []
    for s in range(2):
        total = jnp.concatenate(totals[1 + s], axis=0)
        albedo = jnp.where(here, total / safe, 0.0).astype(BF16)
        placed.append(
            lax.dot_general(
                where_to, albedo, (((0,), (0,)), ((), ())), preferred_element_type=F32
            ).astype(BF16)
        )
    return placed


def spread_weights(weight_ref, wide_ref):
    row = lax.broadcasted_iota(jnp.int32, (F, F * STEP), 0)
    col = lax.broadcasted_iota(jnp.int32, (F, F * STEP), 1)
    spread = jnp.where(col // STEP == row, 1.0, 0.0).astype(BF16)
    depth = lax.broadcasted_iota(jnp.int32, (F, 2 * G), 1) < G
    scaled = weight_ref[...].astype(F32) * jnp.where(depth, LOG2E, 0.5)
    high = scaled.astype(BF16)
    low = (scaled - high.astype(F32)).astype(BF16)
    wide = jnp.concatenate(
        [
            lax.dot_general(x, spread, (((0,), (0,)), ((), ())), preferred_element_type=F32)
            for x in (high, low)
        ],
        axis=1,
    )
    level = lax.broadcasted_iota(jnp.int32, (2 * G, 2 * F * STEP), 1) % STEP
    for l in range(STEP):
        wide_ref[l * 2 * G : (l + 1) * 2 * G, :] = jnp.where(level == l, wide, 0.0).astype(BF16)


def column_constants(cosine, lit, column_ref):
    back = 0.5 * (1.0 - ASYM * cosine)
    rising = back * SCATTER
    column_ref[0] = -TAU_SCALE / cosine
    column_ref[1] = (1.0 - back) / back
    column_ref[2] = 1.0 / rising
    column_ref[3] = cosine
    column_ref[4] = lit * rising


WINDOWS = ((0,), (NB - 1, 1, 2), (3, 4))
LATE = (5, 6)


def surface_kernel(
    parent_hbm,
    area_hbm,
    albedo_hbm,
    weight_hbm,
    cosine_hbm,
    lit_hbm,
    solar_hbm,
    neighbour_hbm,
    side_hbm,
    gas_hbm,
    send_ref,
    keep_ref,
    gas_ref,
    wide_ref,
    column_ref,
    solar_ref,
    neighbour_ref,
    side_ref,
    parent_ref,
    area_ref,
    albedo_ref,
    weight_ref,
    cosine_ref,
    lit_ref,
    sun_ref,
    sems,
):
    pairs = (
        (parent_hbm, parent_ref),
        (area_hbm, area_ref),
        (albedo_hbm.at[:, 0, :], albedo_ref.at[0]),
        (albedo_hbm.at[:, 1, :], albedo_ref.at[1]),
        (weight_hbm, weight_ref),
        (cosine_hbm, cosine_ref),
        (lit_hbm, lit_ref),
        (solar_hbm, sun_ref),
        (neighbour_hbm, neighbour_ref),
        (side_hbm, side_ref),
        (gas_hbm, gas_ref),
    )
    copies = [
        pltpu.make_async_copy(source, target, sems.at[i])
        for i, (source, target) in enumerate(pairs)
    ]
    for copy in copies:
        copy.start()
    for copy in copies[:8]:
        copy.wait()
    mine = lax.axis_index("blk")
    placed = place_albedo(parent_ref, area_ref, albedo_ref, mine)
    for s in range(2):
        for i in range(NBLK // 2):
            keep_ref[i, s] = placed[s][2 * i * NB : (2 * i + 1) * NB]
            send_ref[i, s] = placed[s][(2 * i + 1) * NB : (2 * i + 2) * NB]
    spread_weights(weight_ref, wide_ref)
    column_constants(cosine_ref[...].astype(F32), lit_ref[...].astype(F32), column_ref)
    row = lax.broadcasted_iota(jnp.int32, (G, G), 0)
    col = lax.broadcasted_iota(jnp.int32, (G, G), 1)
    sun = jnp.sum(jnp.where(row == col, sun_ref[...], 0.0), axis=1, keepdims=True)
    solar_ref[...] = jnp.broadcast_to(sun, (G, CB))
    for copy in copies[8:]:
        copy.wait()


def surface(
    parent_of,
    fine_area,
    fine_albedo,
    optics_weight,
    cos_zenith,
    daylit,
    solar_weight,
    neighbours,
    side_weight,
    gas_state,
):
    return pl.pallas_call(
        surface_kernel,
        in_specs=[IN_HBM] * 10,
        out_specs=[IN_VMEM] * 8,
        out_shape=[
            shape((NBLK // 2, 2, NB, CB), BF16),
            shape((NBLK // 2, 2, NB, CB), BF16),
            shape((F, LEV, COLS), BF16),
            shape((2 * G * STEP, 2 * F * STEP), BF16),
            shape((5, NB, CB)),
            shape((G, CB)),
            shape((3, COLS), jnp.int32),
            shape((3, COLS)),
        ],
        scratch_shapes=[
            pltpu.VMEM((FINE_BLOCKS, CB), jnp.int32),
            pltpu.VMEM((FINE_BLOCKS, CB), F32),
            pltpu.VMEM((2, FINE_BLOCKS, CB), F32),
            pltpu.VMEM((F, 2 * G), BF16),
            pltpu.VMEM((NB, CB), BF16),
            pltpu.VMEM((NB, CB), jnp.int32),
            pltpu.VMEM((1, G), F32),
            pltpu.SemaphoreType.DMA((11,)),
        ],
        compiler_params=params(4),
        name="surface",
    )(
        *[
            pltpu.with_memory_space_constraint(x, pltpu.HBM)
            for x in (
                parent_of.reshape(FINE_BLOCKS, CB),
                fine_area.reshape(FINE_BLOCKS, CB),
                fine_albedo.reshape(2, FINE_BLOCKS, CB).transpose(1, 0, 2),
                optics_weight.T,
                cos_zenith.reshape(NB, CB),
                daylit.reshape(NB, CB),
                solar_weight.reshape(1, G),
                neighbours,
                side_weight,
                gas_state,
            )
        ]
    )


def merge_kernel(keep_ref, got_ref, after_ref, send_ref, next_ref):
    del after_ref
    for i in range(keep_ref.shape[0]):
        total = (keep_ref[i].astype(F32) + got_ref[i].astype(F32)).astype(BF16)
        target = send_ref if i % 2 else next_ref
        target[i // 2] = total


def merge(keep, got, after):
    half = shape((keep.shape[0] // 2,) + keep.shape[1:], BF16)
    return pl.pallas_call(
        merge_kernel,
        in_specs=[IN_VMEM, IN_VMEM, UNREAD],
        out_specs=[IN_VMEM] * 2,
        out_shape=[half, half],
        compiler_params=params(2),
        name="merge",
    )(keep, got, after)


def layer_terms(depth_mix, albedo_mix, slant_rate):
    soft = jnp.maximum(depth_mix, jnp.log2(1.0 + jnp.exp2(jnp.minimum(depth_mix, 60.0))))
    e_dir = jnp.exp2(soft * slant_rate)
    bend = jnp.tanh(albedo_mix)
    gamma_one = SHIFT - bend
    gamma_two = BETA * bend + BETA
    product = (gamma_one - gamma_two) * (gamma_one + gamma_two)
    root = product * lax.rsqrt(product)
    damping = jnp.exp2(RATE * (root * soft))
    damped_sq = damping * damping
    lost = 1.0 - damped_sq
    even = root + root * damped_sq
    odd = gamma_one * lost
    transmit = (root + root) * damping
    return e_dir, gamma_two, even + odd, even - odd, gamma_two * lost, transmit


def mix_all(gas_ref, lanes, wide_ref):
    products = []
    for step in range(LEV // STEP):
        gas = gas_ref[:, step * STEP : (step + 1) * STEP, lanes].reshape(F * STEP, CB)
        products.append(
            jnp.dot(
                wide_ref[...],
                jnp.concatenate([gas, gas], axis=0),
                preferred_element_type=F32,
            )
        )
    return products


def eliminate(block, gas_ref, wide_ref, column_ref, solar_ref, coef_ref, esum_ref, state_ref):
    products = mix_all(gas_ref, slice(block * CB, (block + 1) * CB), wide_ref)
    slant_rate, falling, scale, cosine = [
        column_ref[i, block : block + 1, :] for i in range(4)
    ]
    direct = solar_ref[...] * cosine
    above = jnp.zeros((G, CB), F32)
    source = jnp.zeros((G, CB), F32)
    for l in range(LEV):
        at = (l % STEP) * 2 * G
        mix = products[l // STEP]
        e_dir, gamma_two, divisor, mirrored, reflect, transmit = layer_terms(
            mix[at : at + G], mix[at + G : at + 2 * G], slant_rate
        )
        esum_ref[l] = sum_tiles(direct) * scale + sum_tiles(source)
        below = direct * e_dir
        scattered = gamma_two * (direct - below)
        inverse = pl.reciprocal(divisor - above * reflect, approx=False)
        incident = (source + above * scattered) * inverse
        coef_ref[l, 0] = above
        coef_ref[l, 1] = transmit * inverse
        coef_ref[l, 2] = scattered + reflect * incident
        source = scattered * falling + transmit * incident
        above = (reflect + above * mirrored) * inverse
        direct = below
    esum_ref[LEV] = sum_tiles(direct) * scale + sum_tiles(source)
    state_ref[0] = above
    state_ref[1] = source
    state_ref[2] = direct * scale


def add_sublanes(rows):
    sub = lax.broadcasted_iota(jnp.int32, (8, CB), 0)
    four, two, one = sub < 4, (sub & 2) == 0, (sub & 1) == 0
    rows = [
        jnp.where(four, rows[r], rows[r + 4])
        + pltpu.roll(jnp.where(four, rows[r + 4], rows[r]), 4, 0)
        for r in range(4)
    ]
    rows = [
        jnp.where(
            two,
            rows[r] + pltpu.roll(rows[r], 6, 0),
            rows[r + 2] + pltpu.roll(rows[r + 2], 2, 0),
        )
        for r in range(2)
    ]
    return jnp.where(
        one, rows[0] + pltpu.roll(rows[0], 7, 0), rows[1] + pltpu.roll(rows[1], 1, 0)
    )


def substitute(coef_ref, esum_ref, state_ref, albedo_direct, albedo_diffuse, lit, flux_ref):
    above, source, direct = state_ref[0], state_ref[1], state_ref[2]
    upward = (albedo_diffuse * source + albedo_direct * direct) * pl.reciprocal(
        1.0 - albedo_diffuse * above, approx=False
    )
    none = jnp.zeros((8, CB), F32)
    pending = [esum_ref[LEV] + sum_tiles(above * upward), sum_tiles(upward)] + [none] * 6
    flux_ref[2 * LEV : 2 * LEV + 8, :] = add_sublanes(pending) * lit
    pending = []
    for l in range(LEV - 1, -1, -1):
        upward = coef_ref[l, 1] * upward + coef_ref[l, 2]
        pending = [
            esum_ref[l] + sum_tiles(coef_ref[l, 0] * upward),
            sum_tiles(upward),
        ] + pending
        if l % 4 == 0:
            flux_ref[2 * l : 2 * l + 8, :] = add_sublanes(pending) * lit
            pending = []


COEF = (LEV, 3, G, CB)
ESUM = (LEV + 1, 8, CB)
STATE = (3, G, CB)


def down_kernel(blocks):
    def kernel(gas_ref, wide_ref, column_ref, solar_ref, after_ref, coef_ref, esum_ref, state_ref):
        del after_ref
        for i, block in enumerate(blocks):
            eliminate(
                block,
                gas_ref,
                wide_ref,
                column_ref,
                solar_ref,
                coef_ref.at[i],
                esum_ref.at[i],
                state_ref.at[i],
            )

    return kernel


def down(blocks, gas, wide, column, solar, after):
    count = len(blocks)
    return pl.pallas_call(
        down_kernel(blocks),
        in_specs=[IN_VMEM] * 4 + [UNREAD],
        out_specs=[IN_VMEM] * 3,
        out_shape=[shape((count,) + x) for x in (COEF, ESUM, STATE)],
        compiler_params=params(24),
        cost_estimate=pl.CostEstimate(
            flops=200000000 * count, transcendentals=0, bytes_accessed=4000000
        ),
        name="down",
    )(gas, wide, column, solar, after)


def ground(albedo_ref, column_ref, block):
    row = slice(block, block + 1)
    return albedo_ref[0, row, :], albedo_ref[1, row, :], column_ref[4, row, :]


def up_kernel(
    coef_a,
    esum_a,
    state_a,
    coef_b,
    esum_b,
    state_b,
    keep_ref,
    got_ref,
    column_ref,
    first_ref,
    final_ref,
    near_ref,
    far_ref,
    albedo_ref,
):
    for s in range(2):
        albedo_ref[s] = keep_ref[0, s].astype(F32) + got_ref[0, s].astype(F32)
    substitute(
        coef_a.at[0], esum_a.at[0], state_a.at[0], *ground(albedo_ref, column_ref, 0), first_ref
    )
    substitute(
        coef_b.at[0],
        esum_b.at[0],
        state_b.at[0],
        *ground(albedo_ref, column_ref, NB - 1),
        final_ref,
    )
    even = lax.axis_index("blk") % 2 == 0
    near_ref[...] = jnp.where(even, final_ref[...], first_ref[...])
    far_ref[...] = jnp.where(even, first_ref[...], final_ref[...])


def up(parts, keep, got, column):
    return pl.pallas_call(
        up_kernel,
        in_specs=[IN_VMEM] * 9,
        out_specs=[IN_VMEM] * 5,
        out_shape=[shape((ROWS, CB))] * 4 + [shape((2, NB, CB))],
        compiler_params=params(2),
        cost_estimate=pl.CostEstimate(flops=4000000, transcendentals=0, bytes_accessed=4000000),
        name="up",
    )(*parts[0], *parts[1], keep, got, column)


def neighbour_rows(block, neighbour_ref, side_ref):
    lanes = slice(block * CB, (block + 1) * CB)
    at_lane, places, weights = [], [], []
    for k in range(3):
        at = jnp.broadcast_to(neighbour_ref[k : k + 1, lanes], (8, CB))
        places.append(((at >> 7) - block + 1) & (NB - 1))
        at_lane.append(at & (CB - 1))
        weights.append(jnp.broadcast_to(side_ref[k : k + 1, lanes], (8, CB)))
    return at_lane, places, weights


def pick(x, at_lane):
    return jnp.take_along_axis(x, at_lane, axis=1, mode="promise_in_bounds")


def correct(block, before, own, after, neighbour_ref, side_ref, put):
    at_lane, places, weights = neighbour_rows(block, neighbour_ref, side_ref)
    for k in range(3):
        for code, part in ((0, before), (2, after)):
            if part is None:
                weights[k] = jnp.where(places[k] == code, 0.0, weights[k])
    totals = {row: own(row) for row in range(0, ROWS, 8)}
    for k in range(3):
        for row in totals:
            here = own(row)
            beside = pick(here, at_lane[k])
            for code, part in ((0, before), (2, after)):
                if part is not None:
                    beside = jnp.where(places[k] == code, pick(part(row), at_lane[k]), beside)
            totals[row] = totals[row] + weights[k] * (beside - here)
    for row, total in totals.items():
        put(row, total)


def correct_rest(block, code, outer, own, partial, neighbour_ref, side_ref, put):
    at_lane, places, weights = neighbour_rows(block, neighbour_ref, side_ref)
    weights = [jnp.where(places[k] == code, weights[k], 0.0) for k in range(3)]
    totals = {row: partial(row) for row in range(0, ROWS, 8)}
    for k in range(3):
        for row in totals:
            beside = pick(outer(row), at_lane[k])
            totals[row] = totals[row] + weights[k] * (beside - own(row))
    for row, total in totals.items():
        put(row, total)


def put_levels(out_ref, block):
    lanes = slice(block * CB, (block + 1) * CB)

    def put(row, total):
        for l in range(row // 2, min(row // 2 + 4, LEV + 1)):
            out_ref[l, :, lanes] = total[2 * l - row : 2 * l - row + 2]

    return put


def rows_of(ref):
    return lambda row: ref[row : row + 8, :]


def inner_kernel(
    gas_ref,
    wide_ref,
    column_ref,
    solar_ref,
    albedo_ref,
    first_ref,
    final_ref,
    coef_b,
    esum_b,
    state_b,
    coef_c,
    esum_c,
    state_c,
    neighbour_ref,
    side_ref,
    out_ref,
    partial_ref,
    coef_ref,
    esum_ref,
    state_ref,
    flux_ref,
):
    kept = {}
    for i, n in enumerate(WINDOWS[1]):
        kept[n] = coef_b.at[i], esum_b.at[i], state_b.at[i]
    for i, n in enumerate(WINDOWS[2]):
        kept[n] = coef_c.at[i], esum_c.at[i], state_c.at[i]
    for i, n in enumerate(LATE):
        kept[n] = coef_ref.at[i], esum_ref.at[i], state_ref.at[i]
    flux = {0: first_ref, NB - 1: final_ref}
    for n in range(1, NB - 1):
        flux[n] = flux_ref.at[n - 1]

    def finish(n):
        substitute(*kept[n], *ground(albedo_ref, column_ref, n), flux[n])

    def side(n):
        before, own, after = [
            rows_of(flux[n + i]) if n + i in flux else None for i in (-1, 0, 1)
        ]
        if n in (0, NB - 1):
            partial = partial_ref.at[n // (NB - 1)]

            def put(row, total):
                partial[row : row + 8, :] = total

        else:
            put = put_levels(out_ref, n)
        correct(n, before, own, after, neighbour_ref, side_ref, put)

    for n in LATE:
        eliminate(n, gas_ref, wide_ref, column_ref, solar_ref, *kept[n])
    for n in range(1, NB - 1):
        finish(n)
    for n in range(NB):
        side(n)


def inner(gas, wide, column, solar, albedo, first, final, parts, neighbours, side_weight):
    return pl.pallas_call(
        inner_kernel,
        in_specs=[IN_VMEM] * 15,
        out_specs=[IN_VMEM] * 2,
        out_shape=[shape((LEV + 1, 2, COLS)), shape((2, ROWS, CB))],
        scratch_shapes=[
            pltpu.VMEM((len(LATE),) + COEF, F32),
            pltpu.VMEM((len(LATE),) + ESUM, F32),
            pltpu.VMEM((len(LATE),) + STATE, F32),
            pltpu.VMEM((NB - 2, ROWS, CB), F32),
        ],
        compiler_params=params(24),
        cost_estimate=pl.CostEstimate(
            flops=2000000000, transcendentals=0, bytes_accessed=4000000
        ),
        name="inner",
    )(
        gas,
        wide,
        column,
        solar,
        albedo,
        first,
        final,
        *parts[1],
        *parts[2],
        neighbours,
        side_weight,
    )


def edge_side_kernel(
    far_got,
    near_got,
    first_ref,
    final_ref,
    partial_ref,
    neighbour_ref,
    side_ref,
    full_ref,
    out_hbm,
    edge_ref,
    sems,
):
    def copy(source, lanes, i):
        return pltpu.make_async_copy(
            source.at[:, :, lanes], out_hbm.at[:, :, lanes], sems.at[i]
        )

    copies = [copy(full_ref, pl.ds(CB, COLS - 2 * CB), 0)]
    copies[0].start()
    even = lax.axis_index("blk") % 2 == 0
    near, far = rows_of(near_got), rows_of(far_got)
    edges = (
        (0, 0, lambda row: jnp.where(even, far(row), near(row)), first_ref),
        (NB - 1, 2, lambda row: jnp.where(even, near(row), far(row)), final_ref),
    )
    for i, (block, code, outer, own) in enumerate(edges):
        correct_rest(
            block,
            code,
            outer,
            rows_of(own),
            rows_of(partial_ref.at[i]),
            neighbour_ref,
            side_ref,
            put_levels(edge_ref, block),
        )
    for i, block in enumerate((0, NB - 1)):
        copies.append(copy(edge_ref, pl.ds(block * CB, CB), 1 + i))
        copies[-1].start()
    for started in copies:
        started.wait()


def edge_side(far_got, near_got, first, final, partial, neighbours, side_weight, full):
    return pl.pallas_call(
        edge_side_kernel,
        in_specs=[IN_VMEM] * 8,
        out_specs=IN_HBM,
        out_shape=shape((LEV + 1, 2, COLS)),
        scratch_shapes=[
            pltpu.VMEM((LEV + 1, 2, COLS), F32),
            pltpu.SemaphoreType.DMA((3,)),
        ],
        compiler_params=params(4),
        name="edge_side",
    )(far_got, near_got, first, final, partial, neighbours, side_weight, full)


PARTNERS = (1, 2, 6)


def exchange(x, mask):
    count = lax.axis_size("blk")
    return lax.ppermute(x, "blk", [(i, i ^ mask) for i in range(count)])


def beyond(x):
    count = lax.axis_size("blk")
    pairs = [(i, (i + (1 if i % 2 else -1)) % count) for i in range(count)]
    return lax.ppermute(x, "blk", pairs)


def local(
    gas_state,
    cos_zenith,
    daylit,
    fine_area,
    fine_albedo,
    parent_of,
    optics_weight,
    solar_weight,
    neighbours,
    side_weight,
):
    send, keep, gas, wide, column, solar, beside, weights = surface(
        parent_of,
        fine_area,
        fine_albedo,
        optics_weight,
        cos_zenith,
        daylit,
        solar_weight,
        neighbours,
        side_weight,
        gas_state,
    )
    parts = []
    for i, blocks in enumerate(WINDOWS):
        got = exchange(send, PARTNERS[i])
        parts.append(down(blocks, gas, wide, column, solar, keep))
        if i < 2:
            send, keep = merge(keep, got, parts[-1][2])
    first, final, near, far, albedo = up(parts, keep, got, column)
    far_got = beyond(far)
    near_got = exchange(near, 1)
    full, partial = inner(
        gas, wide, column, solar, albedo, first, final, parts, beside, weights
    )
    done = edge_side(far_got, near_got, first, final, partial, beside, weights, full)
    return done.transpose(1, 0, 2)


def solution(mesh):
    both = ("grp", "blk")
    in_specs = (
        P(None, None, both),
        P(both),
        P(both),
        P(both),
        P(None, both),
        P(both),
        P(),
        P(),
        P(None, both),
        P(None, both),
    )
    return jax.shard_map(
        local, mesh=mesh, in_specs=in_specs, out_specs=P(None, None, both), check_vma=False
    )
```

```python
import jax
import jax.numpy as jnp
from jax import lax
from jax.experimental import pallas as pl
from jax.experimental.pallas import tpu as pltpu
from jax.sharding import PartitionSpec as P

F = 16
LEV = 32
CB = 128
G = 32
KIDS = 4
NB = 8
NBLK = 8
ROWS = 72
STEP = 8
FINE_BLOCKS = NB * KIDS
COLS = NB * CB

ASYM = 0.8
TAU_SCALE = 0.08
SSA_MAX = 0.98
LOG2E = 1.4426950408889634

SLOPE = 0.5 * (1.25 + 0.75 * ASYM)
UNIT = 0.5 * SLOPE * SSA_MAX
SHIFT = 1.0 / UNIT - 1.0
BETA = 0.375 * (1.0 - ASYM) / SLOPE
RATE = -2.0 * TAU_SCALE * UNIT
SCATTER = UNIT / (0.375 * (1.0 - ASYM))

F32 = jnp.float32
BF16 = jnp.bfloat16
IN_VMEM = pl.BlockSpec(memory_space=pltpu.VMEM)
IN_HBM = pl.BlockSpec(memory_space=pltpu.HBM)
UNREAD = pl.BlockSpec(memory_space=pl.ANY)


def params(mebibytes):
    return pltpu.CompilerParams(vmem_limit_bytes=mebibytes << 20)


def shape(dims, kind=F32):
    return jax.ShapeDtypeStruct(dims, kind)


def sum_tiles(x):
    return (x[0:8] + x[8:16]) + (x[16:24] + x[24:32])


def place_albedo(parent_ref, area_ref, albedo_ref, mine):
    sub = lax.broadcasted_iota(jnp.int32, (CB, CB), 0).astype(F32).astype(BF16)
    line = lax.broadcasted_iota(jnp.int32, (8, CB), 0)
    one, zero = jnp.ones((), BF16), jnp.zeros((), BF16)
    totals = [[], [], []]
    for group in range(0, FINE_BLOCKS, 8):
        rows = slice(group, group + 8)
        area = area_ref[rows, :]
        terms = [area, area * albedo_ref[0, rows, :], area * albedo_ref[1, rows, :]]
        pieces = []
        for term in terms:
            for _ in range(3):
                piece = term.astype(BF16).astype(F32)
                pieces.append(piece)
                term = term - piece
        column = (parent_ref[rows, :] & (CB - 1)).astype(F32).astype(BF16)
        hots, values = [], []
        for j in range(8):
            hots.append(
                jnp.where(jnp.broadcast_to(column[j : j + 1, :], (CB, CB)) == sub, one, zero)
            )
            values.append(
                jnp.concatenate([jnp.where(line == j, x, 0.0) for x in pieces], axis=0).astype(
                    BF16
                )
            )
        total = lax.dot_general(
            jnp.concatenate(values, axis=1),
            jnp.concatenate(hots, axis=1),
            (((1,), (1,)), ((), ())),
            preferred_element_type=F32,
        )
        for i in range(3):
            at = 24 * i
            totals[i].append(
                total[at : at + 8] + (total[at + 8 : at + 16] + total[at + 16 : at + 24])
            )
    area = jnp.concatenate(totals[0], axis=0)
    here = area > 0.0
    safe = jnp.where(here, area, 1.0)
    owner = (parent_ref[:, 0:1] >> 7) ^ (mine * NB)
    owner = owner ^ ((owner >> 1) & (2 * NB))
    slot = lax.broadcasted_iota(jnp.int32, (FINE_BLOCKS, NBLK * NB), 1)
    where_to = jnp.where(owner == slot, 1.0, 0.0).astype(BF16)
    placed = []
    for s in range(2):
        total = jnp.concatenate(totals[1 + s], axis=0)
        albedo = jnp.where(here, total / safe, 0.0).astype(BF16)
        placed.append(
            lax.dot_general(
                where_to, albedo, (((0,), (0,)), ((), ())), preferred_element_type=F32
            ).astype(BF16)
        )
    return placed


def spread_weights(weight_ref, wide_ref):
    row = lax.broadcasted_iota(jnp.int32, (F, F * STEP), 0)
    col = lax.broadcasted_iota(jnp.int32, (F, F * STEP), 1)
    spread = jnp.where(col // STEP == row, 1.0, 0.0).astype(BF16)
    depth = lax.broadcasted_iota(jnp.int32, (F, 2 * G), 1) < G
    scaled = weight_ref[...].astype(F32) * jnp.where(depth, LOG2E, 0.5)
    high = scaled.astype(BF16)
    low = (scaled - high.astype(F32)).astype(BF16)
    wide = jnp.concatenate(
        [
            lax.dot_general(x, spread, (((0,), (0,)), ((), ())), preferred_element_type=F32)
            for x in (high, low)
        ],
        axis=1,
    )
    level = lax.broadcasted_iota(jnp.int32, (2 * G, 2 * F * STEP), 1) % STEP
    for l in range(STEP):
        wide_ref[l * 2 * G : (l + 1) * 2 * G, :] = jnp.where(level == l, wide, 0.0).astype(BF16)


def column_constants(cosine, lit, column_ref):
    back = 0.5 * (1.0 - ASYM * cosine)
    rising = back * SCATTER
    column_ref[0] = -TAU_SCALE / cosine
    column_ref[1] = (1.0 - back) / back
    column_ref[2] = 1.0 / rising
    column_ref[3] = cosine
    column_ref[4] = lit * rising


WINDOWS = ((0,), (NB - 1, 1, 2), (3, 4))
LATE = (5, 6)


def surface_kernel(
    parent_hbm,
    area_hbm,
    albedo_hbm,
    weight_hbm,
    cosine_hbm,
    lit_hbm,
    solar_hbm,
    neighbour_hbm,
    side_hbm,
    gas_hbm,
    send_ref,
    keep_ref,
    gas_ref,
    wide_ref,
    column_ref,
    solar_ref,
    neighbour_ref,
    side_ref,
    parent_ref,
    area_ref,
    albedo_ref,
    weight_ref,
    cosine_ref,
    lit_ref,
    sun_ref,
    sems,
):
    pairs = (
        (parent_hbm, parent_ref),
        (area_hbm, area_ref),
        (albedo_hbm.at[:, 0, :], albedo_ref.at[0]),
        (albedo_hbm.at[:, 1, :], albedo_ref.at[1]),
        (weight_hbm, weight_ref),
        (cosine_hbm, cosine_ref),
        (lit_hbm, lit_ref),
        (solar_hbm, sun_ref),
        (neighbour_hbm, neighbour_ref),
        (side_hbm, side_ref),
        (gas_hbm, gas_ref),
    )
    copies = [
        pltpu.make_async_copy(source, target, sems.at[i])
        for i, (source, target) in enumerate(pairs)
    ]
    for copy in copies:
        copy.start()
    for copy in copies[:8]:
        copy.wait()
    mine = lax.axis_index("blk")
    placed = place_albedo(parent_ref, area_ref, albedo_ref, mine)
    for s in range(2):
        for i in range(NBLK // 2):
            keep_ref[i, s] = placed[s][2 * i * NB : (2 * i + 1) * NB]
            send_ref[i, s] = placed[s][(2 * i + 1) * NB : (2 * i + 2) * NB]
    spread_weights(weight_ref, wide_ref)
    column_constants(cosine_ref[...].astype(F32), lit_ref[...].astype(F32), column_ref)
    row = lax.broadcasted_iota(jnp.int32, (G, G), 0)
    col = lax.broadcasted_iota(jnp.int32, (G, G), 1)
    sun = jnp.sum(jnp.where(row == col, sun_ref[...], 0.0), axis=1, keepdims=True)
    solar_ref[...] = jnp.broadcast_to(sun, (G, CB))
    for copy in copies[8:]:
        copy.wait()


def surface(
    parent_of,
    fine_area,
    fine_albedo,
    optics_weight,
    cos_zenith,
    daylit,
    solar_weight,
    neighbours,
    side_weight,
    gas_state,
):
    return pl.pallas_call(
        surface_kernel,
        in_specs=[IN_HBM] * 10,
        out_specs=[IN_VMEM] * 8,
        out_shape=[
            shape((NBLK // 2, 2, NB, CB), BF16),
            shape((NBLK // 2, 2, NB, CB), BF16),
            shape((F, LEV, COLS), BF16),
            shape((2 * G * STEP, 2 * F * STEP), BF16),
            shape((5, NB, CB)),
            shape((G, CB)),
            shape((3, COLS), jnp.int32),
            shape((3, COLS)),
        ],
        scratch_shapes=[
            pltpu.VMEM((FINE_BLOCKS, CB), jnp.int32),
            pltpu.VMEM((FINE_BLOCKS, CB), F32),
            pltpu.VMEM((2, FINE_BLOCKS, CB), F32),
            pltpu.VMEM((F, 2 * G), BF16),
            pltpu.VMEM((NB, CB), BF16),
            pltpu.VMEM((NB, CB), jnp.int32),
            pltpu.VMEM((1, G), F32),
            pltpu.SemaphoreType.DMA((11,)),
        ],
        compiler_params=params(4),
        name="surface",
    )(
        *[
            pltpu.with_memory_space_constraint(x, pltpu.HBM)
            for x in (
                parent_of.reshape(FINE_BLOCKS, CB),
                fine_area.reshape(FINE_BLOCKS, CB),
                fine_albedo.reshape(2, FINE_BLOCKS, CB).transpose(1, 0, 2),
                optics_weight.T,
                cos_zenith.reshape(NB, CB),
                daylit.reshape(NB, CB),
                solar_weight.reshape(1, G),
                neighbours,
                side_weight,
                gas_state,
            )
        ]
    )


def merge_kernel(keep_ref, got_ref, after_ref, send_ref, next_ref):
    del after_ref
    for i in range(keep_ref.shape[0]):
        total = (keep_ref[i].astype(F32) + got_ref[i].astype(F32)).astype(BF16)
        target = send_ref if i % 2 else next_ref
        target[i // 2] = total


def merge(keep, got, after):
    half = shape((keep.shape[0] // 2,) + keep.shape[1:], BF16)
    return pl.pallas_call(
        merge_kernel,
        in_specs=[IN_VMEM, IN_VMEM, UNREAD],
        out_specs=[IN_VMEM] * 2,
        out_shape=[half, half],
        compiler_params=params(2),
        name="merge",
    )(keep, got, after)


def layer_terms(depth_mix, albedo_mix, slant_rate):
    soft = jnp.maximum(depth_mix, jnp.log2(1.0 + jnp.exp2(jnp.minimum(depth_mix, 60.0))))
    e_dir = jnp.exp2(soft * slant_rate)
    bend = jnp.tanh(albedo_mix)
    gamma_one = SHIFT - bend
    gamma_two = BETA * bend + BETA
    product = (gamma_one - gamma_two) * (gamma_one + gamma_two)
    root = product * lax.rsqrt(product)
    damping = jnp.exp2(RATE * (root * soft))
    damped_sq = damping * damping
    lost = 1.0 - damped_sq
    even = root + root * damped_sq
    odd = gamma_one * lost
    transmit = (root + root) * damping
    return e_dir, gamma_two, even + odd, even - odd, gamma_two * lost, transmit


def mix_step(gas_ref, block, step, wide_ref):
    lanes = slice(block * CB, (block + 1) * CB)
    gas = gas_ref[:, step * STEP : (step + 1) * STEP, lanes].reshape(F * STEP, CB)
    return jnp.dot(
        wide_ref[...], jnp.concatenate([gas, gas], axis=0), preferred_element_type=F32
    )


def eliminate(
    block, gas_ref, wide_ref, column_ref, solar_ref, coef_ref, esum_ref, state_ref, first_mix=None
):
    products = [
        mix_step(gas_ref, block, step, wide_ref) if step or first_mix is None else first_mix
        for step in range(LEV // STEP)
    ]
    slant_rate, falling, scale, cosine = [
        column_ref[i, block : block + 1, :] for i in range(4)
    ]
    direct = solar_ref[...] * cosine
    above = jnp.zeros((G, CB), F32)
    source = jnp.zeros((G, CB), F32)
    for l in range(LEV):
        at = (l % STEP) * 2 * G
        mix = products[l // STEP]
        e_dir, gamma_two, divisor, mirrored, reflect, transmit = layer_terms(
            mix[at : at + G], mix[at + G : at + 2 * G], slant_rate
        )
        esum_ref[l] = sum_tiles(direct) * scale + sum_tiles(source)
        below = direct * e_dir
        scattered = gamma_two * (direct - below)
        inverse = pl.reciprocal(divisor - above * reflect, approx=False)
        incident = (source + above * scattered) * inverse
        coef_ref[l, 0] = above
        coef_ref[l, 1] = transmit * inverse
        coef_ref[l, 2] = scattered + reflect * incident
        source = scattered * falling + transmit * incident
        above = (reflect + above * mirrored) * inverse
        direct = below
    esum_ref[LEV] = sum_tiles(direct) * scale + sum_tiles(source)
    state_ref[0] = above
    state_ref[1] = source
    state_ref[2] = direct * scale


def add_sublanes(rows):
    sub = lax.broadcasted_iota(jnp.int32, (8, CB), 0)
    four, two, one = sub < 4, (sub & 2) == 0, (sub & 1) == 0
    rows = [
        jnp.where(four, rows[r], rows[r + 4])
        + pltpu.roll(jnp.where(four, rows[r + 4], rows[r]), 4, 0)
        for r in range(4)
    ]
    rows = [
        jnp.where(
            two,
            rows[r] + pltpu.roll(rows[r], 6, 0),
            rows[r + 2] + pltpu.roll(rows[r + 2], 2, 0),
        )
        for r in range(2)
    ]
    return jnp.where(
        one, rows[0] + pltpu.roll(rows[0], 7, 0), rows[1] + pltpu.roll(rows[1], 1, 0)
    )


def substitute(coef_ref, esum_ref, state_ref, albedo_direct, albedo_diffuse, lit, flux_ref):
    above, source, direct = state_ref[0], state_ref[1], state_ref[2]
    upward = (albedo_diffuse * source + albedo_direct * direct) * pl.reciprocal(
        1.0 - albedo_diffuse * above, approx=False
    )
    none = jnp.zeros((8, CB), F32)
    pending = [esum_ref[LEV] + sum_tiles(above * upward), sum_tiles(upward)] + [none] * 6
    flux_ref[2 * LEV : 2 * LEV + 8, :] = add_sublanes(pending) * lit
    pending = []
    for l in range(LEV - 1, -1, -1):
        upward = coef_ref[l, 1] * upward + coef_ref[l, 2]
        pending = [
            esum_ref[l] + sum_tiles(coef_ref[l, 0] * upward),
            sum_tiles(upward),
        ] + pending
        if l % 4 == 0:
            flux_ref[2 * l : 2 * l + 8, :] = add_sublanes(pending) * lit
            pending = []


COEF = (LEV, 3, G, CB)
ESUM = (LEV + 1, 8, CB)
STATE = (3, G, CB)


def down_kernel(blocks, has_first, following):
    def kernel(gas_ref, wide_ref, column_ref, solar_ref, _, *refs):
        first_ref = None
        if has_first:
            first_ref, *refs = refs
        coef_ref, esum_ref, state_ref, *next_ref = refs
        for i, block in enumerate(blocks):
            eliminate(
                block,
                gas_ref,
                wide_ref,
                column_ref,
                solar_ref,
                coef_ref.at[i],
                esum_ref.at[i],
                state_ref.at[i],
                None if i else first_ref,
            )
        if following is not None:
            next_ref[0][...] = mix_step(gas_ref, following, 0, wide_ref)

    return kernel


def down(blocks, first, following, gas, wide, column, solar, after):
    count = len(blocks)
    mixes = [] if following is None else [shape((2 * G * STEP, CB))]
    return pl.pallas_call(
        down_kernel(blocks, bool(first), following),
        in_specs=[IN_VMEM] * 4 + [UNREAD] + [IN_VMEM] * len(first),
        out_specs=[IN_VMEM] * (3 + len(mixes)),
        out_shape=[shape((count,) + x) for x in (COEF, ESUM, STATE)] + mixes,
        compiler_params=params(24),
        cost_estimate=pl.CostEstimate(
            flops=200000000 * count, transcendentals=0, bytes_accessed=4000000
        ),
        name="down",
    )(gas, wide, column, solar, after, *first)


def ground(albedo_ref, column_ref, block):
    row = slice(block, block + 1)
    return albedo_ref[0, row, :], albedo_ref[1, row, :], column_ref[4, row, :]


def up_kernel(
    coef_a,
    esum_a,
    state_a,
    coef_b,
    esum_b,
    state_b,
    keep_ref,
    got_ref,
    column_ref,
    first_ref,
    final_ref,
    near_ref,
    far_ref,
    albedo_ref,
):
    for s in range(2):
        albedo_ref[s] = keep_ref[0, s].astype(F32) + got_ref[0, s].astype(F32)
    substitute(
        coef_a.at[0], esum_a.at[0], state_a.at[0], *ground(albedo_ref, column_ref, 0), first_ref
    )
    substitute(
        coef_b.at[0],
        esum_b.at[0],
        state_b.at[0],
        *ground(albedo_ref, column_ref, NB - 1),
        final_ref,
    )
    even = lax.axis_index("blk") % 2 == 0
    near_ref[...] = jnp.where(even, final_ref[...], first_ref[...])
    far_ref[...] = jnp.where(even, first_ref[...], final_ref[...])


def up(parts, keep, got, column):
    return pl.pallas_call(
        up_kernel,
        in_specs=[IN_VMEM] * 9,
        out_specs=[IN_VMEM] * 5,
        out_shape=[shape((ROWS, CB))] * 4 + [shape((2, NB, CB))],
        compiler_params=params(2),
        cost_estimate=pl.CostEstimate(flops=4000000, transcendentals=0, bytes_accessed=4000000),
        name="up",
    )(*parts[0], *parts[1], keep, got, column)


def neighbour_rows(block, neighbour_ref, side_ref):
    lanes = slice(block * CB, (block + 1) * CB)
    at_lane, places, weights = [], [], []
    for k in range(3):
        at = jnp.broadcast_to(neighbour_ref[k : k + 1, lanes], (8, CB))
        places.append(((at >> 7) - block + 1) & (NB - 1))
        at_lane.append(at & (CB - 1))
        weights.append(jnp.broadcast_to(side_ref[k : k + 1, lanes], (8, CB)))
    return at_lane, places, weights


def pick(x, at_lane):
    return jnp.take_along_axis(x, at_lane, axis=1, mode="promise_in_bounds")


def correct(block, before, own, after, neighbour_ref, side_ref, put):
    at_lane, places, weights = neighbour_rows(block, neighbour_ref, side_ref)
    for k in range(3):
        for code, part in ((0, before), (2, after)):
            if part is None:
                weights[k] = jnp.where(places[k] == code, 0.0, weights[k])
    totals = {row: own(row) for row in range(0, ROWS, 8)}
    for k in range(3):
        for row in totals:
            here = own(row)
            beside = pick(here, at_lane[k])
            for code, part in ((0, before), (2, after)):
                if part is not None:
                    beside = jnp.where(places[k] == code, pick(part(row), at_lane[k]), beside)
            totals[row] = totals[row] + weights[k] * (beside - here)
    for row, total in totals.items():
        put(row, total)


def correct_rest(block, code, outer, own, partial, neighbour_ref, side_ref, put):
    at_lane, places, weights = neighbour_rows(block, neighbour_ref, side_ref)
    weights = [jnp.where(places[k] == code, weights[k], 0.0) for k in range(3)]
    totals = {row: partial(row) for row in range(0, ROWS, 8)}
    for k in range(3):
        for row in totals:
            beside = pick(outer(row), at_lane[k])
            totals[row] = totals[row] + weights[k] * (beside - own(row))
    for row, total in totals.items():
        put(row, total)


def put_levels(out_ref, block):
    lanes = slice(block * CB, (block + 1) * CB)

    def put(row, total):
        for l in range(row // 2, min(row // 2 + 4, LEV + 1)):
            out_ref[l, :, lanes] = total[2 * l - row : 2 * l - row + 2]

    return put


def rows_of(ref):
    return lambda row: ref[row : row + 8, :]


def inner_kernel(
    gas_ref,
    wide_ref,
    column_ref,
    solar_ref,
    albedo_ref,
    first_ref,
    final_ref,
    coef_b,
    esum_b,
    state_b,
    coef_c,
    esum_c,
    state_c,
    neighbour_ref,
    side_ref,
    out_ref,
    partial_ref,
    coef_ref,
    esum_ref,
    state_ref,
    flux_ref,
):
    kept = {}
    for i, n in enumerate(WINDOWS[1]):
        kept[n] = coef_b.at[i], esum_b.at[i], state_b.at[i]
    for i, n in enumerate(WINDOWS[2]):
        kept[n] = coef_c.at[i], esum_c.at[i], state_c.at[i]
    for i, n in enumerate(LATE):
        kept[n] = coef_ref.at[i], esum_ref.at[i], state_ref.at[i]
    flux = {0: first_ref, NB - 1: final_ref}
    for n in range(1, NB - 1):
        flux[n] = flux_ref.at[n - 1]

    def finish(n):
        substitute(*kept[n], *ground(albedo_ref, column_ref, n), flux[n])

    def side(n):
        before, own, after = [
            rows_of(flux[n + i]) if n + i in flux else None for i in (-1, 0, 1)
        ]
        if n in (0, NB - 1):
            partial = partial_ref.at[n // (NB - 1)]

            def put(row, total):
                partial[row : row + 8, :] = total

        else:
            put = put_levels(out_ref, n)
        correct(n, before, own, after, neighbour_ref, side_ref, put)

    for n in LATE:
        eliminate(n, gas_ref, wide_ref, column_ref, solar_ref, *kept[n])
    for n in range(1, NB - 1):
        finish(n)
    for n in range(NB):
        side(n)


def inner(gas, wide, column, solar, albedo, first, final, parts, neighbours, side_weight):
    return pl.pallas_call(
        inner_kernel,
        in_specs=[IN_VMEM] * 15,
        out_specs=[IN_VMEM] * 2,
        out_shape=[shape((LEV + 1, 2, COLS)), shape((2, ROWS, CB))],
        scratch_shapes=[
            pltpu.VMEM((len(LATE),) + COEF, F32),
            pltpu.VMEM((len(LATE),) + ESUM, F32),
            pltpu.VMEM((len(LATE),) + STATE, F32),
            pltpu.VMEM((NB - 2, ROWS, CB), F32),
        ],
        compiler_params=params(24),
        cost_estimate=pl.CostEstimate(
            flops=2000000000, transcendentals=0, bytes_accessed=4000000
        ),
        name="inner",
    )(
        gas,
        wide,
        column,
        solar,
        albedo,
        first,
        final,
        *parts[1],
        *parts[2],
        neighbours,
        side_weight,
    )


def edge_side_kernel(
    near_got,
    far_got,
    first_ref,
    final_ref,
    partial_ref,
    neighbour_ref,
    side_ref,
    full_ref,
    out_hbm,
    edge_ref,
    sems,
):
    def copy(source, lanes, i):
        return pltpu.make_async_copy(
            source.at[:, :, lanes], out_hbm.at[:, :, lanes], sems.at[i]
        )

    copies = [copy(full_ref, pl.ds(CB, COLS - 2 * CB), 0)]
    copies[0].start()
    even = lax.axis_index("blk") % 2 == 0
    near, far = rows_of(near_got), rows_of(far_got)
    edges = (
        (0, 0, lambda row: jnp.where(even, far(row), near(row)), first_ref),
        (NB - 1, 2, lambda row: jnp.where(even, near(row), far(row)), final_ref),
    )
    for i, (block, code, outer, own) in enumerate(edges):
        correct_rest(
            block,
            code,
            outer,
            rows_of(own),
            rows_of(partial_ref.at[i]),
            neighbour_ref,
            side_ref,
            put_levels(edge_ref, block),
        )
    for i, block in enumerate((0, NB - 1)):
        copies.append(copy(edge_ref, pl.ds(block * CB, CB), 1 + i))
        copies[-1].start()
    for started in copies:
        started.wait()


def edge_side(near_got, far_got, first, final, partial, neighbours, side_weight, full):
    return pl.pallas_call(
        edge_side_kernel,
        in_specs=[IN_VMEM] * 8,
        out_specs=IN_HBM,
        out_shape=shape((LEV + 1, 2, COLS)),
        scratch_shapes=[
            pltpu.VMEM((LEV + 1, 2, COLS), F32),
            pltpu.SemaphoreType.DMA((3,)),
        ],
        compiler_params=params(4),
        name="edge_side",
    )(near_got, far_got, first, final, partial, neighbours, side_weight, full)


PARTNERS = (1, 2, 6)


def exchange(x, mask):
    count = lax.axis_size("blk")
    return lax.ppermute(x, "blk", [(i, i ^ mask) for i in range(count)])


def beyond(x):
    count, bands = lax.axis_size("blk"), lax.axis_size("grp")
    pairs = []
    for i in range(count):
        for band in range(bands):
            if i in (0, count - 1):
                pairs.append((i * bands + band, i * bands + (band ^ 4)))
            else:
                pairs.append((i * bands + band, (i + (1 if i % 2 else -1)) * bands + band))
    return lax.ppermute(x, ("blk", "grp"), pairs)


def local(
    gas_state,
    cos_zenith,
    daylit,
    fine_area,
    fine_albedo,
    parent_of,
    optics_weight,
    solar_weight,
    neighbours,
    side_weight,
):
    send, keep, gas, wide, column, solar, beside, weights = surface(
        parent_of,
        fine_area,
        fine_albedo,
        optics_weight,
        cos_zenith,
        daylit,
        solar_weight,
        neighbours,
        side_weight,
        gas_state,
    )
    parts, first_mix = [], []
    for i, blocks in enumerate(WINDOWS):
        got = exchange(send, PARTNERS[i])
        following = WINDOWS[i + 1][0] if i < 2 else None
        *part, first_mix = (
            *down(blocks, first_mix, following, gas, wide, column, solar, keep),
            None,
        )[:4]
        first_mix = [first_mix]
        parts.append(part)
        if i < 2:
            send, keep = merge(keep, got, parts[-1][2])
    first, final, near, far, albedo = up(parts, keep, got, column)
    far_got = beyond(far)
    near_got = exchange(near, 1)
    full, partial = inner(
        gas, wide, column, solar, albedo, first, final, parts, beside, weights
    )
    done = edge_side(near_got, far_got, first, final, partial, beside, weights, full)
    return done.transpose(1, 0, 2)


def solution(mesh):
    both = ("grp", "blk")
    in_specs = (
        P(None, None, both),
        P(both),
        P(both),
        P(both),
        P(None, both),
        P(both),
        P(),
        P(),
        P(None, both),
        P(None, both),
    )
    return jax.shard_map(
        local, mesh=mesh, in_specs=in_specs, out_specs=P(None, None, both), check_vma=False
    )
```

```python
import jax
import jax.numpy as jnp
from jax import lax
from jax.experimental import pallas as pl
from jax.experimental.pallas import tpu as pltpu
from jax.sharding import PartitionSpec as P

F = 16
LEV = 32
CB = 128
G = 32
KIDS = 4
NB = 8
NBLK = 8
ROWS = 72
STEP = 8
FINE_BLOCKS = NB * KIDS
COLS = NB * CB

ASYM = 0.8
TAU_SCALE = 0.08
SSA_MAX = 0.98
LOG2E = 1.4426950408889634

SLOPE = 0.5 * (1.25 + 0.75 * ASYM)
UNIT = 0.5 * SLOPE * SSA_MAX
SHIFT = 1.0 / UNIT - 1.0
BETA = 0.375 * (1.0 - ASYM) / SLOPE
RATE = -2.0 * TAU_SCALE * UNIT
SCATTER = UNIT / (0.375 * (1.0 - ASYM))

F32 = jnp.float32
BF16 = jnp.bfloat16
IN_VMEM = pl.BlockSpec(memory_space=pltpu.VMEM)
IN_HBM = pl.BlockSpec(memory_space=pltpu.HBM)
UNREAD = pl.BlockSpec(memory_space=pl.ANY)


def params(mebibytes):
    return pltpu.CompilerParams(vmem_limit_bytes=mebibytes << 20)


def shape(dims, kind=F32):
    return jax.ShapeDtypeStruct(dims, kind)


def sum_tiles(x):
    return (x[0:8] + x[8:16]) + (x[16:24] + x[24:32])


def place_albedo(parent_ref, area_ref, albedo_ref, mine):
    sub = lax.broadcasted_iota(jnp.int32, (CB, CB), 0).astype(F32).astype(BF16)
    line = lax.broadcasted_iota(jnp.int32, (8, CB), 0)
    one, zero = jnp.ones((), BF16), jnp.zeros((), BF16)
    totals = [[], [], []]
    for group in range(0, FINE_BLOCKS, 8):
        rows = slice(group, group + 8)
        area = area_ref[rows, :]
        terms = [area, area * albedo_ref[0, rows, :], area * albedo_ref[1, rows, :]]
        pieces = []
        for term in terms:
            for _ in range(3):
                piece = term.astype(BF16).astype(F32)
                pieces.append(piece)
                term = term - piece
        column = (parent_ref[rows, :] & (CB - 1)).astype(F32).astype(BF16)
        hots, values = [], []
        for j in range(8):
            hots.append(
                jnp.where(jnp.broadcast_to(column[j : j + 1, :], (CB, CB)) == sub, one, zero)
            )
            values.append(
                jnp.concatenate([jnp.where(line == j, x, 0.0) for x in pieces], axis=0).astype(
                    BF16
                )
            )
        total = lax.dot_general(
            jnp.concatenate(values, axis=1),
            jnp.concatenate(hots, axis=1),
            (((1,), (1,)), ((), ())),
            preferred_element_type=F32,
        )
        for i in range(3):
            at = 24 * i
            totals[i].append(
                total[at : at + 8] + (total[at + 8 : at + 16] + total[at + 16 : at + 24])
            )
    area = jnp.concatenate(totals[0], axis=0)
    here = area > 0.0
    safe = jnp.where(here, area, 1.0)
    owner = (parent_ref[:, 0:1] >> 7) ^ (mine * NB)
    side, across = owner & (2 * NB), owner & (4 * NB)
    owner = (owner & (2 * NB - 1)) + (across >> 1) + ((side << 1) ^ across)
    slot = lax.broadcasted_iota(jnp.int32, (FINE_BLOCKS, NBLK * NB), 1)
    where_to = jnp.where(owner == slot, 1.0, 0.0).astype(BF16)
    placed = []
    for s in range(2):
        total = jnp.concatenate(totals[1 + s], axis=0)
        albedo = jnp.where(here, total / safe, 0.0).astype(BF16)
        placed.append(
            lax.dot_general(
                where_to, albedo, (((0,), (0,)), ((), ())), preferred_element_type=F32
            ).astype(BF16)
        )
    return placed


def spread_weights(weight_ref, wide_ref):
    row = lax.broadcasted_iota(jnp.int32, (F, F * STEP), 0)
    col = lax.broadcasted_iota(jnp.int32, (F, F * STEP), 1)
    spread = jnp.where(col // STEP == row, 1.0, 0.0).astype(BF16)
    depth = lax.broadcasted_iota(jnp.int32, (F, 2 * G), 1) < G
    scaled = weight_ref[...].astype(F32) * jnp.where(depth, LOG2E, 0.5)
    high = scaled.astype(BF16)
    low = (scaled - high.astype(F32)).astype(BF16)
    wide = jnp.concatenate(
        [
            lax.dot_general(x, spread, (((0,), (0,)), ((), ())), preferred_element_type=F32)
            for x in (high, low)
        ],
        axis=1,
    )
    level = lax.broadcasted_iota(jnp.int32, (2 * G, 2 * F * STEP), 1) % STEP
    for l in range(STEP):
        wide_ref[l * 2 * G : (l + 1) * 2 * G, :] = jnp.where(level == l, wide, 0.0).astype(BF16)


def column_constants(cosine, lit, column_ref):
    back = 0.5 * (1.0 - ASYM * cosine)
    rising = back * SCATTER
    column_ref[0] = -TAU_SCALE / cosine
    column_ref[1] = (1.0 - back) / back
    column_ref[2] = 1.0 / rising
    column_ref[3] = cosine
    column_ref[4] = lit * rising


WINDOWS = ((0,), (NB - 1, 1), (2, 3, 4))
LATE = (5, 6)


def surface_kernel(
    parent_hbm,
    area_hbm,
    albedo_hbm,
    weight_hbm,
    cosine_hbm,
    lit_hbm,
    solar_hbm,
    neighbour_hbm,
    side_hbm,
    gas_hbm,
    send_ref,
    keep_ref,
    gas_ref,
    wide_ref,
    column_ref,
    solar_ref,
    neighbour_ref,
    side_ref,
    parent_ref,
    area_ref,
    albedo_ref,
    weight_ref,
    cosine_ref,
    lit_ref,
    sun_ref,
    sems,
):
    pairs = (
        (parent_hbm, parent_ref),
        (area_hbm, area_ref),
        (albedo_hbm.at[:, 0, :], albedo_ref.at[0]),
        (albedo_hbm.at[:, 1, :], albedo_ref.at[1]),
        (weight_hbm, weight_ref),
        (cosine_hbm, cosine_ref),
        (lit_hbm, lit_ref),
        (solar_hbm, sun_ref),
        (neighbour_hbm, neighbour_ref),
        (side_hbm, side_ref),
        (gas_hbm, gas_ref),
    )
    copies = [
        pltpu.make_async_copy(source, target, sems.at[i])
        for i, (source, target) in enumerate(pairs)
    ]
    for copy in copies:
        copy.start()
    for copy in copies[:8]:
        copy.wait()
    mine = lax.axis_index("blk")
    placed = place_albedo(parent_ref, area_ref, albedo_ref, mine)
    for s in range(2):
        for i in range(NBLK // 2):
            keep_ref[i, s] = placed[s][2 * i * NB : (2 * i + 1) * NB]
            send_ref[i, s] = placed[s][(2 * i + 1) * NB : (2 * i + 2) * NB]
    spread_weights(weight_ref, wide_ref)
    column_constants(cosine_ref[...].astype(F32), lit_ref[...].astype(F32), column_ref)
    row = lax.broadcasted_iota(jnp.int32, (G, G), 0)
    col = lax.broadcasted_iota(jnp.int32, (G, G), 1)
    sun = jnp.sum(jnp.where(row == col, sun_ref[...], 0.0), axis=1, keepdims=True)
    solar_ref[...] = jnp.broadcast_to(sun, (G, CB))
    for copy in copies[8:]:
        copy.wait()


def surface(
    parent_of,
    fine_area,
    fine_albedo,
    optics_weight,
    cos_zenith,
    daylit,
    solar_weight,
    neighbours,
    side_weight,
    gas_state,
):
    return pl.pallas_call(
        surface_kernel,
        in_specs=[IN_HBM] * 10,
        out_specs=[IN_VMEM] * 8,
        out_shape=[
            shape((NBLK // 2, 2, NB, CB), BF16),
            shape((NBLK // 2, 2, NB, CB), BF16),
            shape((F, LEV, COLS), BF16),
            shape((2 * G * STEP, 2 * F * STEP), BF16),
            shape((5, NB, CB)),
            shape((G, CB)),
            shape((3, COLS), jnp.int32),
            shape((3, COLS)),
        ],
        scratch_shapes=[
            pltpu.VMEM((FINE_BLOCKS, CB), jnp.int32),
            pltpu.VMEM((FINE_BLOCKS, CB), F32),
            pltpu.VMEM((2, FINE_BLOCKS, CB), F32),
            pltpu.VMEM((F, 2 * G), BF16),
            pltpu.VMEM((NB, CB), BF16),
            pltpu.VMEM((NB, CB), jnp.int32),
            pltpu.VMEM((1, G), F32),
            pltpu.SemaphoreType.DMA((11,)),
        ],
        compiler_params=params(4),
        name="surface",
    )(
        *[
            pltpu.with_memory_space_constraint(x, pltpu.HBM)
            for x in (
                parent_of.reshape(FINE_BLOCKS, CB),
                fine_area.reshape(FINE_BLOCKS, CB),
                fine_albedo.reshape(2, FINE_BLOCKS, CB).transpose(1, 0, 2),
                optics_weight.T,
                cos_zenith.reshape(NB, CB),
                daylit.reshape(NB, CB),
                solar_weight.reshape(1, G),
                neighbours,
                side_weight,
                gas_state,
            )
        ]
    )


def merge_kernel(keep_ref, got_ref, after_ref, send_ref, next_ref):
    del after_ref
    for i in range(keep_ref.shape[0]):
        total = (keep_ref[i].astype(F32) + got_ref[i].astype(F32)).astype(BF16)
        target = send_ref if i % 2 else next_ref
        target[i // 2] = total


def merge(keep, got, after):
    half = shape((keep.shape[0] // 2,) + keep.shape[1:], BF16)
    return pl.pallas_call(
        merge_kernel,
        in_specs=[IN_VMEM, IN_VMEM, UNREAD],
        out_specs=[IN_VMEM] * 2,
        out_shape=[half, half],
        compiler_params=params(2),
        name="merge",
    )(keep, got, after)


def layer_terms(depth_mix, albedo_mix, slant_rate):
    soft = jnp.maximum(depth_mix, jnp.log2(1.0 + jnp.exp2(jnp.minimum(depth_mix, 60.0))))
    e_dir = jnp.exp2(soft * slant_rate)
    bend = jnp.tanh(albedo_mix)
    gamma_one = SHIFT - bend
    gamma_two = BETA * bend + BETA
    product = (gamma_one - gamma_two) * (gamma_one + gamma_two)
    root = product * lax.rsqrt(product)
    damping = jnp.exp2(RATE * (root * soft))
    damped_sq = damping * damping
    lost = 1.0 - damped_sq
    even = root + root * damped_sq
    odd = gamma_one * lost
    transmit = (root + root) * damping
    return e_dir, gamma_two, even + odd, even - odd, gamma_two * lost, transmit


def mix_step(gas_ref, block, step, wide_ref):
    lanes = slice(block * CB, (block + 1) * CB)
    gas = gas_ref[:, step * STEP : (step + 1) * STEP, lanes].reshape(F * STEP, CB)
    return jnp.dot(
        wide_ref[...], jnp.concatenate([gas, gas], axis=0), preferred_element_type=F32
    )


def eliminate(
    block, gas_ref, wide_ref, column_ref, solar_ref, coef_ref, esum_ref, state_ref, first_mix=None
):
    products = [
        mix_step(gas_ref, block, step, wide_ref) if step or first_mix is None else first_mix
        for step in range(LEV // STEP)
    ]
    slant_rate, falling, scale, cosine = [
        column_ref[i, block : block + 1, :] for i in range(4)
    ]
    direct = solar_ref[...] * cosine
    above = jnp.zeros((G, CB), F32)
    source = jnp.zeros((G, CB), F32)
    for l in range(LEV):
        at = (l % STEP) * 2 * G
        mix = products[l // STEP]
        e_dir, gamma_two, divisor, mirrored, reflect, transmit = layer_terms(
            mix[at : at + G], mix[at + G : at + 2 * G], slant_rate
        )
        esum_ref[l] = sum_tiles(direct) * scale + sum_tiles(source)
        below = direct * e_dir
        scattered = gamma_two * (direct - below)
        inverse = pl.reciprocal(divisor - above * reflect, approx=False)
        incident = (source + above * scattered) * inverse
        coef_ref[l, 0] = above
        coef_ref[l, 1] = transmit * inverse
        coef_ref[l, 2] = scattered + reflect * incident
        source = scattered * falling + transmit * incident
        above = (reflect + above * mirrored) * inverse
        direct = below
    esum_ref[LEV] = sum_tiles(direct) * scale + sum_tiles(source)
    state_ref[0] = above
    state_ref[1] = source
    state_ref[2] = direct * scale


def add_sublanes(rows):
    sub = lax.broadcasted_iota(jnp.int32, (8, CB), 0)
    four, two, one = sub < 4, (sub & 2) == 0, (sub & 1) == 0
    rows = [
        jnp.where(four, rows[r], rows[r + 4])
        + pltpu.roll(jnp.where(four, rows[r + 4], rows[r]), 4, 0)
        for r in range(4)
    ]
    rows = [
        jnp.where(
            two,
            rows[r] + pltpu.roll(rows[r], 6, 0),
            rows[r + 2] + pltpu.roll(rows[r + 2], 2, 0),
        )
        for r in range(2)
    ]
    return jnp.where(
        one, rows[0] + pltpu.roll(rows[0], 7, 0), rows[1] + pltpu.roll(rows[1], 1, 0)
    )


def substitute(coef_ref, esum_ref, state_ref, albedo_direct, albedo_diffuse, lit, flux_ref):
    above, source, direct = state_ref[0], state_ref[1], state_ref[2]
    upward = (albedo_diffuse * source + albedo_direct * direct) * pl.reciprocal(
        1.0 - albedo_diffuse * above, approx=False
    )
    none = jnp.zeros((8, CB), F32)
    pending = [esum_ref[LEV] + sum_tiles(above * upward), sum_tiles(upward)] + [none] * 6
    flux_ref[2 * LEV : 2 * LEV + 8, :] = add_sublanes(pending) * lit
    pending = []
    for l in range(LEV - 1, -1, -1):
        upward = coef_ref[l, 1] * upward + coef_ref[l, 2]
        pending = [
            esum_ref[l] + sum_tiles(coef_ref[l, 0] * upward),
            sum_tiles(upward),
        ] + pending
        if l % 4 == 0:
            flux_ref[2 * l : 2 * l + 8, :] = add_sublanes(pending) * lit
            pending = []


COEF = (LEV, 3, G, CB)
ESUM = (LEV + 1, 8, CB)
STATE = (3, G, CB)


def down_kernel(blocks, has_first, following):
    def kernel(gas_ref, wide_ref, column_ref, solar_ref, _, *refs):
        first_ref = None
        if has_first:
            first_ref, *refs = refs
        coef_ref, esum_ref, state_ref, *next_ref = refs
        for i, block in enumerate(blocks):
            eliminate(
                block,
                gas_ref,
                wide_ref,
                column_ref,
                solar_ref,
                coef_ref.at[i],
                esum_ref.at[i],
                state_ref.at[i],
                None if i else first_ref,
            )
        if following is not None:
            next_ref[0][...] = mix_step(gas_ref, following, 0, wide_ref)

    return kernel


def down(blocks, first, following, gas, wide, column, solar, after):
    count = len(blocks)
    mixes = [] if following is None else [shape((2 * G * STEP, CB))]
    return pl.pallas_call(
        down_kernel(blocks, bool(first), following),
        in_specs=[IN_VMEM] * 4 + [UNREAD] + [IN_VMEM] * len(first),
        out_specs=[IN_VMEM] * (3 + len(mixes)),
        out_shape=[shape((count,) + x) for x in (COEF, ESUM, STATE)] + mixes,
        compiler_params=params(24),
        cost_estimate=pl.CostEstimate(
            flops=200000000 * count, transcendentals=0, bytes_accessed=4000000
        ),
        name="down",
    )(gas, wide, column, solar, after, *first)


def ground(albedo_ref, column_ref, block):
    row = slice(block, block + 1)
    return albedo_ref[0, row, :], albedo_ref[1, row, :], column_ref[4, row, :]


def up_kernel(
    coef_a,
    esum_a,
    state_a,
    coef_b,
    esum_b,
    state_b,
    keep_ref,
    got_ref,
    column_ref,
    first_ref,
    final_ref,
    near_ref,
    far_ref,
    albedo_ref,
):
    for s in range(2):
        albedo_ref[s] = keep_ref[0, s].astype(F32) + got_ref[0, s].astype(F32)
    substitute(
        coef_a.at[0], esum_a.at[0], state_a.at[0], *ground(albedo_ref, column_ref, 0), first_ref
    )
    substitute(
        coef_b.at[0],
        esum_b.at[0],
        state_b.at[0],
        *ground(albedo_ref, column_ref, NB - 1),
        final_ref,
    )
    even = lax.axis_index("blk") % 2 == 0
    near_ref[...] = jnp.where(even, final_ref[...], first_ref[...])
    far_ref[...] = jnp.where(even, first_ref[...], final_ref[...])


def up(parts, keep, got, column):
    return pl.pallas_call(
        up_kernel,
        in_specs=[IN_VMEM] * 9,
        out_specs=[IN_VMEM] * 5,
        out_shape=[shape((ROWS, CB))] * 4 + [shape((2, NB, CB))],
        compiler_params=params(2),
        cost_estimate=pl.CostEstimate(flops=4000000, transcendentals=0, bytes_accessed=4000000),
        name="up",
    )(*parts[0], *parts[1], keep, got, column)


def neighbour_rows(block, neighbour_ref, side_ref):
    lanes = slice(block * CB, (block + 1) * CB)
    at_lane, places, weights = [], [], []
    for k in range(3):
        at = jnp.broadcast_to(neighbour_ref[k : k + 1, lanes], (8, CB))
        places.append(((at >> 7) - block + 1) & (NB - 1))
        at_lane.append(at & (CB - 1))
        weights.append(jnp.broadcast_to(side_ref[k : k + 1, lanes], (8, CB)))
    return at_lane, places, weights


def pick(x, at_lane):
    return jnp.take_along_axis(x, at_lane, axis=1, mode="promise_in_bounds")


def correct(block, before, own, after, neighbour_ref, side_ref, put):
    at_lane, places, weights = neighbour_rows(block, neighbour_ref, side_ref)
    for k in range(3):
        for code, part in ((0, before), (2, after)):
            if part is None:
                weights[k] = jnp.where(places[k] == code, 0.0, weights[k])
    totals = {row: own(row) for row in range(0, ROWS, 8)}
    for k in range(3):
        for row in totals:
            here = own(row)
            beside = pick(here, at_lane[k])
            for code, part in ((0, before), (2, after)):
                if part is not None:
                    beside = jnp.where(places[k] == code, pick(part(row), at_lane[k]), beside)
            totals[row] = totals[row] + weights[k] * (beside - here)
    for row, total in totals.items():
        put(row, total)


def correct_rest(block, code, outer, own, partial, neighbour_ref, side_ref, put):
    at_lane, places, weights = neighbour_rows(block, neighbour_ref, side_ref)
    weights = [jnp.where(places[k] == code, weights[k], 0.0) for k in range(3)]
    totals = {row: partial(row) for row in range(0, ROWS, 8)}
    for k in range(3):
        for row in totals:
            beside = pick(outer(row), at_lane[k])
            totals[row] = totals[row] + weights[k] * (beside - own(row))
    for row, total in totals.items():
        put(row, total)


def put_levels(out_ref, block):
    lanes = slice(block * CB, (block + 1) * CB)

    def put(row, total):
        for l in range(row // 2, min(row // 2 + 4, LEV + 1)):
            out_ref[l, :, lanes] = total[2 * l - row : 2 * l - row + 2]

    return put


def rows_of(ref):
    return lambda row: ref[row : row + 8, :]


def inner_kernel(
    gas_ref,
    wide_ref,
    column_ref,
    solar_ref,
    albedo_ref,
    first_ref,
    final_ref,
    coef_b,
    esum_b,
    state_b,
    coef_c,
    esum_c,
    state_c,
    neighbour_ref,
    side_ref,
    out_ref,
    partial_ref,
    coef_ref,
    esum_ref,
    state_ref,
    flux_ref,
):
    kept = {}
    for i, n in enumerate(WINDOWS[1]):
        kept[n] = coef_b.at[i], esum_b.at[i], state_b.at[i]
    for i, n in enumerate(WINDOWS[2]):
        kept[n] = coef_c.at[i], esum_c.at[i], state_c.at[i]
    for i, n in enumerate(LATE):
        kept[n] = coef_ref.at[i], esum_ref.at[i], state_ref.at[i]
    flux = {0: first_ref, NB - 1: final_ref}
    for n in range(1, NB - 1):
        flux[n] = flux_ref.at[n - 1]

    def finish(n):
        substitute(*kept[n], *ground(albedo_ref, column_ref, n), flux[n])

    def side(n):
        before, own, after = [
            rows_of(flux[n + i]) if n + i in flux else None for i in (-1, 0, 1)
        ]
        if n in (0, NB - 1):
            partial = partial_ref.at[n // (NB - 1)]

            def put(row, total):
                partial[row : row + 8, :] = total

        else:
            put = put_levels(out_ref, n)
        correct(n, before, own, after, neighbour_ref, side_ref, put)

    for n in LATE:
        eliminate(n, gas_ref, wide_ref, column_ref, solar_ref, *kept[n])
    for n in range(1, NB - 1):
        finish(n)
    for n in range(NB):
        side(n)


def inner(gas, wide, column, solar, albedo, first, final, parts, neighbours, side_weight):
    return pl.pallas_call(
        inner_kernel,
        in_specs=[IN_VMEM] * 15,
        out_specs=[IN_VMEM] * 2,
        out_shape=[shape((LEV + 1, 2, COLS)), shape((2, ROWS, CB))],
        scratch_shapes=[
            pltpu.VMEM((len(LATE),) + COEF, F32),
            pltpu.VMEM((len(LATE),) + ESUM, F32),
            pltpu.VMEM((len(LATE),) + STATE, F32),
            pltpu.VMEM((NB - 2, ROWS, CB), F32),
        ],
        compiler_params=params(24),
        cost_estimate=pl.CostEstimate(
            flops=2000000000, transcendentals=0, bytes_accessed=4000000
        ),
        name="inner",
    )(
        gas,
        wide,
        column,
        solar,
        albedo,
        first,
        final,
        *parts[1],
        *parts[2],
        neighbours,
        side_weight,
    )


def edge_side_kernel(
    near_got,
    far_got,
    first_ref,
    final_ref,
    partial_ref,
    neighbour_ref,
    side_ref,
    full_ref,
    out_hbm,
    edge_ref,
    sems,
):
    def copy(source, lanes, i):
        return pltpu.make_async_copy(
            source.at[:, :, lanes], out_hbm.at[:, :, lanes], sems.at[i]
        )

    copies = [copy(full_ref, pl.ds(CB, COLS - 2 * CB), 0)]
    copies[0].start()
    even = lax.axis_index("blk") % 2 == 0
    near, far = rows_of(near_got), rows_of(far_got)
    edges = (
        (0, 0, lambda row: jnp.where(even, far(row), near(row)), first_ref),
        (NB - 1, 2, lambda row: jnp.where(even, near(row), far(row)), final_ref),
    )
    for i, (block, code, outer, own) in enumerate(edges):
        correct_rest(
            block,
            code,
            outer,
            rows_of(own),
            rows_of(partial_ref.at[i]),
            neighbour_ref,
            side_ref,
            put_levels(edge_ref, block),
        )
    for i, block in enumerate((0, NB - 1)):
        copies.append(copy(edge_ref, pl.ds(block * CB, CB), 1 + i))
        copies[-1].start()
    for started in copies:
        started.wait()


def edge_side(near_got, far_got, first, final, partial, neighbours, side_weight, full):
    return pl.pallas_call(
        edge_side_kernel,
        in_specs=[IN_VMEM] * 8,
        out_specs=IN_HBM,
        out_shape=shape((LEV + 1, 2, COLS)),
        scratch_shapes=[
            pltpu.VMEM((LEV + 1, 2, COLS), F32),
            pltpu.SemaphoreType.DMA((3,)),
        ],
        compiler_params=params(4),
        name="edge_side",
    )(near_got, far_got, first, final, partial, neighbours, side_weight, full)


PARTNERS = (1, 6, 2)


def exchange(x, mask):
    count = lax.axis_size("blk")
    return lax.ppermute(x, "blk", [(i, i ^ mask) for i in range(count)])


def beyond(x):
    count, bands = lax.axis_size("blk"), lax.axis_size("grp")
    pairs = []
    for i in range(count):
        for band in range(bands):
            if i in (0, count - 1):
                pairs.append((i * bands + band, i * bands + (band ^ 4)))
            else:
                pairs.append((i * bands + band, (i + (1 if i % 2 else -1)) * bands + band))
    return lax.ppermute(x, ("blk", "grp"), pairs)


def local(
    gas_state,
    cos_zenith,
    daylit,
    fine_area,
    fine_albedo,
    parent_of,
    optics_weight,
    solar_weight,
    neighbours,
    side_weight,
):
    send, keep, gas, wide, column, solar, beside, weights = surface(
        parent_of,
        fine_area,
        fine_albedo,
        optics_weight,
        cos_zenith,
        daylit,
        solar_weight,
        neighbours,
        side_weight,
        gas_state,
    )
    parts, first_mix = [], []
    for i, blocks in enumerate(WINDOWS):
        got = exchange(send, PARTNERS[i])
        following = WINDOWS[i + 1][0] if i < 2 else None
        *part, first_mix = (
            *down(blocks, first_mix, following, gas, wide, column, solar, keep),
            None,
        )[:4]
        first_mix = [first_mix]
        parts.append(part)
        if i < 2:
            send, keep = merge(keep, got, parts[-1][2])
    first, final, near, far, albedo = up(parts, keep, got, column)
    far_got = beyond(far)
    near_got = exchange(near, 1)
    full, partial = inner(
        gas, wide, column, solar, albedo, first, final, parts, beside, weights
    )
    done = edge_side(near_got, far_got, first, final, partial, beside, weights, full)
    return done.transpose(1, 0, 2)


def solution(mesh):
    both = ("grp", "blk")
    in_specs = (
        P(None, None, both),
        P(both),
        P(both),
        P(both),
        P(None, both),
        P(both),
        P(),
        P(),
        P(None, both),
        P(None, both),
    )
    return jax.shard_map(
        local, mesh=mesh, in_specs=in_specs, out_specs=P(None, None, both), check_vma=False
    )
```
